256 devices in a mesh: group: 4 (over x), dp: 64 (over y, z, core).
Axes of the slice: x: 4, y: 4, z: 8, core: 2. Of those that a mesh axis runs over, the one named last changes fastest.
Arguments:
- hidden: bfloat16 [65536, 2048], P(('group', 'dp')), may hold values from 0 to 40, as said below
- weight: bfloat16 [2048, 1024], replicated, may hold values from -0.125 to 0.125
- partners: int32 [256, 256], P(('group', 'dp')), may hold values from 0 to 255, each once within a row
Outputs:
- whitened: bfloat16 [65536, 1024], P(('group', 'dp'))
- grad_weight: float32 [2048, 1024], P(('group', 'dp'))
- grad_hidden: bfloat16 [65536, 2048], P(('group', 'dp'))
The draws below stay inside these ranges and needn't reach their ends.
Inputs may be any that keep to these rules, and one draw needn't show every extreme that they name: `hidden`: nonnegative activations. `partners`: each row is a permutation of 0 to 255.
All inputs are finite; a program needn't handle non-finite values.
Results may differ from the reference program's by a relative error of at most 0.0089.
Values sent between devices are 32-bit elements; how exact they have to be, the bound alone decides.
A program may use at most 128 MiB of HBM per device.

```python
import math
import jax
import jax.numpy as jnp
from jax import lax

HID = 2048
EMB = 1024
ROWS_DEV = 256
ROWS = 65536
N_GROUP = 4
N_DP = 64


def mixed_columns(key, base_vals):
    shift_key, coef_key = jax.random.split(key)
    shifts = jax.random.randint(shift_key, (5,), 1, HID)
    coefs = jax.random.uniform(coef_key, (5,), jnp.float32, 0.1, 0.25)
    total = 1.5 * base_vals
    for term in range(5):
        total = total + coefs[term] * jnp.roll(base_vals, shifts[term], axis=1)
    return total / jnp.sqrt(2.25 + jnp.sum(coefs * coefs))


def draw_hidden(key, part):
    first_key = jax.random.fold_in(key, 0)
    second_key = jax.random.fold_in(key, 1)
    fourth_key = jax.random.fold_in(key, 3)
    col_scale = jnp.exp(jax.random.uniform(second_key, (1, HID), jnp.float32, math.log(0.3), math.log(3.0)))
    base_vals = jnp.clip(jax.random.normal(first_key, (ROWS, HID), jnp.float32), -6.0, 6.0)
    mixed = mixed_columns(fourth_key, base_vals) + 0.5
    return jnp.minimum(jnp.maximum(mixed, 0.0) * col_scale, 40.0).astype(jnp.bfloat16)


def normal_values(own_key, extent, deviation, most, kind=jnp.bfloat16):
    return jnp.clip(deviation * jax.random.normal(own_key, extent, jnp.float32), -most, most).astype(kind)


def setup_inputs(seed: int = 0) -> dict:
    seeds = jax.random.split(jax.random.key(seed), 4)
    hidden = draw_hidden(jax.random.fold_in(seeds[3], 71), 0)
    weight = normal_values(seeds[1], (HID, EMB), HID ** -0.5, 0.125)
    partners = jax.vmap(lambda own: jax.random.permutation(own, ROWS_DEV))(jax.random.split(seeds[2], (N_GROUP * N_DP))).reshape((N_GROUP * N_DP, ROWS_DEV)).astype(jnp.int32)
    return {"hidden": hidden, "weight": weight, "partners": partners}


epsilon = 1e-06
highest = lax.Precision.HIGHEST

def reference(hidden, weight, partners):
    total_rows = hidden.shape[0]
    embedded = jnp.dot(hidden.astype(jnp.float32), weight.astype(jnp.float32), preferred_element_type=jnp.float32)
    mean_row = lax.optimization_barrier(jnp.sum(embedded, axis=0)) / total_rows
    centered = embedded - mean_row
    scatter = jnp.dot(centered.T, centered, precision=highest)
    cov = scatter / (total_rows - 1)
    factor = jnp.linalg.cholesky(cov)
    white = lax.linalg.triangular_solve(factor, centered, left_side=False, lower=True, transpose_a=True)
    whitened = white.astype(jnp.bfloat16)
    row_norm = jnp.sqrt(lax.optimization_barrier(jnp.sum(white * white, axis=1, keepdims=True)) + epsilon)
    unit = white / row_norm
    offsets = jnp.arange(total_rows, dtype=jnp.int32) // ROWS_DEV * ROWS_DEV
    partner = partners.reshape(-1).astype(jnp.int32) + offsets
    inverse = jnp.zeros((total_rows,), jnp.int32).at[partner].set(jnp.arange(total_rows, dtype=jnp.int32))
    grad_unit = 2.0 * (2.0 * unit - unit[partner] - unit[inverse])
    inner_prod = lax.optimization_barrier(jnp.sum(white * grad_unit, axis=1, keepdims=True))
    grad_white = grad_unit / row_norm - white * (inner_prod / row_norm ** 3)
    pair_moment = jnp.dot(grad_white.T, white, precision=highest)
    lower_half = -(jnp.tril(pair_moment) - 0.5 * jnp.diag(jnp.diag(pair_moment)))
    left_solved = lax.linalg.triangular_solve(factor, lower_half, left_side=True, lower=True, transpose_a=True)
    solved = lax.linalg.triangular_solve(factor, left_solved, left_side=False, lower=True, transpose_a=False)
    grad_cov = 0.5 * (solved + solved.T)
    direct = lax.linalg.triangular_solve(factor, grad_white, left_side=False, lower=True, transpose_a=False)
    grad_cent = direct + 2.0 / (total_rows - 1) * jnp.dot(centered, grad_cov, precision=highest)
    grad_z = (grad_cent - lax.optimization_barrier(jnp.sum(grad_cent, axis=0)) / total_rows).astype(jnp.bfloat16)
    grad_weight = lax.dot_general(hidden.astype(jnp.float32), grad_z.astype(jnp.float32), (((0,), (0,)), ((), ())), preferred_element_type=jnp.float32)
    grad_hidden = jnp.dot(grad_z.astype(jnp.float32), weight.T.astype(jnp.float32), preferred_element_type=jnp.float32).astype(jnp.bfloat16)
    return (whitened, grad_weight, grad_hidden)
```

```python
import jax
import jax.numpy as jnp
from jax import lax
from jax.experimental import pallas as pl
from jax.experimental.pallas import tpu as pltpu
from jax.sharding import PartitionSpec as P

epsilon = 1e-06
highest = lax.Precision.HIGHEST
MESH = pl.DeviceIdType.MESH
NX, NY, NZ, NC = 4, 4, 8, 2
BLK = 128
MB = 1 << 20


def place():
    dp = lax.axis_index("dp")
    x = lax.axis_index("group")
    return x, lax.div(dp, NZ * NC), lax.rem(lax.div(dp, NC), NZ), lax.rem(dp, NC)


def device(x, y, z, c):
    return (x, (y * NZ + z) * NC + c)


def x_peers(x, y, z, c):
    return [device(lax.rem(x + k, NX), y, z, c) for k in range(1, NX)]


def y_peers(x, y, z, c):
    return [device(x, lax.rem(y + k, NY), z, c) for k in range(1, NY)]


def z_peers(x, y, z, c):
    return [device(x, y, lax.rem(z + k, NZ), c) for k in range(1, NZ)]


def meet(peers):
    barrier = pltpu.get_barrier_semaphore()
    for peer in peers:
        pl.semaphore_signal(barrier, inc=1, device_id=peer, device_id_type=MESH)
    pl.semaphore_wait(barrier, len(peers))


def send(src, dst, sems, slot, peer):
    copy = pltpu.make_async_remote_copy(
        src_ref=src,
        dst_ref=dst,
        send_sem=sems.at[0, slot],
        recv_sem=sems.at[1, slot],
        device_id=peer,
        device_id_type=MESH,
    )
    copy.start()
    return copy


def tile_sum_kernel(in_ref, out_ref, part, got_a, got_b, sems):
    x, y, z, c = place()
    near = []
    for k in range(1, NZ * NC):
        own = lax.rem(z * NC + c + k, NZ * NC)
        near.append(device(x, y, lax.div(own, NC), lax.rem(own, NC)))
    far = []
    for k in range(1, NX * NY):
        own = lax.rem(x * NY + y + k, NX * NY)
        far.append(device(lax.div(own, NY), lax.rem(own, NY), z, c))
    meet(near + far)
    copies = [send(in_ref, got_a.at[k], sems, k, peer) for k, peer in enumerate(near)]
    total = in_ref[...]
    for k, copy in enumerate(copies):
        copy.wait()
        total = total + got_a[k]
    part[...] = total
    copies = [send(part, got_b.at[k], sems, 15 + k, peer) for k, peer in enumerate(far)]
    for k, copy in enumerate(copies):
        copy.wait()
        total = total + got_b[k]
    out_ref[...] = total


def tile_sum(tile, collective_id):
    vmem = pl.BlockSpec(memory_space=pltpu.VMEM)
    return pl.pallas_call(
        tile_sum_kernel,
        out_shape=jax.ShapeDtypeStruct((8, 128), jnp.float32),
        in_specs=[vmem],
        out_specs=vmem,
        scratch_shapes=[
            pltpu.VMEM((8, 128), jnp.float32),
            pltpu.VMEM((15, 8, 128), jnp.float32),
            pltpu.VMEM((15, 8, 128), jnp.float32),
            pltpu.SemaphoreType.DMA((2, 30)),
        ],
        compiler_params=pltpu.CompilerParams(collective_id=collective_id, has_side_effects=True),
        name="tile_sum",
    )(tile)


TILES = 9


def all_sum_kernel(in_ref, out_ref, acc, got_c, got_1, acc_1, got_2, acc_2, got_z, full_z, sems):
    x, y, z, c = place()
    here = (x, y, z, c)
    across = device(x, y, z, 1 - c)
    xs, ys, zs = x_peers(*here), y_peers(*here), z_peers(*here)
    meet([across] + xs + ys + zs)
    copy = send(in_ref.at[1 - c], got_c, sems, 0, across)
    copy.wait()
    acc[...] = in_ref[c] + got_c[...]
    copies = []
    for k in range(3):
        copies.append(send(acc.at[0, lax.rem(x + k + 1, NX)], got_1.at[0, k], sems, 1 + k, xs[k]))
        copies.append(send(acc.at[1, lax.rem(y + k + 1, NY)], got_1.at[1, k], sems, 4 + k, ys[k]))
    for copy in copies:
        copy.wait()
    acc_1[0] = acc[0, x] + got_1[0, 0] + got_1[0, 1] + got_1[0, 2]
    acc_1[1] = acc[1, y] + got_1[1, 0] + got_1[1, 1] + got_1[1, 2]
    copies = []
    for k in range(3):
        copies.append(send(acc_1.at[0, lax.rem(y + k + 1, NY)], got_2.at[0, k], sems, 7 + k, ys[k]))
        copies.append(send(acc_1.at[1, lax.rem(x + k + 1, NX)], got_2.at[1, k], sems, 10 + k, xs[k]))
    for copy in copies:
        copy.wait()
    acc_2[pl.ds(0, TILES)] = acc_1[0, y] + got_2[0, 0] + got_2[0, 1] + got_2[0, 2]
    acc_2[pl.ds(TILES, TILES)] = acc_1[1, x] + got_2[1, 0] + got_2[1, 1] + got_2[1, 2]
    acc_2[pl.ds(2 * TILES, 24 - 2 * TILES)] = jnp.zeros((24 - 2 * TILES, 8, 128), jnp.float32)
    copies = []
    for k in range(7):
        copies.append(send(acc_2.at[pl.ds(3 * lax.rem(z + k + 1, NZ), 3)], got_z.at[k], sems, 13 + k, zs[k]))
    for copy in copies:
        copy.wait()
    own = acc_2[pl.ds(3 * z, 3)]
    for k in range(7):
        own = own + got_z[k]
    full_z[pl.ds(3 * z, 3)] = own
    mine = full_z.at[pl.ds(3 * z, 3)]
    copies = [send(mine, mine, sems, 20 + k, zs[k]) for k in range(7)]
    for copy in copies:
        copy.wait()
    out_ref[c, 0, x, y] = full_z[pl.ds(0, TILES)]
    out_ref[c, 1, y, x] = full_z[pl.ds(TILES, TILES)]
    first, second = out_ref.at[c, 0, x, y], out_ref.at[c, 1, y, x]
    copies = []
    for k in range(3):
        copies.append(send(first, first, sems, 27 + k, ys[k]))
        copies.append(send(second, second, sems, 30 + k, xs[k]))
    for copy in copies:
        copy.wait()
    first, second = out_ref.at[c, 0, x], out_ref.at[c, 1, y]
    copies = []
    for k in range(3):
        copies.append(send(first, first, sems, 33 + k, xs[k]))
        copies.append(send(second, second, sems, 36 + k, ys[k]))
    for copy in copies:
        copy.wait()
    send(out_ref.at[c], out_ref.at[c], sems, 39, across).wait()


def all_sum(packed, collective_id):
    vmem = pl.BlockSpec(memory_space=pltpu.VMEM)
    shape = (NC, 2, 4, 4, TILES, 8, 128)
    f32 = jnp.float32
    out = pl.pallas_call(
        all_sum_kernel,
        out_shape=jax.ShapeDtypeStruct(shape, f32),
        in_specs=[vmem],
        out_specs=vmem,
        scratch_shapes=[
            pltpu.VMEM(shape[1:], f32),
            pltpu.VMEM(shape[1:], f32),
            pltpu.VMEM((2, 3, 4, TILES, 8, 128), f32),
            pltpu.VMEM((2, 4, TILES, 8, 128), f32),
            pltpu.VMEM((2, 3, TILES, 8, 128), f32),
            pltpu.VMEM((24, 8, 128), f32),
            pltpu.VMEM((7, 3, 8, 128), f32),
            pltpu.VMEM((24, 8, 128), f32),
            pltpu.SemaphoreType.DMA((2, 40)),
        ],
        compiler_params=pltpu.CompilerParams(
            collective_id=collective_id, has_side_effects=True, vmem_limit_bytes=24 * MB
        ),
        name="all_sum",
    )(packed.reshape(shape))
    return out.reshape(36, BLK, BLK)


def scatter_sum_kernel(in_ref, out_ref, got_c, acc_a, acc_b, got_1, acc_1, got_2, acc_2, got_z, sems):
    x, y, z, c = place()
    here = (x, y, z, c)
    across = device(x, y, z, 1 - c)
    xs, ys, zs = x_peers(*here), y_peers(*here), z_peers(*here)
    meet([across] + xs + ys + zs)
    send(in_ref.at[:, :, :, 1 - c], got_c, sems, 0, across).wait()

    def add_core(step, carry):
        i = lax.div(step, NY)
        j = lax.rem(step, NY)
        both = in_ref[i, j, :, c] + got_c[i, j]
        acc_a[i, j] = both[:, :, :512]
        acc_b[j, i] = both[:, :, 512:]
        return carry

    lax.fori_loop(0, NX * NY, add_core, 0)
    copies = []
    for k in range(3):
        copies.append(send(acc_a.at[lax.rem(x + k + 1, NX)], got_1.at[0, k], sems, 1 + k, xs[k]))
        copies.append(send(acc_b.at[lax.rem(y + k + 1, NY)], got_1.at[1, k], sems, 4 + k, ys[k]))
    for copy in copies:
        copy.wait()

    def add_first(j, carry):
        acc_1[0, j] = acc_a[x, j] + got_1[0, 0, j] + got_1[0, 1, j] + got_1[0, 2, j]
        acc_1[1, j] = acc_b[y, j] + got_1[1, 0, j] + got_1[1, 1, j] + got_1[1, 2, j]
        return carry

    lax.fori_loop(0, 4, add_first, 0)
    copies = []
    for k in range(3):
        copies.append(send(acc_1.at[0, lax.rem(y + k + 1, NY)], got_2.at[0, k], sems, 7 + k, ys[k]))
        copies.append(send(acc_1.at[1, lax.rem(x + k + 1, NX)], got_2.at[1, k], sems, 10 + k, xs[k]))
    for copy in copies:
        copy.wait()
    acc_2[:, 0] = acc_1[0, y] + got_2[0, 0] + got_2[0, 1] + got_2[0, 2]
    acc_2[:, 1] = acc_1[1, x] + got_2[1, 0] + got_2[1, 1] + got_2[1, 2]
    copies = []
    for k in range(7):
        copies.append(send(acc_2.at[lax.rem(z + k + 1, NZ)], got_z.at[k], sems, 13 + k, zs[k]))
    for copy in copies:
        copy.wait()
    own = acc_2[z]
    for k in range(7):
        own = own + got_z[k]
    out_ref[:, :512] = own[0]
    out_ref[:, 512:] = own[1]


def scatter_sum(part, collective_id):
    vmem = pl.BlockSpec(memory_space=pltpu.VMEM)
    f32 = jnp.float32
    return pl.pallas_call(
        scatter_sum_kernel,
        out_shape=jax.ShapeDtypeStruct((8, 1024), f32),
        in_specs=[vmem],
        out_specs=vmem,
        scratch_shapes=[
            pltpu.VMEM((4, 4, 8, 8, 1024), f32),
            pltpu.VMEM((4, 4, 8, 8, 512), f32),
            pltpu.VMEM((4, 4, 8, 8, 512), f32),
            pltpu.VMEM((2, 3, 4, 8, 8, 512), f32),
            pltpu.VMEM((2, 4, 8, 8, 512), f32),
            pltpu.VMEM((2, 3, 8, 8, 512), f32),
            pltpu.VMEM((8, 2, 8, 512), f32),
            pltpu.VMEM((7, 2, 8, 512), f32),
            pltpu.SemaphoreType.DMA((2, 20)),
        ],
        compiler_params=pltpu.CompilerParams(
            collective_id=collective_id, has_side_effects=True, vmem_limit_bytes=40 * MB
        ),
        name="scatter_sum",
    )(part.reshape(NX, NY, NZ, NC, 8, 1024))


def pack(square):
    return jnp.stack(
        [square[i * BLK : (i + 1) * BLK, j * BLK : (j + 1) * BLK] for i in range(8) for j in range(i + 1)]
    )


def unpack(blocks):
    rows = []
    at = 0
    for i in range(8):
        row = [blocks[at + j] for j in range(i + 1)]
        at += i + 1
        if i < 7:
            row.append(jnp.zeros((BLK, (7 - i) * BLK), jnp.float32))
        rows.append(jnp.concatenate(row, axis=1))
    return jnp.concatenate(rows, axis=0)


def body(hidden, weight, partners):
    local_rows = hidden.shape[0]
    total_rows = local_rows * lax.axis_size("group") * lax.axis_size("dp")
    embedded = jnp.dot(hidden, weight, preferred_element_type=jnp.float32)
    sums = tile_sum(jnp.sum(embedded, axis=0).reshape(8, 128), 0)
    centered = embedded - sums.reshape(1, -1) / total_rows
    scatter = unpack(all_sum(pack(jnp.dot(centered.T, centered, precision=highest)), 1))
    cov = jnp.tril(scatter) / (total_rows - 1)
    factor = jnp.linalg.cholesky(cov, symmetrize_input=False)
    inv = lax.linalg.triangular_solve(
        factor, jnp.eye(1024, dtype=jnp.float32), left_side=True, lower=True
    )
    white = jnp.dot(centered, inv.T, precision=highest)
    whitened = white.astype(jnp.bfloat16)
    row_norm = jnp.sqrt(jnp.sum(white * white, axis=1, keepdims=True) + epsilon)
    unit = white / row_norm
    pick = (partners[0][:, None] == jnp.arange(local_rows, dtype=jnp.int32)[None, :]).astype(jnp.float32)
    grad_unit = 2.0 * (2.0 * unit - jnp.dot(pick + pick.T, unit, precision=highest))
    inner_prod = jnp.sum(white * grad_unit, axis=1, keepdims=True)
    grad_white = grad_unit / row_norm - white * (inner_prod / row_norm**3)
    grad_sums = tile_sum(jnp.sum(grad_white, axis=0).reshape(8, 128), 2).reshape(1, -1)
    pair = unpack(all_sum(pack(jnp.dot(grad_white.T, white, precision=highest)), 3))
    low = jnp.tril(pair, -1)
    mirror = low + low.T + pair * jnp.eye(1024, dtype=jnp.float32)
    total = grad_white - grad_sums / total_rows - jnp.dot(white, mirror, precision=highest) / (total_rows - 1)
    grad_z = jnp.dot(total, inv, precision=highest).astype(jnp.bfloat16)
    part = lax.dot_general(hidden, grad_z, (((0,), (0,)), ((), ())), preferred_element_type=jnp.float32)
    grad_weight = scatter_sum(part, 4)
    grad_hidden = jnp.dot(grad_z, weight.T, preferred_element_type=jnp.float32).astype(jnp.bfloat16)
    return (whitened, grad_weight, grad_hidden)


def solution(mesh):
    return jax.shard_map(
        body,
        mesh=mesh,
        in_specs=(P(("group", "dp"), None), P(), P(("group", "dp"), None)),
        out_specs=(P(("group", "dp"), None), P(("group", "dp"), None), P(("group", "dp"), None)),
        check_vma=False,
    )
```

```python
import functools

import jax
import jax.numpy as jnp
from jax import lax
from jax.experimental import pallas as pl
from jax.experimental.pallas import tpu as pltpu
from jax.sharding import PartitionSpec as P

epsilon = 1e-06
highest = lax.Precision.HIGHEST
MESH = pl.DeviceIdType.MESH
NX, NY, NZ, NC = 4, 4, 8, 2
BLK = 128
MB = 1 << 20


def place():
    dp = lax.axis_index("dp")
    x = lax.axis_index("group")
    return x, lax.div(dp, NZ * NC), lax.rem(lax.div(dp, NC), NZ), lax.rem(dp, NC)


def device(x, y, z, c):
    return (x, (y * NZ + z) * NC + c)


def x_peers(x, y, z, c):
    return [device(lax.rem(x + k, NX), y, z, c) for k in range(1, NX)]


def y_peers(x, y, z, c):
    return [device(x, lax.rem(y + k, NY), z, c) for k in range(1, NY)]


def z_peers(x, y, z, c):
    return [device(x, y, lax.rem(z + k, NZ), c) for k in range(1, NZ)]


def meet(peers):
    barrier = pltpu.get_barrier_semaphore()
    for peer in peers:
        pl.semaphore_signal(barrier, inc=1, device_id=peer, device_id_type=MESH)
    pl.semaphore_wait(barrier, len(peers))


def send(src, dst, sems, slot, peer):
    copy = pltpu.make_async_remote_copy(
        src_ref=src,
        dst_ref=dst,
        send_sem=sems.at[0, slot],
        recv_sem=sems.at[1, slot],
        device_id=peer,
        device_id_type=MESH,
    )
    copy.start()
    return copy


def tile_sum_kernel(in_ref, out_ref, part, got_a, got_b, sems):
    x, y, z, c = place()
    near = []
    for k in range(1, NZ * NC):
        own = lax.rem(z * NC + c + k, NZ * NC)
        near.append(device(x, y, lax.div(own, NC), lax.rem(own, NC)))
    far = []
    for k in range(1, NX * NY):
        own = lax.rem(x * NY + y + k, NX * NY)
        far.append(device(lax.div(own, NY), lax.rem(own, NY), z, c))
    meet(near + far)
    copies = [send(in_ref, got_a.at[k], sems, k, peer) for k, peer in enumerate(near)]
    total = in_ref[...]
    for k, copy in enumerate(copies):
        copy.wait()
        total = total + got_a[k]
    part[...] = total
    copies = [send(part, got_b.at[k], sems, 15 + k, peer) for k, peer in enumerate(far)]
    for k, copy in enumerate(copies):
        copy.wait()
        total = total + got_b[k]
    out_ref[...] = total


def tile_sum(tile, collective_id):
    vmem = pl.BlockSpec(memory_space=pltpu.VMEM)
    return pl.pallas_call(
        tile_sum_kernel,
        out_shape=jax.ShapeDtypeStruct((8, 128), jnp.float32),
        in_specs=[vmem],
        out_specs=vmem,
        scratch_shapes=[
            pltpu.VMEM((8, 128), jnp.float32),
            pltpu.VMEM((15, 8, 128), jnp.float32),
            pltpu.VMEM((15, 8, 128), jnp.float32),
            pltpu.SemaphoreType.DMA((2, 30)),
        ],
        compiler_params=pltpu.CompilerParams(collective_id=collective_id, has_side_effects=True),
        name="tile_sum",
    )(tile)


TILES = 9


def all_sum_kernel(in_ref, out_ref, acc, got_c, got_1, acc_1, got_2, acc_2, got_z, full_z, sems):
    x, y, z, c = place()
    here = (x, y, z, c)
    across = device(x, y, z, 1 - c)
    xs, ys, zs = x_peers(*here), y_peers(*here), z_peers(*here)
    meet([across] + xs + ys + zs)
    copy = send(in_ref.at[1 - c], got_c, sems, 0, across)
    copy.wait()
    acc[...] = in_ref[c] + got_c[...]
    copies = []
    for k in range(3):
        copies.append(send(acc.at[0, lax.rem(x + k + 1, NX)], got_1.at[0, k], sems, 1 + k, xs[k]))
        copies.append(send(acc.at[1, lax.rem(y + k + 1, NY)], got_1.at[1, k], sems, 4 + k, ys[k]))
    for copy in copies:
        copy.wait()
    acc_1[0] = acc[0, x] + got_1[0, 0] + got_1[0, 1] + got_1[0, 2]
    acc_1[1] = acc[1, y] + got_1[1, 0] + got_1[1, 1] + got_1[1, 2]
    copies = []
    for k in range(3):
        copies.append(send(acc_1.at[0, lax.rem(y + k + 1, NY)], got_2.at[0, k], sems, 7 + k, ys[k]))
        copies.append(send(acc_1.at[1, lax.rem(x + k + 1, NX)], got_2.at[1, k], sems, 10 + k, xs[k]))
    for copy in copies:
        copy.wait()
    acc_2[pl.ds(0, TILES)] = acc_1[0, y] + got_2[0, 0] + got_2[0, 1] + got_2[0, 2]
    acc_2[pl.ds(TILES, TILES)] = acc_1[1, x] + got_2[1, 0] + got_2[1, 1] + got_2[1, 2]
    acc_2[pl.ds(2 * TILES, 24 - 2 * TILES)] = jnp.zeros((24 - 2 * TILES, 8, 128), jnp.float32)
    copies = []
    for k in range(7):
        copies.append(send(acc_2.at[pl.ds(3 * lax.rem(z + k + 1, NZ), 3)], got_z.at[k], sems, 13 + k, zs[k]))
    for copy in copies:
        copy.wait()
    own = acc_2[pl.ds(3 * z, 3)]
    for k in range(7):
        own = own + got_z[k]
    full_z[pl.ds(3 * z, 3)] = own
    mine = full_z.at[pl.ds(3 * z, 3)]
    copies = [send(mine, mine, sems, 20 + k, zs[k]) for k in range(7)]
    for copy in copies:
        copy.wait()
    out_ref[c, 0, x, y] = full_z[pl.ds(0, TILES)]
    out_ref[c, 1, y, x] = full_z[pl.ds(TILES, TILES)]
    first, second = out_ref.at[c, 0, x, y], out_ref.at[c, 1, y, x]
    copies = []
    for k in range(3):
        copies.append(send(first, first, sems, 27 + k, ys[k]))
        copies.append(send(second, second, sems, 30 + k, xs[k]))
    for copy in copies:
        copy.wait()
    first, second = out_ref.at[c, 0, x], out_ref.at[c, 1, y]
    copies = []
    for k in range(3):
        copies.append(send(first, first, sems, 33 + k, xs[k]))
        copies.append(send(second, second, sems, 36 + k, ys[k]))
    for copy in copies:
        copy.wait()
    send(out_ref.at[c], out_ref.at[c], sems, 39, across).wait()


def all_sum(packed, collective_id):
    vmem = pl.BlockSpec(memory_space=pltpu.VMEM)
    shape = (NC, 2, 4, 4, TILES, 8, 128)
    f32 = jnp.float32
    out = pl.pallas_call(
        all_sum_kernel,
        out_shape=jax.ShapeDtypeStruct(shape, f32),
        in_specs=[vmem],
        out_specs=vmem,
        scratch_shapes=[
            pltpu.VMEM(shape[1:], f32),
            pltpu.VMEM(shape[1:], f32),
            pltpu.VMEM((2, 3, 4, TILES, 8, 128), f32),
            pltpu.VMEM((2, 4, TILES, 8, 128), f32),
            pltpu.VMEM((2, 3, TILES, 8, 128), f32),
            pltpu.VMEM((24, 8, 128), f32),
            pltpu.VMEM((7, 3, 8, 128), f32),
            pltpu.VMEM((24, 8, 128), f32),
            pltpu.SemaphoreType.DMA((2, 40)),
        ],
        compiler_params=pltpu.CompilerParams(
            collective_id=collective_id, has_side_effects=True, vmem_limit_bytes=24 * MB
        ),
        name="all_sum",
    )(packed.reshape(shape))
    return out.reshape(36, BLK, BLK)


def scatter_sum_kernel(in_ref, out_ref, got_c, acc_a, acc_b, got_1, acc_1, got_2, acc_2, got_z, sems):
    x, y, z, c = place()
    here = (x, y, z, c)
    across = device(x, y, z, 1 - c)
    xs, ys, zs = x_peers(*here), y_peers(*here), z_peers(*here)
    meet([across] + xs + ys + zs)
    send(in_ref.at[:, :, :, 1 - c], got_c, sems, 0, across).wait()

    def add_core(step, carry):
        i = lax.div(step, NY)
        j = lax.rem(step, NY)
        both = in_ref[i, j, :, c] + got_c[i, j]
        acc_a[i, j] = both[:, :, :512]
        acc_b[j, i] = both[:, :, 512:]
        return carry

    lax.fori_loop(0, NX * NY, add_core, 0)
    copies = []
    for k in range(3):
        copies.append(send(acc_a.at[lax.rem(x + k + 1, NX)], got_1.at[0, k], sems, 1 + k, xs[k]))
        copies.append(send(acc_b.at[lax.rem(y + k + 1, NY)], got_1.at[1, k], sems, 4 + k, ys[k]))
    for copy in copies:
        copy.wait()

    def add_first(j, carry):
        acc_1[0, j] = acc_a[x, j] + got_1[0, 0, j] + got_1[0, 1, j] + got_1[0, 2, j]
        acc_1[1, j] = acc_b[y, j] + got_1[1, 0, j] + got_1[1, 1, j] + got_1[1, 2, j]
        return carry

    lax.fori_loop(0, 4, add_first, 0)
    copies = []
    for k in range(3):
        copies.append(send(acc_1.at[0, lax.rem(y + k + 1, NY)], got_2.at[0, k], sems, 7 + k, ys[k]))
        copies.append(send(acc_1.at[1, lax.rem(x + k + 1, NX)], got_2.at[1, k], sems, 10 + k, xs[k]))
    for copy in copies:
        copy.wait()
    acc_2[:, 0] = acc_1[0, y] + got_2[0, 0] + got_2[0, 1] + got_2[0, 2]
    acc_2[:, 1] = acc_1[1, x] + got_2[1, 0] + got_2[1, 1] + got_2[1, 2]
    copies = []
    for k in range(7):
        copies.append(send(acc_2.at[lax.rem(z + k + 1, NZ)], got_z.at[k], sems, 13 + k, zs[k]))
    for copy in copies:
        copy.wait()
    own = acc_2[z]
    for k in range(7):
        own = own + got_z[k]
    out_ref[:, :512] = own[0]
    out_ref[:, 512:] = own[1]


def scatter_sum(part, collective_id):
    vmem = pl.BlockSpec(memory_space=pltpu.VMEM)
    f32 = jnp.float32
    return pl.pallas_call(
        scatter_sum_kernel,
        out_shape=jax.ShapeDtypeStruct((8, 1024), f32),
        in_specs=[vmem],
        out_specs=vmem,
        scratch_shapes=[
            pltpu.VMEM((4, 4, 8, 8, 1024), f32),
            pltpu.VMEM((4, 4, 8, 8, 512), f32),
            pltpu.VMEM((4, 4, 8, 8, 512), f32),
            pltpu.VMEM((2, 3, 4, 8, 8, 512), f32),
            pltpu.VMEM((2, 4, 8, 8, 512), f32),
            pltpu.VMEM((2, 3, 8, 8, 512), f32),
            pltpu.VMEM((8, 2, 8, 512), f32),
            pltpu.VMEM((7, 2, 8, 512), f32),
            pltpu.SemaphoreType.DMA((2, 20)),
        ],
        compiler_params=pltpu.CompilerParams(
            collective_id=collective_id, has_side_effects=True, vmem_limit_bytes=40 * MB
        ),
        name="scatter_sum",
    )(part.reshape(NX, NY, NZ, NC, 8, 1024))


def dots(a, b, ca=1, cb=0):
    return lax.dot_general(a, b, (((ca,), (cb,)), ((), ())), precision=highest, preferred_element_type=jnp.float32)


def inverse_factor_block(pan):
    sub = lax.broadcasted_iota(jnp.int32, (8, BLK), 0)
    lane = lax.broadcasted_iota(jnp.int32, (8, BLK), 1)

    def over_sublanes(tile, k):
        return jnp.broadcast_to(tile[k : k + 1, :], (8, BLK))

    def over_lanes(tile, k):
        return jnp.broadcast_to(tile[:, k : k + 1], (8, BLK))

    pan = list(pan)
    for p in range(16):
        base = 8 * p
        inside = (lane >= base) & (lane < base + 8)
        own = pan[p]
        cols = [over_lanes(own, base + k) for k in range(8)]
        low = {(i, k): over_sublanes(cols[k], i) for k in range(8) for i in range(k, 8)}
        own = jnp.where(inside, jnp.where(lane - base == sub, 1.0, 0.0), own)
        rows = [over_sublanes(own, k) for k in range(8)]
        ahead = p + 1 < 16
        if ahead:
            left = [over_lanes(pan[p + 1], base + k) for k in range(8)]
            after = jnp.where(inside, 0.0, pan[p + 1])
        scale = []
        for k in range(8):
            rs = lax.rsqrt(low[k, k])
            scale.append(rs)
            rows[k] = rows[k] * rs
            for i in range(k + 1, 8):
                low[i, k] = low[i, k] * rs
            if ahead:
                left[k] = left[k] * rs
                after = after - left[k] * rows[k]
            for i in range(k + 1, 8):
                for m in range(k + 1, i + 1):
                    low[i, m] = low[i, m] - low[i, k] * low[m, k]
                rows[i] = rows[i] - low[i, k] * rows[k]
                if ahead:
                    left[i] = left[i] - left[k] * low[i, k]
        done = rows[0]
        for k in range(1, 8):
            done = jnp.where(sub == k, rows[k], done)
        pan[p] = done
        if ahead:
            pan[p + 1] = after
        if p + 2 < 16:
            back = [None] * 8
            for k in range(7, -1, -1):
                t = rows[k]
                for m in range(k + 1, 8):
                    t = t - low[m, k] * back[m]
                back[k] = t * scale[k]
            for q in range(p + 2, 16):
                t = jnp.where(inside, 0.0, pan[q])
                for k in range(8):
                    t = t - over_lanes(pan[q], base + k) * back[k]
                pan[q] = t
    return [jnp.where(lane <= sub + 8 * p, pan[p], 0.0) for p in range(16)]


def inverse_factor_kernel(inv_count, in_ref, out_ref, inv_ref, row_ref):
    at = 0
    for i in range(8):
        for j in range(i + 1):
            block = in_ref[at] * inv_count
            if i == j:
                r = lax.broadcasted_iota(jnp.int32, (BLK, BLK), 0)
                l = lax.broadcasted_iota(jnp.int32, (BLK, BLK), 1)
                block = jnp.where(r >= l, block, block.T)
                out_ref[i * BLK : (i + 1) * BLK, j * BLK : (j + 1) * BLK] = block
            else:
                out_ref[i * BLK : (i + 1) * BLK, j * BLK : (j + 1) * BLK] = block
                out_ref[j * BLK : (j + 1) * BLK, i * BLK : (i + 1) * BLK] = block.T
            at += 1

    lane = lax.broadcasted_iota(jnp.int32, (BLK, 1024), 1)

    def step(i, carry):
        own = pl.ds(pl.multiple_of(i * BLK, BLK), BLK)
        pans = [out_ref[pl.ds(pl.multiple_of(i * BLK + 8 * p, 8), 8), own] for p in range(16)]
        for p, tile in enumerate(inverse_factor_block(pans)):
            inv_ref[8 * p : 8 * p + 8, :] = tile
        inv = inv_ref[...]
        row_ref[...] = dots(inv, out_ref[own, :])
        row_ref[:, own] = inv
        out_ref[own, :] = jnp.where(lane < (i + 1) * BLK, row_ref[...], 0.0)

        def lower(j, inner):
            its = pl.ds(pl.multiple_of(j * BLK, BLK), BLK)
            left = dots(out_ref[its, own], inv_ref[...], 1, 1)
            out_ref[its, own] = jnp.zeros((BLK, BLK), jnp.float32)
            out_ref[its, :] = out_ref[its, :] - dots(left, row_ref[...])
            return inner

        lax.fori_loop(i + 1, 8, lower, 0)
        return carry

    lax.fori_loop(0, 8, step, 0)


def inverse_factor(packed, count):
    vmem = pl.BlockSpec(memory_space=pltpu.VMEM)
    return pl.pallas_call(
        functools.partial(inverse_factor_kernel, 1.0 / count),
        out_shape=jax.ShapeDtypeStruct((1024, 1024), jnp.float32),
        in_specs=[vmem], out_specs=vmem,
        scratch_shapes=[pltpu.VMEM((BLK, BLK), jnp.float32), pltpu.VMEM((BLK, 1024), jnp.float32)],
        compiler_params=pltpu.CompilerParams(vmem_limit_bytes=32 * MB),
        name="inverse_factor",
    )(packed)


def store_lower(out_ref, a, b):
    for half in range(4):
        strip = dots(a[:, half * 256 : half * 256 + 256], b[:, : half * 256 + 256], 0, 0)
        for i in (2 * half, 2 * half + 1):
            for j in range(i + 1):
                r = (i - 2 * half) * BLK
                out_ref[i * (i + 1) // 2 + j] = strip[r : r + BLK, j * BLK : (j + 1) * BLK]


def center_kernel(count, emb_ref, sum_ref, cent_ref, packed_ref):
    cent = emb_ref[...] - sum_ref[...] * (1.0 / count)
    cent_ref[...] = cent
    store_lower(packed_ref, cent_ref, cent_ref)


def center(embedded, sums, count):
    vmem = pl.BlockSpec(memory_space=pltpu.VMEM)
    f32 = jnp.float32
    return pl.pallas_call(
        functools.partial(center_kernel, count),
        out_shape=(jax.ShapeDtypeStruct((256, 1024), f32), jax.ShapeDtypeStruct((36, BLK, BLK), f32)),
        in_specs=[vmem] * 2,
        out_specs=(vmem, vmem),
        compiler_params=pltpu.CompilerParams(vmem_limit_bytes=32 * MB),
        name="center",
    )(embedded, sums)


def white_kernel(cent_ref, inv_ref, partner_ref, whitened_ref, white_ref, grad_ref, packed_ref):
    bf16 = jnp.bfloat16
    for part in range(4):
        stop = part * 256 + 256
        white_ref[:, stop - 256 : stop] = dots(cent_ref[:, :stop], inv_ref[stop - 256 : stop, :stop], 1, 1)
    white = white_ref[...]
    whitened_ref[...] = white.astype(bf16)
    row_norm = jnp.sqrt(jnp.sum(white * white, axis=1, keepdims=True) + epsilon)
    unit = white / row_norm
    ids = lax.broadcasted_iota(jnp.int32, (256, 256), 0)
    pick = (ids == partner_ref[...]).astype(jnp.float32)
    pick = (pick + pick.T).astype(bf16)
    near = jnp.zeros_like(unit)
    rest = unit
    for _ in range(3):
        term = rest.astype(bf16)
        near = near + jnp.dot(pick, term, preferred_element_type=jnp.float32)
        rest = rest - term.astype(jnp.float32)
    grad_unit = 2.0 * (2.0 * unit - near)
    inner_prod = jnp.sum(white * grad_unit, axis=1, keepdims=True)
    grad = grad_unit / row_norm - white * (inner_prod / (row_norm * row_norm * row_norm))
    grad_ref[...] = grad
    store_lower(packed_ref, grad_ref, white_ref)
    sums = jnp.sum(grad, axis=0, keepdims=True)
    sub = lax.broadcasted_iota(jnp.int32, (8, BLK), 0)
    lane = lax.broadcasted_iota(jnp.int32, (8, BLK), 1)
    for i in range(8):
        at = i * (i + 1) // 2 + i
        own = jnp.broadcast_to(sums[:, i * BLK : (i + 1) * BLK], (8, BLK))
        swapped = pltpu.roll(own, 64, 1)
        tile = packed_ref[at, 0:8, :]
        tile = jnp.where((lane >= 64) & (sub == 0), swapped, jnp.where((lane >= 64) & (sub == 1), own, tile))
        packed_ref[at, 0:8, :] = tile


def whiten(centered, inv, partners):
    vmem = pl.BlockSpec(memory_space=pltpu.VMEM)
    f32 = jnp.float32
    return pl.pallas_call(
        white_kernel,
        out_shape=(
            jax.ShapeDtypeStruct((256, 1024), jnp.bfloat16),
            jax.ShapeDtypeStruct((256, 1024), f32),
            jax.ShapeDtypeStruct((256, 1024), f32),
            jax.ShapeDtypeStruct((36, BLK, BLK), f32),
        ),
        in_specs=[vmem] * 3,
        out_specs=(vmem,) * 4,
        compiler_params=pltpu.CompilerParams(vmem_limit_bytes=40 * MB),
        name="whiten",
    )(centered, inv, partners)


def grads_kernel(count, white_ref, grad_ref, packed_ref, inv_ref, hidden_ref, weight_ref, gh_ref, part_ref, mirror, total, grad_z):
    lane = lax.broadcasted_iota(jnp.int32, (1, BLK), 1)
    r = lax.broadcasted_iota(jnp.int32, (BLK, BLK), 0)
    l = lax.broadcasted_iota(jnp.int32, (BLK, BLK), 1)
    scale = 1.0 / (count - 1)
    for i in range(8):
        for j in range(i + 1):
            at = i * (i + 1) // 2 + j
            block = packed_ref[at]
            turned = block.T
            rows, cols = slice(i * BLK, (i + 1) * BLK), slice(j * BLK, (j + 1) * BLK)
            if i == j:
                mirror[rows, cols] = jnp.where(r >= l, block, turned) * scale
                first, second = packed_ref[at, 0:1, :], packed_ref[at, 1:2, :]
                sums = jnp.where(lane < 64, pltpu.roll(first, 64, 1), second)
                total[:, cols] = grad_ref[:, cols] - sums * (1.0 / count)
            else:
                mirror[rows, cols] = block * scale
                mirror[cols, rows] = turned * scale
    for part in range(4):
        cols = slice(part * 256, part * 256 + 256)
        total[:, cols] = total[:, cols] - dots(white_ref[...], mirror[:, cols])
    for part in range(4):
        start = part * 256
        cols = slice(start, start + 256)
        grad_z[:, cols] = dots(total[:, start:], inv_ref[start:, cols]).astype(jnp.bfloat16)

    def chunk(k, carry):
        own = pl.ds(pl.multiple_of(k * 256, 256), 256)
        part_ref[own, :] = lax.dot_general(
            hidden_ref[:, own], grad_z[...], (((0,), (0,)), ((), ())), preferred_element_type=jnp.float32
        )
        gh_ref[:, own] = lax.dot_general(
            grad_z[...], weight_ref[own, :], (((1,), (1,)), ((), ())), preferred_element_type=jnp.float32
        ).astype(jnp.bfloat16)
        return carry

    lax.fori_loop(0, 8, chunk, 0)


def grads(white, grad, packed, inv, hidden, weight, count):
    vmem = pl.BlockSpec(memory_space=pltpu.VMEM)
    f32 = jnp.float32
    return pl.pallas_call(
        functools.partial(grads_kernel, count),
        out_shape=(jax.ShapeDtypeStruct((256, 2048), jnp.bfloat16), jax.ShapeDtypeStruct((2048, 1024), f32)),
        in_specs=[vmem] * 6,
        out_specs=(vmem,) * 2,
        scratch_shapes=[
            pltpu.VMEM((1024, 1024), f32),
            pltpu.VMEM((256, 1024), f32),
            pltpu.VMEM((256, 1024), jnp.bfloat16),
        ],
        compiler_params=pltpu.CompilerParams(vmem_limit_bytes=48 * MB),
        name="grads",
    )(white, grad, packed, inv, hidden, weight)


def body(hidden, weight, partners):
    local_rows = hidden.shape[0]
    total_rows = local_rows * lax.axis_size("group") * lax.axis_size("dp")
    embedded = jnp.dot(hidden, weight, preferred_element_type=jnp.float32)
    sums = tile_sum(jnp.sum(embedded, axis=0).reshape(8, 128), 0)
    centered, packed = center(embedded, sums.reshape(1, -1), total_rows)
    inv = inverse_factor(all_sum(packed, 1), total_rows - 1)
    whitened, white, grad_white, packed = whiten(centered, inv, partners)
    grad_hidden, part = grads(white, grad_white, all_sum(packed, 2), inv, hidden, weight, total_rows)
    grad_weight = scatter_sum(part, 3)
    return (whitened, grad_weight, grad_hidden)


def solution(mesh):
    return jax.shard_map(
        body,
        mesh=mesh,
        in_specs=(P(("group", "dp"), None), P(), P(("group", "dp"), None)),
        out_specs=(P(("group", "dp"), None), P(("group", "dp"), None), P(("group", "dp"), None)),
        check_vma=False,
    )
```

```python
import functools

import jax
import jax.numpy as jnp
from jax import lax
from jax.experimental import pallas as pl
from jax.experimental.pallas import tpu as pltpu
from jax.sharding import PartitionSpec as P

epsilon = 1e-06
highest = lax.Precision.HIGHEST
MESH = pl.DeviceIdType.MESH
NX, NY, NZ, NC = 4, 4, 8, 2
BLK = 128
MB = 1 << 20
f32, bf16 = jnp.float32, jnp.bfloat16


def place():
    dp = lax.axis_index("dp")
    x = lax.axis_index("group")
    return x, lax.div(dp, NZ * NC), lax.rem(lax.div(dp, NC), NZ), lax.rem(dp, NC)


def device(x, y, z, c):
    return (x, (y * NZ + z) * NC + c)


def send(src, dst, sems, slot, peer):
    copy = pltpu.make_async_remote_copy(
        src_ref=src,
        dst_ref=dst,
        send_sem=sems.at[0, slot],
        recv_sem=sems.at[1, slot],
        device_id=peer,
        device_id_type=MESH,
    )
    copy.start()
    return copy


def wait(copies):
    for copy in copies:
        copy.wait()


def dots(a, b, ca=1, cb=0):
    return lax.dot_general(a, b, (((ca,), (cb,)), ((), ())), precision=highest, preferred_element_type=f32)


def dot16(a, b, ca=1, cb=0):
    return lax.dot_general(a, b, (((ca,), (cb,)), ((), ())), preferred_element_type=f32)


def span(start, size):
    return pl.ds(pl.multiple_of(start, size), size)


def inverse_factor_block(pan):
    sub = lax.broadcasted_iota(jnp.int32, (8, BLK), 0)
    lane = lax.broadcasted_iota(jnp.int32, (8, BLK), 1)

    def over_sublanes(tile, k):
        return jnp.broadcast_to(tile[k : k + 1, :], (8, BLK))

    def over_lanes(tile, k):
        return jnp.broadcast_to(tile[:, k : k + 1], (8, BLK))

    pan = list(pan)
    for p in range(16):
        base = 8 * p
        inside = (lane >= base) & (lane < base + 8)
        own = pan[p]
        cols = [over_lanes(own, base + k) for k in range(8)]
        low = {(i, k): over_sublanes(cols[k], i) for k in range(8) for i in range(k, 8)}
        own = jnp.where(inside, jnp.where(lane - base == sub, 1.0, 0.0), own)
        rows = [over_sublanes(own, k) for k in range(8)]
        ahead = p + 1 < 16
        if ahead:
            left = [over_lanes(pan[p + 1], base + k) for k in range(8)]
            after = jnp.where(inside, 0.0, pan[p + 1])
        scale = []
        for k in range(8):
            rs = lax.rsqrt(low[k, k])
            scale.append(rs)
            rows[k] = rows[k] * rs
            for i in range(k + 1, 8):
                low[i, k] = low[i, k] * rs
            if ahead:
                left[k] = left[k] * rs
                after = after - left[k] * rows[k]
            for i in range(k + 1, 8):
                for m in range(k + 1, i + 1):
                    low[i, m] = low[i, m] - low[i, k] * low[m, k]
                rows[i] = rows[i] - low[i, k] * rows[k]
                if ahead:
                    left[i] = left[i] - left[k] * low[i, k]
        done = rows[0]
        for k in range(1, 8):
            done = jnp.where(sub == k, rows[k], done)
        pan[p] = done
        if ahead:
            pan[p + 1] = after
        if p + 2 < 16:
            back = [None] * 8
            for k in range(7, -1, -1):
                t = rows[k]
                for m in range(k + 1, 8):
                    t = t - low[m, k] * back[m]
                back[k] = t * scale[k]
            for q in range(p + 2, 16):
                t = jnp.where(inside, 0.0, pan[q])
                for k in range(8):
                    t = t - over_lanes(pan[q], base + k) * back[k]
                pan[q] = t
    return [jnp.where(lane <= sub + 8 * p, pan[p], 0.0) for p in range(16)]


def inverse_factor(scale, in_ref, out_ref, inv_ref, row_ref):
    for i in range(8):
        for j in range(i + 1):
            block = get_block(in_ref, i, j) * scale
            rows, cols = slice(i * BLK, (i + 1) * BLK), slice(j * BLK, (j + 1) * BLK)
            turned = block.T
            if i == j:
                r = lax.broadcasted_iota(jnp.int32, (BLK, BLK), 0)
                l = lax.broadcasted_iota(jnp.int32, (BLK, BLK), 1)
                out_ref[rows, cols] = jnp.where(r >= l, block, turned)
            else:
                out_ref[rows, cols] = block
                out_ref[cols, rows] = turned
    lane = lax.broadcasted_iota(jnp.int32, (BLK, 1024), 1)

    def step(i, carry):
        own = span(i * BLK, BLK)
        pans = [out_ref[span(i * BLK + 8 * p, 8), own] for p in range(16)]
        for p, tile in enumerate(inverse_factor_block(pans)):
            inv_ref[8 * p : 8 * p + 8, :] = tile
        inv = inv_ref[...]
        row_ref[...] = dots(inv, out_ref[own, :])
        row_ref[:, own] = inv
        out_ref[own, :] = jnp.where(lane < (i + 1) * BLK, row_ref[...], 0.0)

        def lower(j, inner):
            its = span(j * BLK, BLK)
            left = dots(out_ref[its, own], inv_ref[...], 1, 1)
            out_ref[its, own] = jnp.zeros((BLK, BLK), f32)
            out_ref[its, :] = out_ref[its, :] - dots(left, row_ref[...])
            return inner

        lax.fori_loop(i + 1, 8, lower, 0)
        return carry

    lax.fori_loop(0, 8, step, 0)


def get_block(ref, i, j):
    at = i * (i + 1) // 2 + j
    return ref[16 * at : 16 * at + 16].reshape(BLK, BLK)


def store_lower(out_ref, a, b):
    for half in range(4):
        strip = dots(a[:, half * 256 : half * 256 + 256], b[:, : half * 256 + 256], 0, 0)
        for i in (2 * half, 2 * half + 1):
            for j in range(i + 1):
                r = (i - 2 * half) * BLK
                at = i * (i + 1) // 2 + j
                out_ref[16 * at : 16 * at + 16] = strip[r : r + BLK, j * BLK : (j + 1) * BLK].reshape(16, 8, BLK)


def tile_sum(here, tile, got, sems):
    x, y, z, c = here
    copies = []
    for k in range(1, NZ * NC):
        own = lax.rem(z * NC + c + k, NZ * NC)
        peer = device(x, y, lax.div(own, NC), lax.rem(own, NC))
        copies.append(send(tile.at[0], got.at[0, k - 1], sems, k - 1, peer))
    wait(copies)
    total = tile[0]
    for k in range(15):
        total = total + got[0, k]
    tile[1] = total
    copies = []
    for k in range(1, NX * NY):
        own = lax.rem(x * NY + y + k, NX * NY)
        peer = device(lax.div(own, NY), lax.rem(own, NY), z, c)
        copies.append(send(tile.at[1], got.at[1, k - 1], sems, 14 + k, peer))
    wait(copies)
    for k in range(15):
        total = total + got[1, k]
    return total


T = 9


def all_sum(here, in_ref, out_ref, acc, got_c, got_1, acc_1, got_2, acc_2, got_z, full_z, sems):
    x, y, z, c = here
    across = device(x, y, z, 1 - c)
    xs = [device(lax.rem(x + k, NX), y, z, c) for k in range(1, NX)]
    ys = [device(x, lax.rem(y + k, NY), z, c) for k in range(1, NY)]
    zs = [device(x, y, lax.rem(z + k, NZ), c) for k in range(1, NZ)]
    x_at = [lax.rem(x + k, NX) for k in range(1, NX)]
    y_at = [lax.rem(y + k, NY) for k in range(1, NY)]
    z_at = [lax.rem(z + k, NZ) for k in range(1, NZ)]
    send(in_ref.at[pl.ds((1 - c) * 288, 288)], got_c, sems, 0, across).wait()
    acc[...] = in_ref[pl.ds(c * 288, 288)] + got_c[...]
    copies = []
    for k in range(3):
        copies.append(send(acc.at[pl.ds(x_at[k] * 36, 36)], got_1.at[0, k], sems, 1 + k, xs[k]))
        copies.append(send(acc.at[pl.ds(144 + y_at[k] * 36, 36)], got_1.at[1, k], sems, 4 + k, ys[k]))
    wait(copies)
    acc_1[0] = acc[pl.ds(x * 36, 36)] + got_1[0, 0] + got_1[0, 1] + got_1[0, 2]
    acc_1[1] = acc[pl.ds(144 + y * 36, 36)] + got_1[1, 0] + got_1[1, 1] + got_1[1, 2]
    copies = []
    for k in range(3):
        copies.append(send(acc_1.at[0, pl.ds(y_at[k] * T, T)], got_2.at[0, k], sems, 7 + k, ys[k]))
        copies.append(send(acc_1.at[1, pl.ds(x_at[k] * T, T)], got_2.at[1, k], sems, 10 + k, xs[k]))
    wait(copies)
    acc_2[0:T] = acc_1[0, pl.ds(y * T, T)] + got_2[0, 0] + got_2[0, 1] + got_2[0, 2]
    acc_2[T : 2 * T] = acc_1[1, pl.ds(x * T, T)] + got_2[1, 0] + got_2[1, 1] + got_2[1, 2]
    acc_2[2 * T : 24] = jnp.zeros((24 - 2 * T, 8, 128), f32)
    wait([send(acc_2.at[pl.ds(3 * z_at[k], 3)], got_z.at[k], sems, 13 + k, zs[k]) for k in range(7)])
    own = acc_2[pl.ds(3 * z, 3)]
    for k in range(7):
        own = own + got_z[k]
    mine = full_z.at[pl.ds(3 * z, 3)]
    mine[...] = own
    wait([send(mine, mine, sems, 20 + k, zs[k]) for k in range(7)])
    base = c * 288
    first, second = out_ref.at[pl.ds(base + (x * 4 + y) * T, T)], out_ref.at[pl.ds(base + 144 + (y * 4 + x) * T, T)]
    first[...] = full_z[0:T]
    second[...] = full_z[T : 2 * T]
    copies = []
    for k in range(3):
        copies.append(send(first, first, sems, 27 + k, ys[k]))
        copies.append(send(second, second, sems, 30 + k, xs[k]))
    wait(copies)
    first, second = out_ref.at[pl.ds(base + x * 36, 36)], out_ref.at[pl.ds(base + 144 + y * 36, 36)]
    copies = []
    for k in range(3):
        copies.append(send(first, first, sems, 33 + k, xs[k]))
        copies.append(send(second, second, sems, 36 + k, ys[k]))
    wait(copies)
    first = out_ref.at[pl.ds(base, 288)]
    send(first, first, sems, 39, across).wait()


def kernel(count, hidden, weight, partner, whitened, grad_weight, grad_hidden,
           tile, tile_got, tile_sems,
           cent, packed, summed, acc, got_c, got_1, acc_1, got_2, acc_2, got_z, full_z, sems_1, sems_2,
           inv, inv_block, inv_row, white, grad, mirror, total, grad_z,
           strip, away, w_got_c, acc_a, acc_b, w_got_1, w_acc_1, w_got_2, w_acc_2, w_got_z, w_sems):
    here = place()
    x, y, z, c = here
    barrier = pltpu.get_barrier_semaphore()
    for k in range(1, NZ * NC):
        own = lax.rem(z * NC + c + k, NZ * NC)
        pl.semaphore_signal(barrier, inc=1, device_id=device(x, y, lax.div(own, NC), lax.rem(own, NC)), device_id_type=MESH)
    for k in range(1, NX * NY):
        own = lax.rem(x * NY + y + k, NX * NY)
        pl.semaphore_signal(barrier, inc=1, device_id=device(lax.div(own, NY), lax.rem(own, NY), z, c), device_id_type=MESH)
    for part in range(4):
        cols = slice(part * 256, part * 256 + 256)
        strip_e = dot16(hidden[...], weight[:, cols])
        cent[:, cols] = strip_e
        sums = jnp.sum(strip_e, axis=0, keepdims=True)
        tile[0, 2 * part : 2 * part + 1, :] = sums[:, :BLK]
        tile[0, 2 * part + 1 : 2 * part + 2, :] = sums[:, BLK:]
    pl.semaphore_wait(barrier, NZ * NC + NX * NY - 2)
    mean = tile_sum(here, tile, tile_got, tile_sems) * (1.0 / count)
    for i in range(8):
        cols = slice(i * BLK, (i + 1) * BLK)
        cent[:, cols] = cent[:, cols] - mean[i : i + 1, :]
    store_lower(packed, cent, cent)
    all_sum(here, packed, summed, acc, got_c, got_1, acc_1, got_2, acc_2, got_z, full_z, sems_1)
    inverse_factor(1.0 / (count - 1), summed, inv, inv_block, inv_row)
    for part in range(4):
        stop = part * 256 + 256
        white[:, stop - 256 : stop] = dots(cent[:, :stop], inv[stop - 256 : stop, :stop], 1, 1)
    wh = white[...]
    whitened[...] = wh.astype(bf16)
    row_norm = jnp.sqrt(jnp.sum(wh * wh, axis=1, keepdims=True) + epsilon)
    unit = wh / row_norm
    pick = (lax.broadcasted_iota(jnp.int32, (256, 256), 0) == partner[...]).astype(f32)
    pick = (pick + pick.T).astype(bf16)
    near = jnp.zeros_like(unit)
    rest = unit
    for _ in range(3):
        term = rest.astype(bf16)
        near = near + dot16(pick, term)
        rest = rest - term.astype(f32)
    grad_unit = 2.0 * (2.0 * unit - near)
    inner_prod = jnp.sum(wh * grad_unit, axis=1, keepdims=True)
    gr = grad_unit / row_norm - wh * (inner_prod / (row_norm * row_norm * row_norm))
    grad[...] = gr
    store_lower(packed, grad, white)
    sums = jnp.sum(gr, axis=0, keepdims=True)
    sub = lax.broadcasted_iota(jnp.int32, (8, BLK), 0)
    lane = lax.broadcasted_iota(jnp.int32, (8, BLK), 1)
    for i in range(8):
        at = 16 * (i * (i + 1) // 2 + i)
        own = jnp.broadcast_to(sums[:, i * BLK : (i + 1) * BLK], (8, BLK))
        swapped = pltpu.roll(own, 64, 1)
        packed[at] = jnp.where(
            (lane >= 64) & (sub == 0), swapped, jnp.where((lane >= 64) & (sub == 1), own, packed[at])
        )
    all_sum(here, packed, summed, acc, got_c, got_1, acc_1, got_2, acc_2, got_z, full_z, sems_2)
    lane = lax.broadcasted_iota(jnp.int32, (1, BLK), 1)
    r = lax.broadcasted_iota(jnp.int32, (BLK, BLK), 0)
    l = lax.broadcasted_iota(jnp.int32, (BLK, BLK), 1)
    scale = 1.0 / (count - 1)
    for i in range(8):
        for j in range(i + 1):
            block = get_block(summed, i, j)
            turned = block.T
            rows, cols = slice(i * BLK, (i + 1) * BLK), slice(j * BLK, (j + 1) * BLK)
            if i == j:
                mirror[rows, cols] = jnp.where(r >= l, block, turned) * scale
                sums = jnp.where(lane < 64, pltpu.roll(block[0:1, :], 64, 1), block[1:2, :])
                total[:, cols] = grad[:, cols] - sums * (1.0 / count)
            else:
                mirror[rows, cols] = block * scale
                mirror[cols, rows] = turned * scale
    for part in range(4):
        cols = slice(part * 256, part * 256 + 256)
        total[:, cols] = total[:, cols] - dots(white[...], mirror[:, cols])
    for part in range(4):
        start = part * 256
        grad_z[:, start : start + 256] = dots(total[:, start:], inv[start:, start : start + 256]).astype(bf16)
    across = device(x, y, z, 1 - c)
    xs = [device(lax.rem(x + k, NX), y, z, c) for k in range(1, NX)]
    ys = [device(x, lax.rem(y + k, NY), z, c) for k in range(1, NY)]
    zs = [device(x, y, lax.rem(z + k, NZ), c) for k in range(1, NZ)]
    copies = []
    for i in range(4):
        def strips(j, carry):
            own = span(i * 512 + j * BLK, BLK)
            strip[...] = dot16(hidden[:, own], grad_z[...], 0, 0).reshape(NZ, NC, 8, 1024)
            away[i, j] = strip[:, 1 - c]
            keep = strip[:, c]
            acc_a[i, j] = keep[:, :, :512]
            acc_b[j, i] = keep[:, :, 512:]
            return carry

        lax.fori_loop(0, 4, strips, 0)
        copies.append(send(away.at[i], w_got_c.at[i], w_sems, i, across))
    for i in range(4):
        copies[i].wait()

        def add_core(j, carry):
            acc_a[i, j] = acc_a[i, j] + w_got_c[i, j, :, :, :512]
            acc_b[j, i] = acc_b[j, i] + w_got_c[i, j, :, :, 512:]
            return carry

        lax.fori_loop(0, 4, add_core, 0)
    copies = []
    for k in range(3):
        copies.append(send(acc_a.at[lax.rem(x + k + 1, NX)], w_got_1.at[0, k], w_sems, 4 + k, xs[k]))
        copies.append(send(acc_b.at[lax.rem(y + k + 1, NY)], w_got_1.at[1, k], w_sems, 7 + k, ys[k]))

    def hidden_part(k, carry):
        own = span(k * 256, 256)
        grad_hidden[:, own] = dot16(grad_z[...], weight[own, :], 1, 1).astype(bf16)
        return carry

    lax.fori_loop(0, 8, hidden_part, 0)
    wait(copies)

    def add_first(j, carry):
        w_acc_1[0, j] = acc_a[x, j] + w_got_1[0, 0, j] + w_got_1[0, 1, j] + w_got_1[0, 2, j]
        w_acc_1[1, j] = acc_b[y, j] + w_got_1[1, 0, j] + w_got_1[1, 1, j] + w_got_1[1, 2, j]
        return carry

    lax.fori_loop(0, 4, add_first, 0)
    copies = []
    for k in range(3):
        copies.append(send(w_acc_1.at[0, lax.rem(y + k + 1, NY)], w_got_2.at[0, k], w_sems, 10 + k, ys[k]))
        copies.append(send(w_acc_1.at[1, lax.rem(x + k + 1, NX)], w_got_2.at[1, k], w_sems, 13 + k, xs[k]))
    wait(copies)
    w_acc_2[:, 0] = w_acc_1[0, y] + w_got_2[0, 0] + w_got_2[0, 1] + w_got_2[0, 2]
    w_acc_2[:, 1] = w_acc_1[1, x] + w_got_2[1, 0] + w_got_2[1, 1] + w_got_2[1, 2]
    wait([send(w_acc_2.at[lax.rem(z + k + 1, NZ)], w_got_z.at[k], w_sems, 16 + k, zs[k]) for k in range(7)])
    own = w_acc_2[z]
    for k in range(7):
        own = own + w_got_z[k]
    grad_weight[:, :512] = own[0]
    grad_weight[:, 512:] = own[1]


def body(hidden, weight, partners):
    count = hidden.shape[0] * lax.axis_size("group") * lax.axis_size("dp")
    vmem = pl.BlockSpec(memory_space=pltpu.VMEM)
    V, sem = pltpu.VMEM, pltpu.SemaphoreType.DMA
    return pl.pallas_call(
        functools.partial(kernel, count),
        out_shape=(
            jax.ShapeDtypeStruct((256, 1024), bf16),
            jax.ShapeDtypeStruct((8, 1024), f32),
            jax.ShapeDtypeStruct((256, 2048), bf16),
        ),
        in_specs=[vmem] * 3,
        out_specs=(vmem,) * 3,
        scratch_shapes=[
            V((2, 8, 128), f32), V((2, 15, 8, 128), f32), sem((2, 30)),
            V((256, 1024), f32), V((576, 8, 128), f32), V((576, 8, 128), f32),
            V((288, 8, 128), f32), V((288, 8, 128), f32), V((2, 3, 36, 8, 128), f32), V((2, 36, 8, 128), f32),
            V((2, 3, T, 8, 128), f32), V((24, 8, 128), f32), V((7, 3, 8, 128), f32), V((24, 8, 128), f32),
            sem((2, 40)), sem((2, 40)),
            V((1024, 1024), f32), V((BLK, BLK), f32), V((BLK, 1024), f32), V((256, 1024), f32),
            V((256, 1024), f32), V((1024, 1024), f32), V((256, 1024), f32), V((256, 1024), bf16),
            V((8, 2, 8, 1024), f32), V((4, 4, 8, 8, 1024), f32), V((4, 4, 8, 8, 1024), f32),
            V((4, 4, 8, 8, 512), f32), V((4, 4, 8, 8, 512), f32), V((2, 3, 4, 8, 8, 512), f32),
            V((2, 4, 8, 8, 512), f32), V((2, 3, 8, 8, 512), f32), V((8, 2, 8, 512), f32), V((7, 2, 8, 512), f32),
            sem((2, 23)),
        ],
        compiler_params=pltpu.CompilerParams(collective_id=0, has_side_effects=True, vmem_limit_bytes=60 * MB),
        name="whitening_step",
    )(hidden, weight, partners)


def solution(mesh):
    return jax.shard_map(
        body,
        mesh=mesh,
        in_specs=(P(("group", "dp"), None), P(), P(("group", "dp"), None)),
        out_specs=(P(("group", "dp"), None), P(("group", "dp"), None), P(("group", "dp"), None)),
        check_vma=False,
    )
```

```python
import functools

import jax
import jax.numpy as jnp
from jax import lax
from jax.experimental import pallas as pl
from jax.experimental.pallas import tpu as pltpu
from jax.sharding import PartitionSpec as P

epsilon = 1e-06
highest = lax.Precision.HIGHEST
MESH = pl.DeviceIdType.MESH
NX, NY, NZ, NC = 4, 4, 8, 2
BLK = 128
MB = 1 << 20
f32, bf16 = jnp.float32, jnp.bfloat16


def place():
    dp = lax.axis_index("dp")
    x = lax.axis_index("group")
    return x, lax.div(dp, NZ * NC), lax.rem(lax.div(dp, NC), NZ), lax.rem(dp, NC)


def device(x, y, z, c):
    return (x, (y * NZ + z) * NC + c)


def remote(src, dst, sems, slot, peer):
    return pltpu.make_async_remote_copy(
        src_ref=src,
        dst_ref=dst,
        send_sem=sems.at[0, slot],
        recv_sem=sems.at[1, slot],
        device_id=peer,
        device_id_type=MESH,
    )


def start(copies):
    for copy in copies:
        copy.start()


def wait(copies):
    for copy in copies:
        copy.wait()


def send(src, dst, sems, slot, peer):
    copy = remote(src, dst, sems, slot, peer)
    copy.start()
    return copy


def nothing():
    pass


def dots(a, b, ca=1, cb=0):
    return lax.dot_general(a, b, (((ca,), (cb,)), ((), ())), precision=highest, preferred_element_type=f32)


def dot16(a, b, ca=1, cb=0):
    return lax.dot_general(a, b, (((ca,), (cb,)), ((), ())), preferred_element_type=f32)


def span(start, size):
    return pl.ds(pl.multiple_of(start, size), size)


def inverse_factor_block(pan):
    sub = lax.broadcasted_iota(jnp.int32, (8, BLK), 0)
    lane = lax.broadcasted_iota(jnp.int32, (8, BLK), 1)

    def over_sublanes(tile, k):
        return jnp.broadcast_to(tile[k : k + 1, :], (8, BLK))

    def over_lanes(tile, k):
        return jnp.broadcast_to(tile[:, k : k + 1], (8, BLK))

    pan = list(pan)
    for p in range(16):
        base = 8 * p
        inside = (lane >= base) & (lane < base + 8)
        own = pan[p]
        cols = [over_lanes(own, base + k) for k in range(8)]
        low = {(i, k): over_sublanes(cols[k], i) for k in range(8) for i in range(k, 8)}
        own = jnp.where(inside, jnp.where(lane - base == sub, 1.0, 0.0), own)
        rows = [over_sublanes(own, k) for k in range(8)]
        ahead = p + 1 < 16
        if ahead:
            left = [over_lanes(pan[p + 1], base + k) for k in range(8)]
            after = jnp.where(inside, 0.0, pan[p + 1])
        scale = []
        for k in range(8):
            rs = lax.rsqrt(low[k, k])
            scale.append(rs)
            rows[k] = rows[k] * rs
            for i in range(k + 1, 8):
                low[i, k] = low[i, k] * rs
            if ahead:
                left[k] = left[k] * rs
                after = after - left[k] * rows[k]
            for i in range(k + 1, 8):
                for m in range(k + 1, i + 1):
                    low[i, m] = low[i, m] - low[i, k] * low[m, k]
                rows[i] = rows[i] - low[i, k] * rows[k]
                if ahead:
                    left[i] = left[i] - left[k] * low[i, k]
        done = rows[0]
        for k in range(1, 8):
            done = jnp.where(sub == k, rows[k], done)
        pan[p] = done
        if ahead:
            pan[p + 1] = after
        if p + 2 < 16:
            back = [None] * 8
            for k in range(7, -1, -1):
                t = rows[k]
                for m in range(k + 1, 8):
                    t = t - low[m, k] * back[m]
                back[k] = t * scale[k]
            for q in range(p + 2, 16):
                t = jnp.where(inside, 0.0, pan[q])
                for k in range(8):
                    t = t - over_lanes(pan[q], base + k) * back[k]
                pan[q] = t
    return [jnp.where(lane <= sub + 8 * p, pan[p], 0.0) for p in range(16)]


def inverse_factor(scale, in_ref, out_ref, inv_ref, row_ref, beside):
    for i in range(8):
        for j in range(i + 1):
            block = get_block(in_ref, i, j) * scale
            rows, cols = slice(i * BLK, (i + 1) * BLK), slice(j * BLK, (j + 1) * BLK)
            turned = block.T
            if i == j:
                r = lax.broadcasted_iota(jnp.int32, (BLK, BLK), 0)
                l = lax.broadcasted_iota(jnp.int32, (BLK, BLK), 1)
                out_ref[rows, cols] = jnp.where(r >= l, block, turned)
            else:
                out_ref[rows, cols] = block
                out_ref[cols, rows] = turned
    lane = lax.broadcasted_iota(jnp.int32, (BLK, 1024), 1)

    def step(i, carry):
        for at, work in beside.items():
            pl.when(i == at)(work)
        own = span(i * BLK, BLK)
        pans = [out_ref[span(i * BLK + 8 * p, 8), own] for p in range(16)]
        for p, tile in enumerate(inverse_factor_block(pans)):
            inv_ref[8 * p : 8 * p + 8, :] = tile
        inv = inv_ref[...]
        row_ref[...] = dots(inv, out_ref[own, :])
        row_ref[:, own] = inv
        out_ref[own, :] = jnp.where(lane < (i + 1) * BLK, row_ref[...], 0.0)

        def lower(j, inner):
            its = span(j * BLK, BLK)
            left = dots(out_ref[its, own], inv_ref[...], 1, 1)
            out_ref[its, own] = jnp.zeros((BLK, BLK), f32)
            out_ref[its, :] = out_ref[its, :] - dots(left, row_ref[...])
            return inner

        lax.fori_loop(i + 1, 8, lower, 0)
        return carry

    lax.fori_loop(0, 8, step, 0)


def get_block(ref, i, j):
    at = i * (i + 1) // 2 + j
    return ref[16 * at : 16 * at + 16].reshape(BLK, BLK)


def store_lower(out_ref, a, b):
    for half in range(4):
        strip = dots(a[:, half * 256 : half * 256 + 256], b[:, : half * 256 + 256], 0, 0)
        for i in (2 * half, 2 * half + 1):
            for j in range(i + 1):
                r = (i - 2 * half) * BLK
                at = i * (i + 1) // 2 + j
                out_ref[16 * at : 16 * at + 16] = strip[r : r + BLK, j * BLK : (j + 1) * BLK].reshape(16, 8, BLK)


def tile_sum(here, tile, got, sems):
    x, y, z, c = here
    copies = []
    for k in range(1, NZ * NC):
        own = lax.rem(z * NC + c + k, NZ * NC)
        peer = device(x, y, lax.div(own, NC), lax.rem(own, NC))
        copies.append(send(tile.at[0], got.at[0, k - 1], sems, k - 1, peer))
    wait(copies)
    total = tile[0]
    for k in range(15):
        total = total + got[0, k]
    tile[1] = total
    copies = []
    for k in range(1, NX * NY):
        own = lax.rem(x * NY + y + k, NX * NY)
        peer = device(lax.div(own, NY), lax.rem(own, NY), z, c)
        copies.append(send(tile.at[1], got.at[1, k - 1], sems, 14 + k, peer))
    wait(copies)
    for k in range(15):
        total = total + got[1, k]
    tile[2] = total


T = 9


def all_sum(here, in_ref, out_ref, acc, got_c, got_1, acc_1, got_2, acc_2, got_z, full_z, sems, during, after):
    x, y, z, c = here
    across = device(x, y, z, 1 - c)
    xs = [device(lax.rem(x + k, NX), y, z, c) for k in range(1, NX)]
    ys = [device(x, lax.rem(y + k, NY), z, c) for k in range(1, NY)]
    zs = [device(x, y, lax.rem(z + k, NZ), c) for k in range(1, NZ)]
    x_at = [lax.rem(x + k, NX) for k in range(1, NX)]
    y_at = [lax.rem(y + k, NY) for k in range(1, NY)]
    z_at = [lax.rem(z + k, NZ) for k in range(1, NZ)]
    copy = send(in_ref.at[pl.ds((1 - c) * 288, 288)], got_c, sems, 0, across)
    during.get("core", nothing)()
    copy.wait()
    after.get("core", nothing)()
    acc[...] = in_ref[pl.ds(c * 288, 288)] + got_c[...]
    copies = []
    for k in range(3):
        copies.append(send(acc.at[pl.ds(x_at[k] * 36, 36)], got_1.at[0, k], sems, 1 + k, xs[k]))
        copies.append(send(acc.at[pl.ds(144 + y_at[k] * 36, 36)], got_1.at[1, k], sems, 4 + k, ys[k]))
    during.get("first", nothing)()
    wait(copies)
    after.get("first", nothing)()
    acc_1[0] = acc[pl.ds(x * 36, 36)] + got_1[0, 0] + got_1[0, 1] + got_1[0, 2]
    acc_1[1] = acc[pl.ds(144 + y * 36, 36)] + got_1[1, 0] + got_1[1, 1] + got_1[1, 2]
    copies = []
    for k in range(3):
        copies.append(send(acc_1.at[0, pl.ds(y_at[k] * T, T)], got_2.at[0, k], sems, 7 + k, ys[k]))
        copies.append(send(acc_1.at[1, pl.ds(x_at[k] * T, T)], got_2.at[1, k], sems, 10 + k, xs[k]))
    wait(copies)
    acc_2[0:T] = acc_1[0, pl.ds(y * T, T)] + got_2[0, 0] + got_2[0, 1] + got_2[0, 2]
    acc_2[T : 2 * T] = acc_1[1, pl.ds(x * T, T)] + got_2[1, 0] + got_2[1, 1] + got_2[1, 2]
    acc_2[2 * T : 24] = jnp.zeros((24 - 2 * T, 8, 128), f32)
    wait([send(acc_2.at[pl.ds(3 * z_at[k], 3)], got_z.at[k], sems, 13 + k, zs[k]) for k in range(7)])
    own = acc_2[pl.ds(3 * z, 3)]
    for k in range(7):
        own = own + got_z[k]
    mine = full_z.at[pl.ds(3 * z, 3)]
    mine[...] = own
    wait([send(mine, mine, sems, 20 + k, zs[k]) for k in range(7)])
    base = c * 288
    first, second = out_ref.at[pl.ds(base + (x * 4 + y) * T, T)], out_ref.at[pl.ds(base + 144 + (y * 4 + x) * T, T)]
    first[...] = full_z[0:T]
    second[...] = full_z[T : 2 * T]
    copies = []
    for k in range(3):
        copies.append(send(first, first, sems, 27 + k, ys[k]))
        copies.append(send(second, second, sems, 30 + k, xs[k]))
    wait(copies)
    first, second = out_ref.at[pl.ds(base + x * 36, 36)], out_ref.at[pl.ds(base + 144 + y * 36, 36)]
    copies = []
    for k in range(3):
        copies.append(send(first, first, sems, 33 + k, xs[k]))
        copies.append(send(second, second, sems, 36 + k, ys[k]))
    wait(copies)
    first = out_ref.at[pl.ds(base, 288)]
    copy = send(first, first, sems, 39, across)
    during.get("core back", nothing)()
    copy.wait()


class RowScatter:
    def __init__(self, here, hidden, high, low, strip, away, got_c, acc_a, acc_b, got_1, acc_1, got_2, acc_2, got_z, sems):
        self.here, self.hidden, self.high, self.low, self.strip, self.away = here, hidden, high, low, strip, away
        self.got_c, self.acc_a, self.acc_b, self.got_1, self.acc_1 = got_c, acc_a, acc_b, got_1, acc_1
        self.got_2, self.acc_2, self.got_z, self.sems = got_2, acc_2, got_z, sems

    def strips(self):
        c = self.here[3]

        def one(k, carry):
            i, j = lax.div(k, 4), lax.rem(k, 4)
            own = self.hidden[:, span(k * BLK, BLK)]
            both = dot16(own, self.high[...], 0, 0) + dot16(own, self.low[...], 0, 0)
            self.strip[...] = both.reshape(NZ, NC, 8, 1024)
            self.away[i, j] = self.strip[:, 1 - c]
            keep = self.strip[:, c]
            self.acc_a[i, j] = keep[:, :, :512]
            self.acc_b[j, i] = keep[:, :, 512:]
            return carry

        lax.fori_loop(0, 16, one, 0)

    def core(self):
        x, y, z, c = self.here
        return [remote(self.away, self.got_c, self.sems, 0, device(x, y, z, 1 - c))]

    def core_start(self):
        start(self.core())

    def core_end(self):
        wait(self.core())

        def add(k, carry):
            i, j = lax.div(k, 4), lax.rem(k, 4)
            self.acc_a[i, j] = self.acc_a[i, j] + self.got_c[i, j, :, :, :512]
            self.acc_b[j, i] = self.acc_b[j, i] + self.got_c[i, j, :, :, 512:]
            return carry

        lax.fori_loop(0, 16, add, 0)

    def first(self):
        x, y, z, c = self.here
        copies = []
        for k in range(3):
            xk, yk = lax.rem(x + k + 1, NX), lax.rem(y + k + 1, NY)
            copies.append(remote(self.acc_a.at[xk], self.got_1.at[0, k], self.sems, 4 + k, device(xk, y, z, c)))
            copies.append(remote(self.acc_b.at[yk], self.got_1.at[1, k], self.sems, 7 + k, device(x, yk, z, c)))
        return copies

    def first_start(self):
        start(self.first())

    def first_end(self):
        x, y, z, c = self.here
        wait(self.first())
        got = self.got_1

        def add(j, carry):
            self.acc_1[0, j] = self.acc_a[x, j] + got[0, 0, j] + got[0, 1, j] + got[0, 2, j]
            self.acc_1[1, j] = self.acc_b[y, j] + got[1, 0, j] + got[1, 1, j] + got[1, 2, j]
            return carry

        lax.fori_loop(0, 4, add, 0)

    def second(self):
        x, y, z, c = self.here
        copies = []
        for k in range(3):
            xk, yk = lax.rem(x + k + 1, NX), lax.rem(y + k + 1, NY)
            copies.append(remote(self.acc_1.at[0, yk], self.got_2.at[0, k], self.sems, 10 + k, device(x, yk, z, c)))
            copies.append(remote(self.acc_1.at[1, xk], self.got_2.at[1, k], self.sems, 13 + k, device(xk, y, z, c)))
        return copies

    def second_start(self):
        start(self.second())

    def second_end(self):
        x, y, z, c = self.here
        wait(self.second())
        got = self.got_2
        self.acc_2[:, 0] = self.acc_1[0, y] + got[0, 0] + got[0, 1] + got[0, 2]
        self.acc_2[:, 1] = self.acc_1[1, x] + got[1, 0] + got[1, 1] + got[1, 2]

    def third(self):
        x, y, z, c = self.here
        copies = []
        for k in range(7):
            zk = lax.rem(z + k + 1, NZ)
            copies.append(remote(self.acc_2.at[zk], self.got_z.at[k], self.sems, 16 + k, device(x, y, zk, c)))
        return copies

    def third_start(self):
        start(self.third())

    def third_end(self, out_ref, row):
        wait(self.third())
        own = self.acc_2[self.here[2]]
        for k in range(7):
            own = own + self.got_z[k]
        out_ref[row : row + 8, :512] = own[0]
        out_ref[row : row + 8, 512:] = own[1]


def split(rows, high, low):
    high[...] = rows.astype(bf16)
    low[...] = (rows - high[...].astype(f32)).astype(bf16)


def kernel(count, hidden, weight, partner, whitened, grad_weight, grad_hidden,
           tile, tile_got, tile_sems,
           cent, packed, summed, acc, got_c, got_1, acc_1, got_2, acc_2, got_z, full_z, sems_1, sems_2,
           inv, inv_block, inv_row, white, grad, mirror, total, grad_z, grad_mean, late, high, low,
           strip, away, w_got_c, acc_a, acc_b, w_got_1, w_acc_1, w_got_2, w_acc_2, w_got_z, w_sems_1, w_sems_2):
    here = place()
    x, y, z, c = here
    N = 256
    barrier = pltpu.get_barrier_semaphore()
    for k in range(1, NZ * NC):
        own = lax.rem(z * NC + c + k, NZ * NC)
        pl.semaphore_signal(barrier, inc=1, device_id=device(x, y, lax.div(own, NC), lax.rem(own, NC)), device_id_type=MESH)
    for k in range(1, NX * NY):
        own = lax.rem(x * NY + y + k, NX * NY)
        pl.semaphore_signal(barrier, inc=1, device_id=device(lax.div(own, NY), lax.rem(own, NY), z, c), device_id_type=MESH)
    for part in range(4):
        cols = slice(part * 256, part * 256 + 256)
        strip_e = dot16(hidden[...], weight[:, cols])
        cent[:N, cols] = strip_e
        sums = jnp.sum(strip_e, axis=0, keepdims=True)
        tile[0, 2 * part : 2 * part + 1, :] = sums[:, :BLK]
        tile[0, 2 * part + 1 : 2 * part + 2, :] = sums[:, BLK:]
    sums = dot16(jnp.ones((8, N), bf16), hidden[...])
    for i in range(16):
        tile[0, 8 + i : 9 + i, :] = sums[0:1, i * BLK : (i + 1) * BLK]
    pl.semaphore_wait(barrier, NZ * NC + NX * NY - 2)
    tile_sum(here, tile, tile_got, tile_sems)
    for i in range(8):
        cols = slice(i * BLK, (i + 1) * BLK)
        cent[:N, cols] = cent[:N, cols] - tile[2, i : i + 1, :] * (1.0 / count)
    store_lower(packed, cent[:N, :], cent[:N, :])
    split(cent[:N, :], high, low)
    reduce_buffers = (acc, got_c, got_1, acc_1, got_2, acc_2, got_z, full_z)
    row_buffers = (high, low, strip, away, w_got_c, acc_a, acc_b, w_got_1, w_acc_1, w_got_2, w_acc_2, w_got_z)
    by_cent = RowScatter(here, hidden, *row_buffers, w_sems_1)
    by_grad = RowScatter(here, hidden, *row_buffers, w_sems_2)

    def cent_strips():
        by_cent.strips()
        by_cent.core_start()

    all_sum(here, packed, summed, *reduce_buffers, sems_1, {"first": cent_strips, "core back": by_cent.core_end}, {})
    by_cent.first_start()

    def to_second():
        by_cent.first_end()
        by_cent.second_start()

    def to_third():
        by_cent.second_end()
        by_cent.third_start()

    inverse_factor(1.0 / (count - 1), summed, inv, inv_block, inv_row, {4: to_second, 6: to_third})
    by_cent.third_end(cent, N)
    for part in range(4):
        stop = part * 256 + 256
        white[:, stop - 256 : stop] = dots(cent[:, :stop], inv[stop - 256 : stop, :stop], 1, 1)
    wh = white[:N, :]
    whitened[...] = wh.astype(bf16)
    row_norm = jnp.sqrt(jnp.sum(wh * wh, axis=1, keepdims=True) + epsilon)
    unit = wh / row_norm
    pick = (lax.broadcasted_iota(jnp.int32, (N, N), 0) == partner[...]).astype(f32)
    pick = (pick + pick.T).astype(bf16)
    near = jnp.zeros_like(unit)
    rest = unit
    for _ in range(3):
        term = rest.astype(bf16)
        near = near + dot16(pick, term)
        rest = rest - term.astype(f32)
    grad_unit = 2.0 * (2.0 * unit - near)
    inner_prod = jnp.sum(wh * grad_unit, axis=1, keepdims=True)
    gr = grad_unit / row_norm - wh * (inner_prod / (row_norm * row_norm * row_norm))
    grad[...] = gr
    split(gr, high, low)
    store_lower(packed, grad[...], white[:N, :])
    sums = jnp.sum(gr, axis=0, keepdims=True)
    sub = lax.broadcasted_iota(jnp.int32, (8, BLK), 0)
    lane = lax.broadcasted_iota(jnp.int32, (8, BLK), 1)
    for i in range(8):
        at = 16 * (i * (i + 1) // 2 + i)
        own = jnp.broadcast_to(sums[:, i * BLK : (i + 1) * BLK], (8, BLK))
        swapped = pltpu.roll(own, 64, 1)
        packed[at] = jnp.where(
            (lane >= 64) & (sub == 0), swapped, jnp.where((lane >= 64) & (sub == 1), own, packed[at])
        )
    all_sum(
        here, packed, summed, *reduce_buffers, sems_2,
        {"core": by_grad.strips, "first": by_grad.core_end},
        {"core": by_grad.core_start, "first": by_grad.first_start},
    )
    lane1 = lax.broadcasted_iota(jnp.int32, (1, BLK), 1)
    r = lax.broadcasted_iota(jnp.int32, (BLK, BLK), 0)
    l = lax.broadcasted_iota(jnp.int32, (BLK, BLK), 1)
    scale = 1.0 / (count - 1)
    for i in range(8):
        for j in range(i + 1):
            block = get_block(summed, i, j)
            turned = block.T
            rows, cols = slice(i * BLK, (i + 1) * BLK), slice(j * BLK, (j + 1) * BLK)
            if i == j:
                mirror[rows, cols] = jnp.where(r >= l, block, turned) * scale
                sums = jnp.where(lane1 < 64, pltpu.roll(block[0:1, :], 64, 1), block[1:2, :]) * (1.0 / count)
                grad_mean[:, cols] = jnp.broadcast_to(sums, (8, BLK))
                total[:N, cols] = grad[:, cols] - sums
            else:
                mirror[rows, cols] = block * scale
                mirror[cols, rows] = turned * scale
    total[N:, :] = jnp.zeros((8, 1024), f32)
    for part in range(4):
        cols = slice(part * 256, part * 256 + 256)
        total[:, cols] = total[:, cols] - dots(white[...], mirror[:, cols])
    for part in range(4):
        start_at = part * 256
        cols = slice(start_at, start_at + 256)
        both = dots(total[:, start_at:], inv[start_at:, cols])
        grad_z[:, cols] = both[:N].astype(bf16)
        late[:, cols] = both[N:]

    def hidden_part(k, carry):
        own = span(k * 256, 256)
        grad_hidden[:, own] = dot16(grad_z[...], weight[own, :], 1, 1).astype(bf16)
        return carry

    by_grad.first_end()
    by_grad.second_start()
    lax.fori_loop(0, 8, hidden_part, 0)
    by_grad.second_end()
    by_grad.third_start()
    units = jnp.broadcast_to(tile[2, pl.ds(8 + x * NY + y, 1), :], (8, BLK))
    mine = jnp.sum(jnp.where(lane == (z * NC + c) * 8 + sub, units, 0.0), axis=1, keepdims=True)
    by_grad.third_end(total, N)
    rows = total[N:, :] - mine * grad_mean[...]
    grad_weight[...] = late[...] + dots(rows, inv[...])


def body(hidden, weight, partners):
    count = hidden.shape[0] * lax.axis_size("group") * lax.axis_size("dp")
    vmem = pl.BlockSpec(memory_space=pltpu.VMEM)
    V, sem = pltpu.VMEM, pltpu.SemaphoreType.DMA
    return pl.pallas_call(
        functools.partial(kernel, count),
        out_shape=(
            jax.ShapeDtypeStruct((256, 1024), bf16),
            jax.ShapeDtypeStruct((8, 1024), f32),
            jax.ShapeDtypeStruct((256, 2048), bf16),
        ),
        in_specs=[vmem] * 3,
        out_specs=(vmem,) * 3,
        scratch_shapes=[
            V((3, 24, 128), f32), V((2, 15, 24, 128), f32), sem((2, 30)),
            V((264, 1024), f32), V((576, 8, 128), f32), V((576, 8, 128), f32),
            V((288, 8, 128), f32), V((288, 8, 128), f32), V((2, 3, 36, 8, 128), f32), V((2, 36, 8, 128), f32),
            V((2, 3, T, 8, 128), f32), V((24, 8, 128), f32), V((7, 3, 8, 128), f32), V((24, 8, 128), f32),
            sem((2, 40)), sem((2, 40)),
            V((1024, 1024), f32), V((BLK, BLK), f32), V((BLK, 1024), f32), V((264, 1024), f32),
            V((256, 1024), f32), V((1024, 1024), f32), V((264, 1024), f32), V((256, 1024), bf16),
            V((8, 1024), f32), V((8, 1024), f32), V((256, 1024), bf16), V((256, 1024), bf16),
            V((8, 2, 8, 1024), f32), V((4, 4, 8, 8, 1024), f32), V((4, 4, 8, 8, 1024), f32),
            V((4, 4, 8, 8, 512), f32), V((4, 4, 8, 8, 512), f32), V((2, 3, 4, 8, 8, 512), f32),
            V((2, 4, 8, 8, 512), f32), V((2, 3, 8, 8, 512), f32), V((8, 2, 8, 512), f32), V((7, 2, 8, 512), f32),
            sem((2, 23)), sem((2, 23)),
        ],
        compiler_params=pltpu.CompilerParams(collective_id=0, has_side_effects=True, vmem_limit_bytes=60 * MB),
        name="whitening_step",
    )(hidden, weight, partners)


def solution(mesh):
    return jax.shard_map(
        body,
        mesh=mesh,
        in_specs=(P(("group", "dp"), None), P(), P(("group", "dp"), None)),
        out_specs=(P(("group", "dp"), None), P(("group", "dp"), None), P(("group", "dp"), None)),
        check_vma=False,
    )
```

```python
import functools

import jax
import jax.numpy as jnp
from jax import lax
from jax.experimental import pallas as pl
from jax.experimental.pallas import tpu as pltpu
from jax.sharding import PartitionSpec as P

epsilon = 1e-06
highest = lax.Precision.HIGHEST
MESH = pl.DeviceIdType.MESH
NX, NY, NZ, NC = 4, 4, 8, 2
BLK = 128
MB = 1 << 20
f32, bf16 = jnp.float32, jnp.bfloat16


def place():
    dp = lax.axis_index("dp")
    x = lax.axis_index("group")
    return x, lax.div(dp, NZ * NC), lax.rem(lax.div(dp, NC), NZ), lax.rem(dp, NC)


def device(x, y, z, c):
    return (x, (y * NZ + z) * NC + c)


def remote(src, dst, sems, slot, peer):
    return pltpu.make_async_remote_copy(
        src_ref=src,
        dst_ref=dst,
        send_sem=sems.at[0, slot],
        recv_sem=sems.at[1, slot],
        device_id=peer,
        device_id_type=MESH,
    )


def start(copies):
    for copy in copies:
        copy.start()


def wait(copies):
    for copy in copies:
        copy.wait()


def send(src, dst, sems, slot, peer):
    copy = remote(src, dst, sems, slot, peer)
    copy.start()
    return copy


def nothing():
    pass


def dots(a, b, ca=1, cb=0):
    return lax.dot_general(a, b, (((ca,), (cb,)), ((), ())), precision=highest, preferred_element_type=f32)


def dot16(a, b, ca=1, cb=0):
    return lax.dot_general(a, b, (((ca,), (cb,)), ((), ())), preferred_element_type=f32)


def span(start, size):
    return pl.ds(pl.multiple_of(start, size), size)


def inverse_factor_block(pan):
    sub = lax.broadcasted_iota(jnp.int32, (8, BLK), 0)
    lane = lax.broadcasted_iota(jnp.int32, (8, BLK), 1)

    def over_sublanes(tile, k):
        return jnp.broadcast_to(tile[k : k + 1, :], (8, BLK))

    def over_lanes(tile, k):
        return jnp.broadcast_to(tile[:, k : k + 1], (8, BLK))

    pan = list(pan)
    for p in range(16):
        base = 8 * p
        inside = (lane >= base) & (lane < base + 8)
        own = pan[p]
        cols = [over_lanes(own, base + k) for k in range(8)]
        low = {(i, k): over_sublanes(cols[k], i) for k in range(8) for i in range(k, 8)}
        own = jnp.where(inside, jnp.where(lane - base == sub, 1.0, 0.0), own)
        rows = [over_sublanes(own, k) for k in range(8)]
        ahead = p + 1 < 16
        if ahead:
            left = [over_lanes(pan[p + 1], base + k) for k in range(8)]
            after = jnp.where(inside, 0.0, pan[p + 1])
        scale = []
        for k in range(8):
            rs = lax.rsqrt(low[k, k])
            scale.append(rs)
            rows[k] = rows[k] * rs
            for i in range(k + 1, 8):
                low[i, k] = low[i, k] * rs
            if ahead:
                left[k] = left[k] * rs
                after = after - left[k] * rows[k]
            for i in range(k + 1, 8):
                for m in range(k + 1, i + 1):
                    low[i, m] = low[i, m] - low[i, k] * low[m, k]
                rows[i] = rows[i] - low[i, k] * rows[k]
                if ahead:
                    left[i] = left[i] - left[k] * low[i, k]
        done = rows[0]
        for k in range(1, 8):
            done = jnp.where(sub == k, rows[k], done)
        pan[p] = done
        if ahead:
            pan[p + 1] = after
        if p + 2 < 16:
            back = [None] * 8
            for k in range(7, -1, -1):
                t = rows[k]
                for m in range(k + 1, 8):
                    t = t - low[m, k] * back[m]
                back[k] = t * scale[k]
            for q in range(p + 2, 16):
                t = jnp.where(inside, 0.0, pan[q])
                for k in range(8):
                    t = t - over_lanes(pan[q], base + k) * back[k]
                pan[q] = t
    return [jnp.where(lane <= sub + 8 * p, pan[p], 0.0) for p in range(16)]


def inverse_factor(scale, in_ref, out_ref, inv_ref, row_ref, beside):
    for i in range(8):
        for j in range(i + 1):
            block = get_block(in_ref, i, j) * scale
            rows, cols = slice(i * BLK, (i + 1) * BLK), slice(j * BLK, (j + 1) * BLK)
            turned = block.T
            if i == j:
                r = lax.broadcasted_iota(jnp.int32, (BLK, BLK), 0)
                l = lax.broadcasted_iota(jnp.int32, (BLK, BLK), 1)
                out_ref[rows, cols] = jnp.where(r >= l, block, turned)
            else:
                out_ref[rows, cols] = block
                out_ref[cols, rows] = turned
    lane = lax.broadcasted_iota(jnp.int32, (BLK, 1024), 1)

    def step(i, carry):
        for at, work in beside.items():
            pl.when(i == at)(work)
        own = span(i * BLK, BLK)
        pans = [out_ref[span(i * BLK + 8 * p, 8), own] for p in range(16)]
        for p, tile in enumerate(inverse_factor_block(pans)):
            inv_ref[8 * p : 8 * p + 8, :] = tile
        inv = inv_ref[...]
        row_ref[...] = dots(inv, out_ref[own, :])
        row_ref[:, own] = inv
        out_ref[own, :] = jnp.where(lane < (i + 1) * BLK, row_ref[...], 0.0)

        def lower(j, inner):
            its = span(j * BLK, BLK)
            left = dots(out_ref[its, own], inv_ref[...], 1, 1)
            out_ref[its, own] = jnp.zeros((BLK, BLK), f32)
            out_ref[its, :] = out_ref[its, :] - dots(left, row_ref[...])
            return inner

        lax.fori_loop(i + 1, 8, lower, 0)
        return carry

    lax.fori_loop(0, 8, step, 0)


def get_block(ref, i, j):
    at = i * (i + 1) // 2 + j
    return ref[16 * at : 16 * at + 16].reshape(BLK, BLK)


def store_lower(out_ref, a, b):
    for half in range(4):
        strip = dots(a[:, half * 256 : half * 256 + 256], b[:, : half * 256 + 256], 0, 0)
        for i in (2 * half, 2 * half + 1):
            for j in range(i + 1):
                r = (i - 2 * half) * BLK
                at = i * (i + 1) // 2 + j
                out_ref[16 * at : 16 * at + 16] = strip[r : r + BLK, j * BLK : (j + 1) * BLK].reshape(16, 8, BLK)


def tile_sum(here, tile, got, sems):
    x, y, z, c = here
    copies = []
    for k in range(1, NZ * NC):
        own = lax.rem(z * NC + c + k, NZ * NC)
        peer = device(x, y, lax.div(own, NC), lax.rem(own, NC))
        copies.append(send(tile.at[0], got.at[0, k - 1], sems, k - 1, peer))
    wait(copies)
    total = tile[0]
    for k in range(15):
        total = total + got[0, k]
    tile[1] = total
    copies = []
    for k in range(1, NX * NY):
        own = lax.rem(x * NY + y + k, NX * NY)
        peer = device(lax.div(own, NY), lax.rem(own, NY), z, c)
        copies.append(send(tile.at[1], got.at[1, k - 1], sems, 14 + k, peer))
    wait(copies)
    for k in range(15):
        total = total + got[1, k]
    tile[2] = total


T = 9


def all_sum(here, in_ref, out_ref, acc, got_c, got_1, acc_1, got_2, acc_2, got_z, full_z, sems, during):
    x, y, z, c = here
    across = device(x, y, z, 1 - c)
    xs = [device(lax.rem(x + k, NX), y, z, c) for k in range(1, NX)]
    ys = [device(x, lax.rem(y + k, NY), z, c) for k in range(1, NY)]
    zs = [device(x, y, lax.rem(z + k, NZ), c) for k in range(1, NZ)]
    x_at = [lax.rem(x + k, NX) for k in range(1, NX)]
    y_at = [lax.rem(y + k, NY) for k in range(1, NY)]
    z_at = [lax.rem(z + k, NZ) for k in range(1, NZ)]
    copy = send(in_ref.at[pl.ds((1 - c) * 288, 288)], got_c, sems, 0, across)
    during.get("core", nothing)()
    copy.wait()
    acc[...] = in_ref[pl.ds(c * 288, 288)] + got_c[...]
    copies = []
    for k in range(3):
        copies.append(send(acc.at[pl.ds(x_at[k] * 36, 36)], got_1.at[0, k], sems, 1 + k, xs[k]))
        copies.append(send(acc.at[pl.ds(144 + y_at[k] * 36, 36)], got_1.at[1, k], sems, 4 + k, ys[k]))
    during.get("first", nothing)()
    wait(copies)
    acc_1[0] = acc[pl.ds(x * 36, 36)] + got_1[0, 0] + got_1[0, 1] + got_1[0, 2]
    acc_1[1] = acc[pl.ds(144 + y * 36, 36)] + got_1[1, 0] + got_1[1, 1] + got_1[1, 2]
    copies = []
    for k in range(3):
        copies.append(send(acc_1.at[0, pl.ds(y_at[k] * T, T)], got_2.at[0, k], sems, 7 + k, ys[k]))
        copies.append(send(acc_1.at[1, pl.ds(x_at[k] * T, T)], got_2.at[1, k], sems, 10 + k, xs[k]))
    during.get("second", nothing)()
    wait(copies)
    acc_2[0:T] = acc_1[0, pl.ds(y * T, T)] + got_2[0, 0] + got_2[0, 1] + got_2[0, 2]
    acc_2[T : 2 * T] = acc_1[1, pl.ds(x * T, T)] + got_2[1, 0] + got_2[1, 1] + got_2[1, 2]
    acc_2[2 * T : 24] = jnp.zeros((24 - 2 * T, 8, 128), f32)
    copies = [send(acc_2.at[pl.ds(3 * z_at[k], 3)], got_z.at[k], sems, 13 + k, zs[k]) for k in range(7)]
    during.get("third", nothing)()
    wait(copies)
    own = acc_2[pl.ds(3 * z, 3)]
    for k in range(7):
        own = own + got_z[k]
    mine = full_z.at[pl.ds(3 * z, 3)]
    mine[...] = own
    copies = [send(mine, mine, sems, 20 + k, zs[k]) for k in range(7)]
    during.get("third back", nothing)()
    wait(copies)
    base = c * 288
    first, second = out_ref.at[pl.ds(base + (x * 4 + y) * T, T)], out_ref.at[pl.ds(base + 144 + (y * 4 + x) * T, T)]
    first[...] = full_z[0:T]
    second[...] = full_z[T : 2 * T]
    copies = []
    for k in range(3):
        copies.append(send(first, first, sems, 27 + k, ys[k]))
        copies.append(send(second, second, sems, 30 + k, xs[k]))
    wait(copies)
    first, second = out_ref.at[pl.ds(base + x * 36, 36)], out_ref.at[pl.ds(base + 144 + y * 36, 36)]
    copies = []
    for k in range(3):
        copies.append(send(first, first, sems, 33 + k, xs[k]))
        copies.append(send(second, second, sems, 36 + k, ys[k]))
    wait(copies)
    first = out_ref.at[pl.ds(base, 288)]
    copy = send(first, first, sems, 39, across)
    during.get("core back", nothing)()
    copy.wait()


class RowScatter:
    def __init__(self, here, hidden, high, low, strip, away, got_c, acc_a, acc_b, got_1, acc_1, got_2, acc_2, got_z, sems):
        self.here, self.hidden, self.high, self.low, self.strip, self.away = here, hidden, high, low, strip, away
        self.got_c, self.acc_a, self.acc_b, self.got_1, self.acc_1 = got_c, acc_a, acc_b, got_1, acc_1
        self.got_2, self.acc_2, self.got_z, self.sems = got_2, acc_2, got_z, sems

    def strips(self):
        c = self.here[3]

        def one(k, carry):
            i, j = lax.div(k, 4), lax.rem(k, 4)
            own = self.hidden[span(k * BLK, BLK), :]
            both = dot16(own, self.high[...]) + dot16(own, self.low[...])
            self.strip[...] = both.reshape(NZ, NC, 8, 1024)
            self.away[i, j] = self.strip[:, 1 - c]
            keep = self.strip[:, c]
            self.acc_a[i, j] = keep[:, :, :512]
            self.acc_b[j, i] = keep[:, :, 512:]
            return carry

        lax.fori_loop(0, 16, one, 0)

    def core(self):
        x, y, z, c = self.here
        return [remote(self.away, self.got_c, self.sems, 0, device(x, y, z, 1 - c))]

    def core_start(self):
        start(self.core())

    def core_end(self):
        wait(self.core())

        def add(k, carry):
            i, j = lax.div(k, 4), lax.rem(k, 4)
            self.acc_a[i, j] = self.acc_a[i, j] + self.got_c[i, j, :, :, :512]
            self.acc_b[j, i] = self.acc_b[j, i] + self.got_c[i, j, :, :, 512:]
            return carry

        lax.fori_loop(0, 16, add, 0)

    def ring(self, slots):
        x, y, z, c = self.here
        copies = []
        for axis, at, size, acc in ((0, x, NX, self.acc_a), (1, y, NY, self.acc_b)):
            up, far, down = lax.rem(at + 1, size), lax.rem(at + 2, size), lax.rem(at + 3, size)
            plus = device(up, y, z, c) if axis == 0 else device(x, up, z, c)
            minus = device(down, y, z, c) if axis == 0 else device(x, down, z, c)
            routes = (
                (acc.at[far, 0:2], plus),
                (acc.at[far, 2:4], minus),
                (acc.at[down, 0:2], minus),
                (acc.at[up, 2:4], plus),
                (acc.at[up, 0:2], plus),
                (acc.at[down, 2:4], minus),
            )
            for slot in slots:
                src, peer = routes[slot]
                copies.append(remote(src, self.got_1.at[axis, slot], self.sems, 1 + 6 * axis + slot, peer))
        return copies

    def far_start(self):
        start(self.ring((0, 1)))

    def near_start(self):
        start(self.ring((2, 3)))

    def pass_on(self):
        x, y, z, c = self.here
        wait(self.ring((0, 1)))
        for axis, at, size, acc in ((0, x, NX, self.acc_a), (1, y, NY, self.acc_b)):
            up, down = lax.rem(at + 1, size), lax.rem(at + 3, size)

            def add(j, carry):
                acc[up, j] = acc[up, j] + self.got_1[axis, 0, j]
                acc[down, 2 + j] = acc[down, 2 + j] + self.got_1[axis, 1, j]
                return carry

            lax.fori_loop(0, 2, add, 0)
        start(self.ring((4, 5)))

    def first_end(self):
        x, y, z, c = self.here
        wait(self.ring((2, 3)))
        wait(self.ring((4, 5)))
        for axis, at, acc in ((0, x, self.acc_a), (1, y, self.acc_b)):
            got = self.got_1

            def add(j, carry):
                self.acc_1[axis, j] = acc[at, j] + got[axis, 2, j] + got[axis, 4, j]
                self.acc_1[axis, 2 + j] = acc[at, 2 + j] + got[axis, 3, j] + got[axis, 5, j]
                return carry

            lax.fori_loop(0, 2, add, 0)

    def second(self):
        x, y, z, c = self.here
        copies = []
        for k in range(3):
            xk, yk = lax.rem(x + k + 1, NX), lax.rem(y + k + 1, NY)
            copies.append(remote(self.acc_1.at[0, yk], self.got_2.at[0, k], self.sems, 13 + k, device(x, yk, z, c)))
            copies.append(remote(self.acc_1.at[1, xk], self.got_2.at[1, k], self.sems, 16 + k, device(xk, y, z, c)))
        return copies

    def second_start(self):
        start(self.second())

    def second_end(self):
        x, y, z, c = self.here
        wait(self.second())
        got = self.got_2
        self.acc_2[:, 0] = self.acc_1[0, y] + got[0, 0] + got[0, 1] + got[0, 2]
        self.acc_2[:, 1] = self.acc_1[1, x] + got[1, 0] + got[1, 1] + got[1, 2]

    def third(self):
        x, y, z, c = self.here
        copies = []
        for k in range(7):
            zk = lax.rem(z + k + 1, NZ)
            copies.append(remote(self.acc_2.at[zk], self.got_z.at[k], self.sems, 19 + k, device(x, y, zk, c)))
        return copies

    def third_start(self):
        start(self.third())

    def third_end(self, out_ref, row):
        wait(self.third())
        own = self.acc_2[self.here[2]]
        for k in range(7):
            own = own + self.got_z[k]
        out_ref[row : row + 8, :512] = own[0]
        out_ref[row : row + 8, 512:] = own[1]


def split(rows, high, low):
    high[...] = rows.astype(bf16)
    low[...] = (rows - high[...].astype(f32)).astype(bf16)


def kernel(count, hidden, weight, partner, whitened, grad_weight, grad_hidden,
           tile, tile_got, tile_sems,
           cent, packed, summed, acc, got_c, got_1, acc_1, got_2, acc_2, got_z, full_z, sems_1, sems_2,
           inv, inv_block, inv_row, white, grad, mirror, total, grad_z, grad_mean, late, hidden_t, high, low,
           strip, away, w_got_c, acc_a, acc_b, w_got_1, w_acc_1, w_got_2, w_acc_2, w_got_z, w_sems_1, w_sems_2):
    here = place()
    x, y, z, c = here
    N = 256
    barrier = pltpu.get_barrier_semaphore()
    for k in range(1, NZ * NC):
        own = lax.rem(z * NC + c + k, NZ * NC)
        pl.semaphore_signal(barrier, inc=1, device_id=device(x, y, lax.div(own, NC), lax.rem(own, NC)), device_id_type=MESH)
    for k in range(1, NX * NY):
        own = lax.rem(x * NY + y + k, NX * NY)
        pl.semaphore_signal(barrier, inc=1, device_id=device(lax.div(own, NY), lax.rem(own, NY), z, c), device_id_type=MESH)
    for part in range(4):
        cols = slice(part * 256, part * 256 + 256)
        strip_e = dot16(hidden[...], weight[:, cols])
        cent[:N, cols] = strip_e
        sums = jnp.sum(strip_e, axis=0, keepdims=True)
        tile[0, 2 * part : 2 * part + 1, :] = sums[:, :BLK]
        tile[0, 2 * part + 1 : 2 * part + 2, :] = sums[:, BLK:]
    sums = dot16(jnp.ones((8, N), bf16), hidden[...])
    for i in range(16):
        tile[0, 8 + i : 9 + i, :] = sums[0:1, i * BLK : (i + 1) * BLK]
    hidden_t[...] = hidden[...].T
    pl.semaphore_wait(barrier, NZ * NC + NX * NY - 2)
    tile_sum(here, tile, tile_got, tile_sems)
    for i in range(8):
        cols = slice(i * BLK, (i + 1) * BLK)
        cent[:N, cols] = cent[:N, cols] - tile[2, i : i + 1, :] * (1.0 / count)
    store_lower(packed, cent[:N, :], cent[:N, :])
    split(cent[:N, :], high, low)
    reduce_buffers = (acc, got_c, got_1, acc_1, got_2, acc_2, got_z, full_z)
    row_buffers = (high, low, strip, away, w_got_c, acc_a, acc_b, w_got_1, w_acc_1, w_got_2, w_acc_2, w_got_z)
    by_cent = RowScatter(here, hidden_t, *row_buffers, w_sems_1)
    by_grad = RowScatter(here, hidden_t, *row_buffers, w_sems_2)

    def cent_strips():
        by_cent.strips()
        by_cent.core_start()

    all_sum(here, packed, summed, *reduce_buffers, sems_1, {"first": cent_strips, "core back": by_cent.core_end})
    by_cent.far_start()
    by_cent.near_start()

    def to_second():
        by_cent.first_end()
        by_cent.second_start()

    def to_third():
        by_cent.second_end()
        by_cent.third_start()

    inverse_factor(1.0 / (count - 1), summed, inv, inv_block, inv_row, {2: by_cent.pass_on, 4: to_second, 6: to_third})
    by_cent.third_end(cent, N)
    for part in range(4):
        stop = part * 256 + 256
        white[:, stop - 256 : stop] = dots(cent[:, :stop], inv[stop - 256 : stop, :stop], 1, 1)
    wh = white[:N, :]
    whitened[...] = wh.astype(bf16)
    row_norm = jnp.sqrt(jnp.sum(wh * wh, axis=1, keepdims=True) + epsilon)
    unit = wh / row_norm
    pick = (lax.broadcasted_iota(jnp.int32, (N, N), 0) == partner[...]).astype(f32)
    pick = (pick + pick.T).astype(bf16)
    near = jnp.zeros_like(unit)
    rest = unit
    for _ in range(3):
        term = rest.astype(bf16)
        near = near + dot16(pick, term)
        rest = rest - term.astype(f32)
    grad_unit = 2.0 * (2.0 * unit - near)
    inner_prod = jnp.sum(wh * grad_unit, axis=1, keepdims=True)
    gr = grad_unit / row_norm - wh * (inner_prod / (row_norm * row_norm * row_norm))
    grad[...] = gr
    split(gr, high, low)
    store_lower(packed, grad[...], white[:N, :])
    sums = jnp.sum(gr, axis=0, keepdims=True)
    sub = lax.broadcasted_iota(jnp.int32, (8, BLK), 0)
    lane = lax.broadcasted_iota(jnp.int32, (8, BLK), 1)
    for i in range(8):
        at = 16 * (i * (i + 1) // 2 + i)
        own = jnp.broadcast_to(sums[:, i * BLK : (i + 1) * BLK], (8, BLK))
        swapped = pltpu.roll(own, 64, 1)
        packed[at] = jnp.where(
            (lane >= 64) & (sub == 0), swapped, jnp.where((lane >= 64) & (sub == 1), own, packed[at])
        )
    all_sum(
        here, packed, summed, *reduce_buffers, sems_2,
        {
            "core": by_grad.strips,
            "first": by_grad.core_start,
            "second": by_grad.core_end,
            "third": by_grad.far_start,
            "third back": by_grad.near_start,
            "core back": by_grad.pass_on,
        },
    )
    by_grad.first_end()
    by_grad.second_start()
    lane1 = lax.broadcasted_iota(jnp.int32, (1, BLK), 1)
    r = lax.broadcasted_iota(jnp.int32, (BLK, BLK), 0)
    l = lax.broadcasted_iota(jnp.int32, (BLK, BLK), 1)
    scale = 1.0 / (count - 1)
    for i in range(8):
        for j in range(i + 1):
            block = get_block(summed, i, j)
            turned = block.T
            rows, cols = slice(i * BLK, (i + 1) * BLK), slice(j * BLK, (j + 1) * BLK)
            if i == j:
                mirror[rows, cols] = jnp.where(r >= l, block, turned) * scale
                sums = jnp.where(lane1 < 64, pltpu.roll(block[0:1, :], 64, 1), block[1:2, :]) * (1.0 / count)
                grad_mean[:, cols] = jnp.broadcast_to(sums, (8, BLK))
                total[:N, cols] = grad[:, cols] - sums
            else:
                mirror[rows, cols] = block * scale
                mirror[cols, rows] = turned * scale
    total[N:, :] = jnp.zeros((8, 1024), f32)
    for part in range(4):
        cols = slice(part * 256, part * 256 + 256)
        total[:, cols] = total[:, cols] - dots(white[...], mirror[:, cols])
    for part in range(4):
        start_at = part * 256
        cols = slice(start_at, start_at + 256)
        both = dots(total[:, start_at:], inv[start_at:, cols])
        grad_z[:, cols] = both[:N].astype(bf16)
        late[:, cols] = both[N:]

    def hidden_part(k, carry):
        own = span(k * 256, 256)
        grad_hidden[:, own] = dot16(grad_z[...], weight[own, :], 1, 1).astype(bf16)
        return carry

    by_grad.second_end()
    by_grad.third_start()
    lax.fori_loop(0, 8, hidden_part, 0)
    units = jnp.broadcast_to(tile[2, pl.ds(8 + x * NY + y, 1), :], (8, BLK))
    mine = jnp.sum(jnp.where(lane == (z * NC + c) * 8 + sub, units, 0.0), axis=1, keepdims=True)
    by_grad.third_end(total, N)
    rows = total[N:, :] - mine * grad_mean[...]
    grad_weight[...] = late[...] + dots(rows, inv[...])


def body(hidden, weight, partners):
    count = hidden.shape[0] * lax.axis_size("group") * lax.axis_size("dp")
    vmem = pl.BlockSpec(memory_space=pltpu.VMEM)
    V, sem = pltpu.VMEM, pltpu.SemaphoreType.DMA
    return pl.pallas_call(
        functools.partial(kernel, count),
        out_shape=(
            jax.ShapeDtypeStruct((256, 1024), bf16),
            jax.ShapeDtypeStruct((8, 1024), f32),
            jax.ShapeDtypeStruct((256, 2048), bf16),
        ),
        in_specs=[vmem] * 3,
        out_specs=(vmem,) * 3,
        scratch_shapes=[
            V((3, 24, 128), f32), V((2, 15, 24, 128), f32), sem((2, 30)),
            V((264, 1024), f32), V((576, 8, 128), f32), V((576, 8, 128), f32),
            V((288, 8, 128), f32), V((288, 8, 128), f32), V((2, 3, 36, 8, 128), f32), V((2, 36, 8, 128), f32),
            V((2, 3, T, 8, 128), f32), V((24, 8, 128), f32), V((7, 3, 8, 128), f32), V((24, 8, 128), f32),
            sem((2, 40)), sem((2, 40)),
            V((1024, 1024), f32), V((BLK, BLK), f32), V((BLK, 1024), f32), V((264, 1024), f32),
            V((256, 1024), f32), V((1024, 1024), f32), V((264, 1024), f32), V((256, 1024), bf16),
            V((8, 1024), f32), V((8, 1024), f32), V((2048, 256), bf16), V((256, 1024), bf16), V((256, 1024), bf16),
            V((8, 2, 8, 1024), f32), V((4, 4, 8, 8, 1024), f32), V((4, 4, 8, 8, 1024), f32),
            V((4, 4, 8, 8, 512), f32), V((4, 4, 8, 8, 512), f32), V((2, 6, 2, 8, 8, 512), f32),
            V((2, 4, 8, 8, 512), f32), V((2, 3, 8, 8, 512), f32), V((8, 2, 8, 512), f32), V((7, 2, 8, 512), f32),
            sem((2, 26)), sem((2, 26)),
        ],
        compiler_params=pltpu.CompilerParams(collective_id=0, has_side_effects=True, vmem_limit_bytes=60 * MB),
        name="whitening_step",
    )(hidden, weight, partners)


def solution(mesh):
    return jax.shard_map(
        body,
        mesh=mesh,
        in_specs=(P(("group", "dp"), None), P(), P(("group", "dp"), None)),
        out_specs=(P(("group", "dp"), None), P(("group", "dp"), None), P(("group", "dp"), None)),
        check_vma=False,
    )
```

```python
import functools

import jax
import jax.numpy as jnp
from jax import lax
from jax.experimental import pallas as pl
from jax.experimental.pallas import tpu as pltpu
from jax.sharding import PartitionSpec as P

epsilon = 1e-06
highest = lax.Precision.HIGHEST
MESH = pl.DeviceIdType.MESH
NX, NY, NZ, NC = 4, 4, 8, 2
BLK = 128
MB = 1 << 20
f32, bf16 = jnp.float32, jnp.bfloat16


def place():
    dp = lax.axis_index("dp")
    x = lax.axis_index("group")
    return x, lax.div(dp, NZ * NC), lax.rem(lax.div(dp, NC), NZ), lax.rem(dp, NC)


def device(x, y, z, c):
    return (x, (y * NZ + z) * NC + c)


def remote(src, dst, sems, slot, peer):
    return pltpu.make_async_remote_copy(
        src_ref=src,
        dst_ref=dst,
        send_sem=sems.at[0, slot],
        recv_sem=sems.at[1, slot],
        device_id=peer,
        device_id_type=MESH,
    )


def start(copies):
    for copy in copies:
        copy.start()


def wait(copies):
    for copy in copies:
        copy.wait()


def send(src, dst, sems, slot, peer):
    copy = remote(src, dst, sems, slot, peer)
    copy.start()
    return copy


def nothing():
    pass


def dots(a, b, ca=1, cb=0):
    return lax.dot_general(a, b, (((ca,), (cb,)), ((), ())), precision=highest, preferred_element_type=f32)


def dot16(a, b, ca=1, cb=0):
    return lax.dot_general(a, b, (((ca,), (cb,)), ((), ())), preferred_element_type=f32)


def span(start, size):
    return pl.ds(pl.multiple_of(start, size), size)


def inverse_factor_block(pan):
    sub = lax.broadcasted_iota(jnp.int32, (8, BLK), 0)
    lane = lax.broadcasted_iota(jnp.int32, (8, BLK), 1)

    def over_sublanes(tile, k):
        return jnp.broadcast_to(tile[k : k + 1, :], (8, BLK))

    def over_lanes(tile, k):
        return jnp.broadcast_to(tile[:, k : k + 1], (8, BLK))

    pan = list(pan)
    for p in range(16):
        base = 8 * p
        inside = (lane >= base) & (lane < base + 8)
        own = pan[p]
        cols = [over_lanes(own, base + k) for k in range(8)]
        low = {(i, k): over_sublanes(cols[k], i) for k in range(8) for i in range(k, 8)}
        own = jnp.where(inside, jnp.where(lane - base == sub, 1.0, 0.0), own)
        rows = [over_sublanes(own, k) for k in range(8)]
        ahead = p + 1 < 16
        if ahead:
            left = [over_lanes(pan[p + 1], base + k) for k in range(8)]
            after = jnp.where(inside, 0.0, pan[p + 1])
        scale = []
        for k in range(8):
            rs = lax.rsqrt(low[k, k])
            scale.append(rs)
            rows[k] = rows[k] * rs
            for i in range(k + 1, 8):
                low[i, k] = low[i, k] * rs
            if ahead:
                left[k] = left[k] * rs
                after = after - left[k] * rows[k]
            for i in range(k + 1, 8):
                for m in range(k + 1, i + 1):
                    low[i, m] = low[i, m] - low[i, k] * low[m, k]
                rows[i] = rows[i] - low[i, k] * rows[k]
                if ahead:
                    left[i] = left[i] - left[k] * low[i, k]
        done = rows[0]
        for k in range(1, 8):
            done = jnp.where(sub == k, rows[k], done)
        pan[p] = done
        if ahead:
            pan[p + 1] = after
        if p + 2 < 16:
            back = [None] * 8
            for k in range(7, -1, -1):
                t = rows[k]
                for m in range(k + 1, 8):
                    t = t - low[m, k] * back[m]
                back[k] = t * scale[k]
            for q in range(p + 2, 16):
                t = jnp.where(inside, 0.0, pan[q])
                for k in range(8):
                    t = t - over_lanes(pan[q], base + k) * back[k]
                pan[q] = t
    return [jnp.where(lane <= sub + 8 * p, pan[p], 0.0) for p in range(16)]


def thirds(v):
    high = v.astype(bf16)
    rest = v - high.astype(f32)
    mid = rest.astype(bf16)
    return high, mid, (rest - mid.astype(f32)).astype(bf16)


def left_stack(v):
    h, m, l = thirds(v)
    return jnp.concatenate([h, h, m, h, l, m], axis=1)


def right_stack(v, axis):
    h, m, l = thirds(v)
    return jnp.concatenate([h, m, h, l, h, m], axis=axis)


def inverse_factor(scale, in_ref, out_ref, inv_ref, stack_ref, beside):
    for i in range(8):
        for j in range(i + 1):
            block = get_block(in_ref, i, j) * scale
            rows, cols = slice(i * BLK, (i + 1) * BLK), slice(j * BLK, (j + 1) * BLK)
            turned = block.T
            if i == j:
                r = lax.broadcasted_iota(jnp.int32, (BLK, BLK), 0)
                l = lax.broadcasted_iota(jnp.int32, (BLK, BLK), 1)
                out_ref[rows, cols] = jnp.where(r >= l, block, turned)
            else:
                out_ref[rows, cols] = block
                out_ref[cols, rows] = turned
    out_ref[1024:, :] = jnp.zeros((7 * BLK, 1024), f32)
    lane = lax.broadcasted_iota(jnp.int32, (BLK, 1024), 1)

    def factor(block):
        return inverse_factor_block([block[8 * p : 8 * p + 8, :] for p in range(16)])

    def keep(tiles):
        for p, tile in enumerate(tiles):
            inv_ref[8 * p : 8 * p + 8, :] = tile

    def scaled_row(i):
        own = span(i * BLK, BLK)
        inv = inv_ref[...]
        row = dot16(left_stack(inv), right_stack(out_ref[own, :], 0))
        inside = (lane >= i * BLK) & (lane < (i + 1) * BLK)
        row = jnp.where(inside, jnp.concatenate([inv] * 8, axis=1), row)
        out_ref[own, :] = jnp.where(lane < (i + 1) * BLK, row, 0.0)
        return row

    keep(factor(out_ref[0:BLK, 0:BLK]))

    def step(i, carry):
        for at, work in beside.items():
            pl.when(i == at)(work)
        own, nxt = span(i * BLK, BLK), span((i + 1) * BLK, BLK)
        below = pl.ds(pl.multiple_of((i + 1) * BLK, BLK), 7 * BLK)
        inv = inv_ref[...]
        left = dots(out_ref[nxt, own], inv, 1, 1)
        block = out_ref[nxt, nxt] - dots(left, left, 1, 1)
        tiles = factor(block)
        stack_ref[...] = right_stack(scaled_row(i), 0)
        left = dot16(left_stack(out_ref[below, own]), right_stack(inv, 1), 1, 1)
        out_ref[below, own] = jnp.zeros((7 * BLK, BLK), f32)
        left = left_stack(left)
        for part in range(4):
            cols = slice(part * 256, part * 256 + 256)
            out_ref[below, cols] = out_ref[below, cols] - dot16(left, stack_ref[:, cols])
        keep(tiles)
        return carry

    lax.fori_loop(0, 7, step, 0)
    scaled_row(7)


def get_block(ref, i, j):
    at = i * (i + 1) // 2 + j
    return ref[16 * at : 16 * at + 16].reshape(BLK, BLK)


def store_lower(out_ref, a, b):
    for half in range(4):
        strip = dots(a[:, half * 256 : half * 256 + 256], b[:, : half * 256 + 256], 0, 0)
        for i in (2 * half, 2 * half + 1):
            for j in range(i + 1):
                r = (i - 2 * half) * BLK
                at = i * (i + 1) // 2 + j
                out_ref[16 * at : 16 * at + 16] = strip[r : r + BLK, j * BLK : (j + 1) * BLK].reshape(16, 8, BLK)


def tile_sum(here, tile, got, sems):
    x, y, z, c = here
    copies = []
    for k in range(1, NZ * NC):
        own = lax.rem(z * NC + c + k, NZ * NC)
        peer = device(x, y, lax.div(own, NC), lax.rem(own, NC))
        copies.append(send(tile.at[0], got.at[0, k - 1], sems, k - 1, peer))
    wait(copies)
    total = tile[0]
    for k in range(15):
        total = total + got[0, k]
    tile[1] = total
    copies = []
    for k in range(1, NX * NY):
        own = lax.rem(x * NY + y + k, NX * NY)
        peer = device(lax.div(own, NY), lax.rem(own, NY), z, c)
        copies.append(send(tile.at[1], got.at[1, k - 1], sems, 14 + k, peer))
    wait(copies)
    for k in range(15):
        total = total + got[1, k]
    tile[2] = total


T = 9


def all_sum(here, in_ref, out_ref, acc, got_c, got_1, acc_1, got_2, acc_2, got_z, full_z, sems, during):
    x, y, z, c = here
    across = device(x, y, z, 1 - c)
    xs = [device(lax.rem(x + k, NX), y, z, c) for k in range(1, NX)]
    ys = [device(x, lax.rem(y + k, NY), z, c) for k in range(1, NY)]
    zs = [device(x, y, lax.rem(z + k, NZ), c) for k in range(1, NZ)]
    x_at = [lax.rem(x + k, NX) for k in range(1, NX)]
    y_at = [lax.rem(y + k, NY) for k in range(1, NY)]
    z_at = [lax.rem(z + k, NZ) for k in range(1, NZ)]
    copy = send(in_ref.at[pl.ds((1 - c) * 288, 288)], got_c, sems, 0, across)
    during.get("core", nothing)()
    copy.wait()
    acc[...] = in_ref[pl.ds(c * 288, 288)] + got_c[...]
    copies = []
    for k in range(3):
        copies.append(send(acc.at[pl.ds(x_at[k] * 36, 36)], got_1.at[0, k], sems, 1 + k, xs[k]))
        copies.append(send(acc.at[pl.ds(144 + y_at[k] * 36, 36)], got_1.at[1, k], sems, 4 + k, ys[k]))
    during.get("first", nothing)()
    wait(copies)
    acc_1[0] = acc[pl.ds(x * 36, 36)] + got_1[0, 0] + got_1[0, 1] + got_1[0, 2]
    acc_1[1] = acc[pl.ds(144 + y * 36, 36)] + got_1[1, 0] + got_1[1, 1] + got_1[1, 2]
    copies = []
    for k in range(3):
        copies.append(send(acc_1.at[0, pl.ds(y_at[k] * T, T)], got_2.at[0, k], sems, 7 + k, ys[k]))
        copies.append(send(acc_1.at[1, pl.ds(x_at[k] * T, T)], got_2.at[1, k], sems, 10 + k, xs[k]))
    during.get("second", nothing)()
    wait(copies)
    acc_2[0:T] = acc_1[0, pl.ds(y * T, T)] + got_2[0, 0] + got_2[0, 1] + got_2[0, 2]
    acc_2[T : 2 * T] = acc_1[1, pl.ds(x * T, T)] + got_2[1, 0] + got_2[1, 1] + got_2[1, 2]
    acc_2[2 * T : 24] = jnp.zeros((24 - 2 * T, 8, 128), f32)
    copies = [send(acc_2.at[pl.ds(3 * z_at[k], 3)], got_z.at[k], sems, 13 + k, zs[k]) for k in range(7)]
    during.get("third", nothing)()
    wait(copies)
    own = acc_2[pl.ds(3 * z, 3)]
    for k in range(7):
        own = own + got_z[k]
    mine = full_z.at[pl.ds(3 * z, 3)]
    mine[...] = own
    copies = [send(mine, mine, sems, 20 + k, zs[k]) for k in range(7)]
    during.get("third back", nothing)()
    wait(copies)
    base = c * 288
    first, second = out_ref.at[pl.ds(base + (x * 4 + y) * T, T)], out_ref.at[pl.ds(base + 144 + (y * 4 + x) * T, T)]
    first[...] = full_z[0:T]
    second[...] = full_z[T : 2 * T]
    copies = []
    for k in range(3):
        copies.append(send(first, first, sems, 27 + k, ys[k]))
        copies.append(send(second, second, sems, 30 + k, xs[k]))
    wait(copies)
    first, second = out_ref.at[pl.ds(base + x * 36, 36)], out_ref.at[pl.ds(base + 144 + y * 36, 36)]
    copies = []
    for k in range(3):
        copies.append(send(first, first, sems, 33 + k, xs[k]))
        copies.append(send(second, second, sems, 36 + k, ys[k]))
    wait(copies)
    first = out_ref.at[pl.ds(base, 288)]
    copy = send(first, first, sems, 39, across)
    during.get("core back", nothing)()
    copy.wait()


class RowScatter:
    def __init__(self, here, hidden, high, low, strip, away, got_c, acc_a, acc_b, got_1, acc_1, got_2, acc_2, got_z, sems):
        self.here, self.hidden, self.high, self.low, self.strip, self.away = here, hidden, high, low, strip, away
        self.got_c, self.acc_a, self.acc_b, self.got_1, self.acc_1 = got_c, acc_a, acc_b, got_1, acc_1
        self.got_2, self.acc_2, self.got_z, self.sems = got_2, acc_2, got_z, sems

    def strips(self):
        c = self.here[3]

        def one(k, carry):
            i, j = lax.div(k, 4), lax.rem(k, 4)
            own = self.hidden[span(k * BLK, BLK), :]
            both = dot16(own, self.high[...]) + dot16(own, self.low[...])
            self.strip[...] = both.reshape(NZ, NC, 8, 1024)
            self.away[i, j] = self.strip[:, 1 - c]
            keep = self.strip[:, c]
            self.acc_a[i, j] = keep[:, :, :512]
            self.acc_b[j, i] = keep[:, :, 512:]
            return carry

        lax.fori_loop(0, 16, one, 0)

    def core(self):
        x, y, z, c = self.here
        return [remote(self.away, self.got_c, self.sems, 0, device(x, y, z, 1 - c))]

    def core_start(self):
        start(self.core())

    def core_end(self):
        wait(self.core())

        def add(k, carry):
            i, j = lax.div(k, 4), lax.rem(k, 4)
            self.acc_a[i, j] = self.acc_a[i, j] + self.got_c[i, j, :, :, :512]
            self.acc_b[j, i] = self.acc_b[j, i] + self.got_c[i, j, :, :, 512:]
            return carry

        lax.fori_loop(0, 16, add, 0)

    def ring(self, slots):
        x, y, z, c = self.here
        copies = []
        for axis, at, size, acc in ((0, x, NX, self.acc_a), (1, y, NY, self.acc_b)):
            up, far, down = lax.rem(at + 1, size), lax.rem(at + 2, size), lax.rem(at + 3, size)
            plus = device(up, y, z, c) if axis == 0 else device(x, up, z, c)
            minus = device(down, y, z, c) if axis == 0 else device(x, down, z, c)
            routes = (
                (acc.at[far, 0:2], plus),
                (acc.at[far, 2:4], minus),
                (acc.at[down, 0:2], minus),
                (acc.at[up, 2:4], plus),
                (acc.at[up, 0:2], plus),
                (acc.at[down, 2:4], minus),
            )
            for slot in slots:
                src, peer = routes[slot]
                copies.append(remote(src, self.got_1.at[axis, slot], self.sems, 1 + 6 * axis + slot, peer))
        return copies

    def far_start(self):
        start(self.ring((0, 1)))

    def near_start(self):
        start(self.ring((2, 3)))

    def pass_on(self):
        x, y, z, c = self.here
        wait(self.ring((0, 1)))
        for axis, at, size, acc in ((0, x, NX, self.acc_a), (1, y, NY, self.acc_b)):
            up, down = lax.rem(at + 1, size), lax.rem(at + 3, size)

            def add(j, carry):
                acc[up, j] = acc[up, j] + self.got_1[axis, 0, j]
                acc[down, 2 + j] = acc[down, 2 + j] + self.got_1[axis, 1, j]
                return carry

            lax.fori_loop(0, 2, add, 0)
        start(self.ring((4, 5)))

    def first_end(self):
        x, y, z, c = self.here
        wait(self.ring((2, 3)))
        wait(self.ring((4, 5)))
        for axis, at, acc in ((0, x, self.acc_a), (1, y, self.acc_b)):
            got = self.got_1

            def add(j, carry):
                self.acc_1[axis, j] = acc[at, j] + got[axis, 2, j] + got[axis, 4, j]
                self.acc_1[axis, 2 + j] = acc[at, 2 + j] + got[axis, 3, j] + got[axis, 5, j]
                return carry

            lax.fori_loop(0, 2, add, 0)

    def second(self):
        x, y, z, c = self.here
        copies = []
        for k in range(3):
            xk, yk = lax.rem(x + k + 1, NX), lax.rem(y + k + 1, NY)
            copies.append(remote(self.acc_1.at[0, yk], self.got_2.at[0, k], self.sems, 13 + k, device(x, yk, z, c)))
            copies.append(remote(self.acc_1.at[1, xk], self.got_2.at[1, k], self.sems, 16 + k, device(xk, y, z, c)))
        return copies

    def second_start(self):
        start(self.second())

    def second_end(self):
        x, y, z, c = self.here
        wait(self.second())
        got = self.got_2
        self.acc_2[:, 0] = self.acc_1[0, y] + got[0, 0] + got[0, 1] + got[0, 2]
        self.acc_2[:, 1] = self.acc_1[1, x] + got[1, 0] + got[1, 1] + got[1, 2]

    def third(self):
        x, y, z, c = self.here
        copies = []
        for k in range(7):
            zk = lax.rem(z + k + 1, NZ)
            copies.append(remote(self.acc_2.at[zk], self.got_z.at[k], self.sems, 19 + k, device(x, y, zk, c)))
        return copies

    def third_start(self):
        start(self.third())

    def third_end(self, out_ref, row):
        wait(self.third())
        own = self.acc_2[self.here[2]]
        for k in range(7):
            own = own + self.got_z[k]
        out_ref[row : row + 8, :512] = own[0]
        out_ref[row : row + 8, 512:] = own[1]


def split(rows, high, low):
    high[...] = rows.astype(bf16)
    low[...] = (rows - high[...].astype(f32)).astype(bf16)


def kernel(count, hidden, weight, partner, whitened, grad_weight, grad_hidden,
           tile, tile_got, tile_sems,
           cent, packed, summed, acc, got_c, got_1, acc_1, got_2, acc_2, got_z, full_z, sems_1, sems_2,
           inv, inv_block, inv_stack, white, grad, mirror, total, grad_z, grad_mean, late, hidden_t, high, low,
           strip, away, w_got_c, acc_a, acc_b, w_got_1, w_acc_1, w_got_2, w_acc_2, w_got_z, w_sems_1, w_sems_2):
    here = place()
    x, y, z, c = here
    N = 256
    barrier = pltpu.get_barrier_semaphore()
    for k in range(1, NZ * NC):
        own = lax.rem(z * NC + c + k, NZ * NC)
        pl.semaphore_signal(barrier, inc=1, device_id=device(x, y, lax.div(own, NC), lax.rem(own, NC)), device_id_type=MESH)
    for k in range(1, NX * NY):
        own = lax.rem(x * NY + y + k, NX * NY)
        pl.semaphore_signal(barrier, inc=1, device_id=device(lax.div(own, NY), lax.rem(own, NY), z, c), device_id_type=MESH)
    for part in range(4):
        cols = slice(part * 256, part * 256 + 256)
        strip_e = dot16(hidden[...], weight[:, cols])
        cent[:N, cols] = strip_e
        sums = jnp.sum(strip_e, axis=0, keepdims=True)
        tile[0, 2 * part : 2 * part + 1, :] = sums[:, :BLK]
        tile[0, 2 * part + 1 : 2 * part + 2, :] = sums[:, BLK:]
    sums = dot16(jnp.ones((8, N), bf16), hidden[...])
    for i in range(16):
        tile[0, 8 + i : 9 + i, :] = sums[0:1, i * BLK : (i + 1) * BLK]
    hidden_t[...] = hidden[...].T
    pl.semaphore_wait(barrier, NZ * NC + NX * NY - 2)
    tile_sum(here, tile, tile_got, tile_sems)
    for i in range(8):
        cols = slice(i * BLK, (i + 1) * BLK)
        cent[:N, cols] = cent[:N, cols] - tile[2, i : i + 1, :] * (1.0 / count)
    store_lower(packed, cent[:N, :], cent[:N, :])
    split(cent[:N, :], high, low)
    reduce_buffers = (acc, got_c, got_1, acc_1, got_2, acc_2, got_z, full_z)
    row_buffers = (high, low, strip, away, w_got_c, acc_a, acc_b, w_got_1, w_acc_1, w_got_2, w_acc_2, w_got_z)
    by_cent = RowScatter(here, hidden_t, *row_buffers, w_sems_1)
    by_grad = RowScatter(here, hidden_t, *row_buffers, w_sems_2)

    def cent_strips():
        by_cent.strips()
        by_cent.core_start()

    all_sum(here, packed, summed, *reduce_buffers, sems_1, {"first": cent_strips, "core back": by_cent.core_end})
    by_cent.far_start()
    by_cent.near_start()

    def to_second():
        by_cent.first_end()
        by_cent.second_start()

    def to_third():
        by_cent.second_end()
        by_cent.third_start()

    inverse_factor(1.0 / (count - 1), summed, inv, inv_block, inv_stack, {2: by_cent.pass_on, 4: to_second, 6: to_third})
    by_cent.third_end(cent, N)
    for part in range(4):
        stop = part * 256 + 256
        white[:, stop - 256 : stop] = dots(cent[:, :stop], inv[stop - 256 : stop, :stop], 1, 1)
    wh = white[:N, :]
    whitened[...] = wh.astype(bf16)
    row_norm = jnp.sqrt(jnp.sum(wh * wh, axis=1, keepdims=True) + epsilon)
    unit = wh / row_norm
    pick = (lax.broadcasted_iota(jnp.int32, (N, N), 0) == partner[...]).astype(f32)
    pick = (pick + pick.T).astype(bf16)
    near = jnp.zeros_like(unit)
    rest = unit
    for _ in range(3):
        term = rest.astype(bf16)
        near = near + dot16(pick, term)
        rest = rest - term.astype(f32)
    grad_unit = 2.0 * (2.0 * unit - near)
    inner_prod = jnp.sum(wh * grad_unit, axis=1, keepdims=True)
    gr = grad_unit / row_norm - wh * (inner_prod / (row_norm * row_norm * row_norm))
    grad[...] = gr
    split(gr, high, low)
    store_lower(packed, grad[...], white[:N, :])
    sums = jnp.sum(gr, axis=0, keepdims=True)
    sub = lax.broadcasted_iota(jnp.int32, (8, BLK), 0)
    lane = lax.broadcasted_iota(jnp.int32, (8, BLK), 1)
    for i in range(8):
        at = 16 * (i * (i + 1) // 2 + i)
        own = jnp.broadcast_to(sums[:, i * BLK : (i + 1) * BLK], (8, BLK))
        swapped = pltpu.roll(own, 64, 1)
        packed[at] = jnp.where(
            (lane >= 64) & (sub == 0), swapped, jnp.where((lane >= 64) & (sub == 1), own, packed[at])
        )
    all_sum(
        here, packed, summed, *reduce_buffers, sems_2,
        {
            "core": by_grad.strips,
            "first": by_grad.core_start,
            "second": by_grad.core_end,
            "third": by_grad.far_start,
            "third back": by_grad.near_start,
            "core back": by_grad.pass_on,
        },
    )
    by_grad.first_end()
    by_grad.second_start()
    lane1 = lax.broadcasted_iota(jnp.int32, (1, BLK), 1)
    r = lax.broadcasted_iota(jnp.int32, (BLK, BLK), 0)
    l = lax.broadcasted_iota(jnp.int32, (BLK, BLK), 1)
    scale = 1.0 / (count - 1)
    for i in range(8):
        for j in range(i + 1):
            block = get_block(summed, i, j)
            turned = block.T
            rows, cols = slice(i * BLK, (i + 1) * BLK), slice(j * BLK, (j + 1) * BLK)
            if i == j:
                mirror[rows, cols] = jnp.where(r >= l, block, turned) * scale
                sums = jnp.where(lane1 < 64, pltpu.roll(block[0:1, :], 64, 1), block[1:2, :]) * (1.0 / count)
                grad_mean[:, cols] = jnp.broadcast_to(sums, (8, BLK))
                total[:N, cols] = grad[:, cols] - sums
            else:
                mirror[rows, cols] = block * scale
                mirror[cols, rows] = turned * scale
    total[N:, :] = jnp.zeros((8, 1024), f32)
    for part in range(4):
        cols = slice(part * 256, part * 256 + 256)
        total[:, cols] = total[:, cols] - dots(white[...], mirror[:, cols])
    for part in range(4):
        start_at = part * 256
        cols = slice(start_at, start_at + 256)
        both = dots(total[:, start_at:], inv[start_at:1024, cols])
        grad_z[:, cols] = both[:N].astype(bf16)
        late[:, cols] = both[N:]

    def hidden_part(k, carry):
        own = span(k * 256, 256)
        grad_hidden[:, own] = dot16(grad_z[...], weight[own, :], 1, 1).astype(bf16)
        return carry

    by_grad.second_end()
    by_grad.third_start()
    lax.fori_loop(0, 8, hidden_part, 0)
    units = jnp.broadcast_to(tile[2, pl.ds(8 + x * NY + y, 1), :], (8, BLK))
    mine = jnp.sum(jnp.where(lane == (z * NC + c) * 8 + sub, units, 0.0), axis=1, keepdims=True)
    by_grad.third_end(total, N)
    rows = total[N:, :] - mine * grad_mean[...]
    grad_weight[...] = late[...] + dots(rows, inv[:1024, :])


def body(hidden, weight, partners):
    count = hidden.shape[0] * lax.axis_size("group") * lax.axis_size("dp")
    vmem = pl.BlockSpec(memory_space=pltpu.VMEM)
    V, sem = pltpu.VMEM, pltpu.SemaphoreType.DMA
    return pl.pallas_call(
        functools.partial(kernel, count),
        out_shape=(
            jax.ShapeDtypeStruct((256, 1024), bf16),
            jax.ShapeDtypeStruct((8, 1024), f32),
            jax.ShapeDtypeStruct((256, 2048), bf16),
        ),
        in_specs=[vmem] * 3,
        out_specs=(vmem,) * 3,
        scratch_shapes=[
            V((3, 24, 128), f32), V((2, 15, 24, 128), f32), sem((2, 30)),
            V((264, 1024), f32), V((576, 8, 128), f32), V((576, 8, 128), f32),
            V((288, 8, 128), f32), V((288, 8, 128), f32), V((2, 3, 36, 8, 128), f32), V((2, 36, 8, 128), f32),
            V((2, 3, T, 8, 128), f32), V((24, 8, 128), f32), V((7, 3, 8, 128), f32), V((24, 8, 128), f32),
            sem((2, 40)), sem((2, 40)),
            V((1920, 1024), f32), V((BLK, BLK), f32), V((768, 1024), bf16), V((264, 1024), f32),
            V((256, 1024), f32), V((1024, 1024), f32), V((264, 1024), f32), V((256, 1024), bf16),
            V((8, 1024), f32), V((8, 1024), f32), V((2048, 256), bf16), V((256, 1024), bf16), V((256, 1024), bf16),
            V((8, 2, 8, 1024), f32), V((4, 4, 8, 8, 1024), f32), V((4, 4, 8, 8, 1024), f32),
            V((4, 4, 8, 8, 512), f32), V((4, 4, 8, 8, 512), f32), V((2, 6, 2, 8, 8, 512), f32),
            V((2, 4, 8, 8, 512), f32), V((2, 3, 8, 8, 512), f32), V((8, 2, 8, 512), f32), V((7, 2, 8, 512), f32),
            sem((2, 26)), sem((2, 26)),
        ],
        compiler_params=pltpu.CompilerParams(collective_id=0, has_side_effects=True, vmem_limit_bytes=60 * MB),
        name="whitening_step",
    )(hidden, weight, partners)


def solution(mesh):
    return jax.shard_map(
        body,
        mesh=mesh,
        in_specs=(P(("group", "dp"), None), P(), P(("group", "dp"), None)),
        out_specs=(P(("group", "dp"), None), P(("group", "dp"), None), P(("group", "dp"), None)),
        check_vma=False,
    )
```

```python
import functools

import jax
import jax.numpy as jnp
from jax import lax
from jax.experimental import pallas as pl
from jax.experimental.pallas import tpu as pltpu
from jax.sharding import PartitionSpec as P

epsilon = 1e-06
highest = lax.Precision.HIGHEST
MESH = pl.DeviceIdType.MESH
NX, NY, NZ, NC = 4, 4, 8, 2
BLK = 128
MB = 1 << 20
f32, bf16 = jnp.float32, jnp.bfloat16


def place():
    dp = lax.axis_index("dp")
    x = lax.axis_index("group")
    return x, lax.div(dp, NZ * NC), lax.rem(lax.div(dp, NC), NZ), lax.rem(dp, NC)


def device(x, y, z, c):
    return (x, (y * NZ + z) * NC + c)


def remote(src, dst, sems, slot, peer):
    return pltpu.make_async_remote_copy(
        src_ref=src,
        dst_ref=dst,
        send_sem=sems.at[0, slot],
        recv_sem=sems.at[1, slot],
        device_id=peer,
        device_id_type=MESH,
    )


def start(copies):
    for copy in copies:
        copy.start()


def wait(copies):
    for copy in copies:
        copy.wait()


def send(src, dst, sems, slot, peer):
    copy = remote(src, dst, sems, slot, peer)
    copy.start()
    return copy


def nothing():
    pass


def dots(a, b, ca=1, cb=0):
    return lax.dot_general(a, b, (((ca,), (cb,)), ((), ())), precision=highest, preferred_element_type=f32)


def dot16(a, b, ca=1, cb=0):
    return lax.dot_general(a, b, (((ca,), (cb,)), ((), ())), preferred_element_type=f32)


def span(start, size):
    return pl.ds(pl.multiple_of(start, size), size)


def inverse_factor_block(pan):
    sub = lax.broadcasted_iota(jnp.int32, (8, BLK), 0)
    lane = lax.broadcasted_iota(jnp.int32, (8, BLK), 1)

    def over_sublanes(tile, k):
        return jnp.broadcast_to(tile[k : k + 1, :], (8, BLK))

    def over_lanes(tile, k):
        return jnp.broadcast_to(tile[:, k : k + 1], (8, BLK))

    pan = list(pan)
    for p in range(16):
        base = 8 * p
        inside = (lane >= base) & (lane < base + 8)
        own = pan[p]
        cols = [over_lanes(own, base + k) for k in range(8)]
        low = {(i, k): over_sublanes(cols[k], i) for k in range(8) for i in range(k, 8)}
        own = jnp.where(inside, jnp.where(lane - base == sub, 1.0, 0.0), own)
        rows = [over_sublanes(own, k) for k in range(8)]
        ahead = p + 1 < 16
        if ahead:
            left = [over_lanes(pan[p + 1], base + k) for k in range(8)]
            after = jnp.where(inside, 0.0, pan[p + 1])
        scale = []
        for k in range(8):
            rs = lax.rsqrt(low[k, k])
            scale.append(rs)
            rows[k] = rows[k] * rs
            for i in range(k + 1, 8):
                low[i, k] = low[i, k] * rs
            if ahead:
                left[k] = left[k] * rs
                after = after - left[k] * rows[k]
            for i in range(k + 1, 8):
                for m in range(k + 1, i + 1):
                    low[i, m] = low[i, m] - low[i, k] * low[m, k]
                rows[i] = rows[i] - low[i, k] * rows[k]
                if ahead:
                    left[i] = left[i] - left[k] * low[i, k]
        done = rows[0]
        for k in range(1, 8):
            done = jnp.where(sub == k, rows[k], done)
        pan[p] = done
        if ahead:
            pan[p + 1] = after
        if p + 2 < 16:
            back = [None] * 8
            for k in range(7, -1, -1):
                t = rows[k]
                for m in range(k + 1, 8):
                    t = t - low[m, k] * back[m]
                back[k] = t * scale[k]
            for q in range(p + 2, 16):
                t = jnp.where(inside, 0.0, pan[q])
                for k in range(8):
                    t = t - over_lanes(pan[q], base + k) * back[k]
                pan[q] = t
    return [jnp.where(lane <= sub + 8 * p, pan[p], 0.0) for p in range(16)]


def thirds(v):
    high = v.astype(bf16)
    rest = v - high.astype(f32)
    mid = rest.astype(bf16)
    return high, mid, (rest - mid.astype(f32)).astype(bf16)


def left_stack(v):
    h, m, l = thirds(v)
    return jnp.concatenate([h, h, m, h, l, m], axis=1)


def right_stack(v, axis):
    h, m, l = thirds(v)
    return jnp.concatenate([h, m, h, l, h, m], axis=axis)


def inverse_factor(scale, in_ref, out_ref, inv_ref, stack_ref, beside):
    for i in range(8):
        for j in range(i + 1):
            block = get_block(in_ref, i, j) * scale
            rows, cols = slice(i * BLK, (i + 1) * BLK), slice(j * BLK, (j + 1) * BLK)
            turned = block.T
            if i == j:
                r = lax.broadcasted_iota(jnp.int32, (BLK, BLK), 0)
                l = lax.broadcasted_iota(jnp.int32, (BLK, BLK), 1)
                out_ref[rows, cols] = jnp.where(r >= l, block, turned)
            else:
                out_ref[rows, cols] = block
                out_ref[cols, rows] = turned
    out_ref[1024:, :] = jnp.zeros((7 * BLK, 1024), f32)
    lane = lax.broadcasted_iota(jnp.int32, (BLK, 1024), 1)

    def factor(block):
        return inverse_factor_block([block[8 * p : 8 * p + 8, :] for p in range(16)])

    def keep(tiles):
        for p, tile in enumerate(tiles):
            inv_ref[8 * p : 8 * p + 8, :] = tile

    def scaled_row(i):
        own = span(i * BLK, BLK)
        inv = inv_ref[...]
        row = dot16(left_stack(inv), right_stack(out_ref[own, :], 0))
        inside = (lane >= i * BLK) & (lane < (i + 1) * BLK)
        row = jnp.where(inside, jnp.concatenate([inv] * 8, axis=1), row)
        out_ref[own, :] = jnp.where(lane < (i + 1) * BLK, row, 0.0)
        return row

    keep(factor(out_ref[0:BLK, 0:BLK]))

    def step(i, carry):
        for at, work in beside.items():
            pl.when(i == at)(work)
        own, nxt = span(i * BLK, BLK), span((i + 1) * BLK, BLK)
        below = pl.ds(pl.multiple_of((i + 1) * BLK, BLK), 7 * BLK)
        inv = inv_ref[...]
        left = dots(out_ref[nxt, own], inv, 1, 1)
        block = out_ref[nxt, nxt] - dots(left, left, 1, 1)
        tiles = factor(block)
        stack_ref[...] = right_stack(scaled_row(i), 0)
        left = dot16(left_stack(out_ref[below, own]), right_stack(inv, 1), 1, 1)
        out_ref[below, own] = jnp.zeros((7 * BLK, BLK), f32)
        left = left_stack(left)
        for part in range(4):
            cols = slice(part * 256, part * 256 + 256)
            out_ref[below, cols] = out_ref[below, cols] - dot16(left, stack_ref[:, cols])
        keep(tiles)
        return carry

    lax.fori_loop(0, 7, step, 0)
    scaled_row(7)


def get_block(ref, i, j):
    at = i * (i + 1) // 2 + j
    return ref[16 * at : 16 * at + 16].reshape(BLK, BLK)


def store_lower(out_ref, a, b):
    for half in range(4):
        strip = dots(a[:, half * 256 : half * 256 + 256], b[:, : half * 256 + 256], 0, 0)
        for i in (2 * half, 2 * half + 1):
            for j in range(i + 1):
                r = (i - 2 * half) * BLK
                at = i * (i + 1) // 2 + j
                out_ref[16 * at : 16 * at + 16] = strip[r : r + BLK, j * BLK : (j + 1) * BLK].reshape(16, 8, BLK)


def tile_sum(here, tile, got, sems):
    x, y, z, c = here
    copies = []
    for k in range(1, NZ * NC):
        own = lax.rem(z * NC + c + k, NZ * NC)
        peer = device(x, y, lax.div(own, NC), lax.rem(own, NC))
        copies.append(send(tile.at[0], got.at[0, k - 1], sems, k - 1, peer))
    wait(copies)
    total = tile[0]
    for k in range(15):
        total = total + got[0, k]
    tile[1] = total
    copies = []
    for k in range(1, NX * NY):
        own = lax.rem(x * NY + y + k, NX * NY)
        peer = device(lax.div(own, NY), lax.rem(own, NY), z, c)
        copies.append(send(tile.at[1], got.at[1, k - 1], sems, 14 + k, peer))
    wait(copies)
    for k in range(15):
        total = total + got[1, k]
    tile[2] = total


T = 9


def all_sum(here, in_ref, out_ref, acc, got_c, got_1, acc_1, got_2, acc_2, got_z, full_z, sems, during):
    x, y, z, c = here
    across = device(x, y, z, 1 - c)
    xs = [device(lax.rem(x + k, NX), y, z, c) for k in range(1, NX)]
    ys = [device(x, lax.rem(y + k, NY), z, c) for k in range(1, NY)]
    zs = [device(x, y, lax.rem(z + k, NZ), c) for k in range(1, NZ)]
    x_at = [lax.rem(x + k, NX) for k in range(1, NX)]
    y_at = [lax.rem(y + k, NY) for k in range(1, NY)]
    z_at = [lax.rem(z + k, NZ) for k in range(1, NZ)]
    copy = send(in_ref.at[pl.ds((1 - c) * 288, 288)], got_c, sems, 0, across)
    during.get("core", nothing)()
    copy.wait()
    acc[...] = in_ref[pl.ds(c * 288, 288)] + got_c[...]
    copies = []
    for k in range(3):
        copies.append(send(acc.at[pl.ds(x_at[k] * 36, 36)], got_1.at[0, k], sems, 1 + k, xs[k]))
        copies.append(send(acc.at[pl.ds(144 + y_at[k] * 36, 36)], got_1.at[1, k], sems, 4 + k, ys[k]))
    during.get("first", nothing)()
    wait(copies)
    acc_1[0] = acc[pl.ds(x * 36, 36)] + got_1[0, 0] + got_1[0, 1] + got_1[0, 2]
    acc_1[1] = acc[pl.ds(144 + y * 36, 36)] + got_1[1, 0] + got_1[1, 1] + got_1[1, 2]
    copies = []
    for k in range(3):
        copies.append(send(acc_1.at[0, pl.ds(y_at[k] * T, T)], got_2.at[0, k], sems, 7 + k, ys[k]))
        copies.append(send(acc_1.at[1, pl.ds(x_at[k] * T, T)], got_2.at[1, k], sems, 10 + k, xs[k]))
    during.get("second", nothing)()
    wait(copies)
    acc_2[0:T] = acc_1[0, pl.ds(y * T, T)] + got_2[0, 0] + got_2[0, 1] + got_2[0, 2]
    acc_2[T : 2 * T] = acc_1[1, pl.ds(x * T, T)] + got_2[1, 0] + got_2[1, 1] + got_2[1, 2]
    acc_2[2 * T : 24] = jnp.zeros((24 - 2 * T, 8, 128), f32)
    copies = [send(acc_2.at[pl.ds(3 * z_at[k], 3)], got_z.at[k], sems, 13 + k, zs[k]) for k in range(7)]
    during.get("third", nothing)()
    wait(copies)
    own = acc_2[pl.ds(3 * z, 3)]
    for k in range(7):
        own = own + got_z[k]
    mine = full_z.at[pl.ds(3 * z, 3)]
    mine[...] = own
    copies = [send(mine, mine, sems, 20 + k, zs[k]) for k in range(7)]
    during.get("third back", nothing)()
    wait(copies)
    base = c * 288
    first, second = out_ref.at[pl.ds(base + (x * 4 + y) * T, T)], out_ref.at[pl.ds(base + 144 + (y * 4 + x) * T, T)]
    first[...] = full_z[0:T]
    second[...] = full_z[T : 2 * T]
    copies = []
    for k in range(3):
        copies.append(send(first, first, sems, 27 + k, ys[k]))
        copies.append(send(second, second, sems, 30 + k, xs[k]))
    wait(copies)
    first, second = out_ref.at[pl.ds(base + x * 36, 36)], out_ref.at[pl.ds(base + 144 + y * 36, 36)]
    copies = []
    for k in range(3):
        copies.append(send(first, first, sems, 33 + k, xs[k]))
        copies.append(send(second, second, sems, 36 + k, ys[k]))
    over = [send(first, first, sems, 39, across), send(second, second, sems, 40, across)]
    during.get("first back", nothing)()
    for k in range(3):
        copies[2 * k].wait()
        chunk = out_ref.at[pl.ds(base + x_at[2 - k] * 36, 36)]
        over.append(send(chunk, chunk, sems, 41 + 2 * k, across))
        copies[2 * k + 1].wait()
        chunk = out_ref.at[pl.ds(base + 144 + y_at[2 - k] * 36, 36)]
        over.append(send(chunk, chunk, sems, 42 + 2 * k, across))
    during.get("core back", nothing)()
    wait(over)


class RowScatter:
    def __init__(self, here, hidden, high, low, strip, away, got_c, acc_a, acc_b, got_1, acc_1, got_2, acc_2, got_z, sems):
        self.here, self.hidden, self.high, self.low, self.strip, self.away = here, hidden, high, low, strip, away
        self.got_c, self.acc_a, self.acc_b, self.got_1, self.acc_1 = got_c, acc_a, acc_b, got_1, acc_1
        self.got_2, self.acc_2, self.got_z, self.sems = got_2, acc_2, got_z, sems

    def strips(self):
        c = self.here[3]

        def one(k, carry):
            i, j = lax.div(k, 4), lax.rem(k, 4)
            own = self.hidden[span(k * BLK, BLK), :]
            both = dot16(own, self.high[...]) + dot16(own, self.low[...])
            self.strip[...] = both.reshape(NZ, NC, 8, 1024)
            self.away[i, j] = self.strip[:, 1 - c]
            keep = self.strip[:, c]
            self.acc_a[i, j] = keep[:, :, :512]
            self.acc_b[j, i] = keep[:, :, 512:]
            return carry

        lax.fori_loop(0, 16, one, 0)

    def core(self):
        x, y, z, c = self.here
        return [remote(self.away, self.got_c, self.sems, 0, device(x, y, z, 1 - c))]

    def core_start(self):
        start(self.core())

    def core_end(self):
        wait(self.core())

        def add(k, carry):
            i, j = lax.div(k, 4), lax.rem(k, 4)
            self.acc_a[i, j] = self.acc_a[i, j] + self.got_c[i, j, :, :, :512]
            self.acc_b[j, i] = self.acc_b[j, i] + self.got_c[i, j, :, :, 512:]
            return carry

        lax.fori_loop(0, 16, add, 0)

    def ring(self, slots):
        x, y, z, c = self.here
        copies = []
        for axis, at, size, acc in ((0, x, NX, self.acc_a), (1, y, NY, self.acc_b)):
            up, far, down = lax.rem(at + 1, size), lax.rem(at + 2, size), lax.rem(at + 3, size)
            plus = device(up, y, z, c) if axis == 0 else device(x, up, z, c)
            minus = device(down, y, z, c) if axis == 0 else device(x, down, z, c)
            routes = (
                (acc.at[far, 0:2], plus),
                (acc.at[far, 2:4], minus),
                (acc.at[down, 0:2], minus),
                (acc.at[up, 2:4], plus),
                (acc.at[up, 0:2], plus),
                (acc.at[down, 2:4], minus),
            )
            for slot in slots:
                src, peer = routes[slot]
                copies.append(remote(src, self.got_1.at[axis, slot], self.sems, 1 + 6 * axis + slot, peer))
        return copies

    def far_start(self):
        start(self.ring((0, 1)))

    def near_start(self):
        start(self.ring((2, 3)))

    def pass_on(self):
        x, y, z, c = self.here
        wait(self.ring((0, 1)))
        for axis, at, size, acc in ((0, x, NX, self.acc_a), (1, y, NY, self.acc_b)):
            up, down = lax.rem(at + 1, size), lax.rem(at + 3, size)

            def add(j, carry):
                acc[up, j] = acc[up, j] + self.got_1[axis, 0, j]
                acc[down, 2 + j] = acc[down, 2 + j] + self.got_1[axis, 1, j]
                return carry

            lax.fori_loop(0, 2, add, 0)
        start(self.ring((4, 5)))

    def first_end(self):
        x, y, z, c = self.here
        wait(self.ring((2, 3)))
        wait(self.ring((4, 5)))
        for axis, at, acc in ((0, x, self.acc_a), (1, y, self.acc_b)):
            got = self.got_1

            def add(j, carry):
                self.acc_1[axis, j] = acc[at, j] + got[axis, 2, j] + got[axis, 4, j]
                self.acc_1[axis, 2 + j] = acc[at, 2 + j] + got[axis, 3, j] + got[axis, 5, j]
                return carry

            lax.fori_loop(0, 2, add, 0)

    def second(self):
        x, y, z, c = self.here
        copies = []
        for k in range(3):
            xk, yk = lax.rem(x + k + 1, NX), lax.rem(y + k + 1, NY)
            copies.append(remote(self.acc_1.at[0, yk], self.got_2.at[0, k], self.sems, 13 + k, device(x, yk, z, c)))
            copies.append(remote(self.acc_1.at[1, xk], self.got_2.at[1, k], self.sems, 16 + k, device(xk, y, z, c)))
        return copies

    def second_start(self):
        start(self.second())

    def second_end(self):
        x, y, z, c = self.here
        wait(self.second())
        got = self.got_2
        self.acc_2[:, 0] = self.acc_1[0, y] + got[0, 0] + got[0, 1] + got[0, 2]
        self.acc_2[:, 1] = self.acc_1[1, x] + got[1, 0] + got[1, 1] + got[1, 2]

    def third(self):
        x, y, z, c = self.here
        copies = []
        for k in range(7):
            zk = lax.rem(z + k + 1, NZ)
            copies.append(remote(self.acc_2.at[zk], self.got_z.at[k], self.sems, 19 + k, device(x, y, zk, c)))
        return copies

    def third_start(self):
        start(self.third())

    def third_end(self, out_ref, row):
        wait(self.third())
        own = self.acc_2[self.here[2]]
        for k in range(7):
            own = own + self.got_z[k]
        out_ref[row : row + 8, :512] = own[0]
        out_ref[row : row + 8, 512:] = own[1]


def split(rows, high, low):
    high[...] = rows.astype(bf16)
    low[...] = (rows - high[...].astype(f32)).astype(bf16)


def kernel(count, hidden_in, weight_in, partner, whitened, grad_weight, grad_hidden,
           hidden, weight, in_sems, tile, tile_got, tile_sems,
           cent, packed, summed, acc, got_c, got_1, acc_1, got_2, acc_2, got_z, full_z, sems_1, sems_2,
           inv, inv_block, inv_stack, white, grad, mirror, total, grad_z, grad_mean, late, hidden_t, high, low,
           strip, away, w_got_c, acc_a, acc_b, w_got_1, w_acc_1, w_got_2, w_acc_2, w_got_z, w_sems_1, w_sems_2):
    here = place()
    x, y, z, c = here
    N = 256
    loads = [
        pltpu.make_async_copy(hidden_in, hidden, in_sems.at[0]),
        pltpu.make_async_copy(weight_in, weight, in_sems.at[1]),
    ]
    start(loads)
    barrier = pltpu.get_barrier_semaphore()
    for k in range(1, NZ * NC):
        own = lax.rem(z * NC + c + k, NZ * NC)
        pl.semaphore_signal(barrier, inc=1, device_id=device(x, y, lax.div(own, NC), lax.rem(own, NC)), device_id_type=MESH)
    for k in range(1, NX * NY):
        own = lax.rem(x * NY + y + k, NX * NY)
        pl.semaphore_signal(barrier, inc=1, device_id=device(lax.div(own, NY), lax.rem(own, NY), z, c), device_id_type=MESH)
    loads[0].wait()
    hidden_t[...] = hidden[...].T
    loads[1].wait()
    for part in range(4):
        cols = slice(part * 256, part * 256 + 256)
        strip_e = dot16(hidden[...], weight[:, cols])
        cent[:N, cols] = strip_e
        sums = jnp.sum(strip_e, axis=0, keepdims=True)
        tile[0, 2 * part : 2 * part + 1, :] = sums[:, :BLK]
        tile[0, 2 * part + 1 : 2 * part + 2, :] = sums[:, BLK:]
    sums = dot16(jnp.ones((8, N), bf16), hidden[...])
    for i in range(16):
        tile[0, 8 + i : 9 + i, :] = sums[0:1, i * BLK : (i + 1) * BLK]
    pl.semaphore_wait(barrier, NZ * NC + NX * NY - 2)
    tile_sum(here, tile, tile_got, tile_sems)
    for i in range(8):
        cols = slice(i * BLK, (i + 1) * BLK)
        cent[:N, cols] = cent[:N, cols] - tile[2, i : i + 1, :] * (1.0 / count)
    store_lower(packed, cent[:N, :], cent[:N, :])
    split(cent[:N, :], high, low)
    reduce_buffers = (acc, got_c, got_1, acc_1, got_2, acc_2, got_z, full_z)
    row_buffers = (high, low, strip, away, w_got_c, acc_a, acc_b, w_got_1, w_acc_1, w_got_2, w_acc_2, w_got_z)
    by_cent = RowScatter(here, hidden_t, *row_buffers, w_sems_1)
    by_grad = RowScatter(here, hidden_t, *row_buffers, w_sems_2)

    def cent_strips():
        by_cent.strips()
        by_cent.core_start()

    all_sum(here, packed, summed, *reduce_buffers, sems_1, {"first": cent_strips, "core back": by_cent.core_end})
    by_cent.far_start()
    by_cent.near_start()

    def to_second():
        by_cent.first_end()
        by_cent.second_start()

    def to_third():
        by_cent.second_end()
        by_cent.third_start()

    inverse_factor(1.0 / (count - 1), summed, inv, inv_block, inv_stack, {2: by_cent.pass_on, 4: to_second, 6: to_third})
    by_cent.third_end(cent, N)
    for part in range(4):
        stop = part * 256 + 256
        white[:, stop - 256 : stop] = dots(cent[:, :stop], inv[stop - 256 : stop, :stop], 1, 1)
    wh = white[:N, :]
    whitened[...] = wh.astype(bf16)
    row_norm = jnp.sqrt(jnp.sum(wh * wh, axis=1, keepdims=True) + epsilon)
    unit = wh / row_norm
    pick = (lax.broadcasted_iota(jnp.int32, (N, N), 0) == partner[...]).astype(f32)
    pick = (pick + pick.T).astype(bf16)
    near = jnp.zeros_like(unit)
    rest = unit
    for _ in range(3):
        term = rest.astype(bf16)
        near = near + dot16(pick, term)
        rest = rest - term.astype(f32)
    grad_unit = 2.0 * (2.0 * unit - near)
    inner_prod = jnp.sum(wh * grad_unit, axis=1, keepdims=True)
    gr = grad_unit / row_norm - wh * (inner_prod / (row_norm * row_norm * row_norm))
    grad[...] = gr
    split(gr, high, low)
    store_lower(packed, grad[...], white[:N, :])
    sums = jnp.sum(gr, axis=0, keepdims=True)
    sub = lax.broadcasted_iota(jnp.int32, (8, BLK), 0)
    lane = lax.broadcasted_iota(jnp.int32, (8, BLK), 1)
    for i in range(8):
        at = 16 * (i * (i + 1) // 2 + i)
        own = jnp.broadcast_to(sums[:, i * BLK : (i + 1) * BLK], (8, BLK))
        swapped = pltpu.roll(own, 64, 1)
        packed[at] = jnp.where(
            (lane >= 64) & (sub == 0), swapped, jnp.where((lane >= 64) & (sub == 1), own, packed[at])
        )
    def to_second_grad():
        by_grad.first_end()
        by_grad.second_start()

    all_sum(
        here, packed, summed, *reduce_buffers, sems_2,
        {
            "core": by_grad.strips,
            "first": by_grad.core_start,
            "second": by_grad.core_end,
            "third": by_grad.far_start,
            "third back": by_grad.near_start,
            "first back": by_grad.pass_on,
            "core back": to_second_grad,
        },
    )
    lane1 = lax.broadcasted_iota(jnp.int32, (1, BLK), 1)
    r = lax.broadcasted_iota(jnp.int32, (BLK, BLK), 0)
    l = lax.broadcasted_iota(jnp.int32, (BLK, BLK), 1)
    scale = 1.0 / (count - 1)
    for i in range(8):
        for j in range(i + 1):
            block = get_block(summed, i, j)
            turned = block.T
            rows, cols = slice(i * BLK, (i + 1) * BLK), slice(j * BLK, (j + 1) * BLK)
            if i == j:
                mirror[rows, cols] = jnp.where(r >= l, block, turned) * scale
                sums = jnp.where(lane1 < 64, pltpu.roll(block[0:1, :], 64, 1), block[1:2, :]) * (1.0 / count)
                grad_mean[:, cols] = jnp.broadcast_to(sums, (8, BLK))
                total[:N, cols] = grad[:, cols] - sums
            else:
                mirror[rows, cols] = block * scale
                mirror[cols, rows] = turned * scale
    total[N:, :] = jnp.zeros((8, 1024), f32)
    for part in range(4):
        cols = slice(part * 256, part * 256 + 256)
        total[:, cols] = total[:, cols] - dots(white[...], mirror[:, cols])
    by_grad.second_end()
    by_grad.third_start()
    for part in range(4):
        start_at = part * 256
        cols = slice(start_at, start_at + 256)
        both = dots(total[:, start_at:], inv[start_at:1024, cols])
        grad_z[:, cols] = both[:N].astype(bf16)
        late[:, cols] = both[N:]

    def hidden_part(k, carry):
        own = span(k * 256, 256)
        grad_hidden[:, own] = dot16(grad_z[...], weight[own, :], 1, 1).astype(bf16)
        return carry

    lax.fori_loop(0, 8, hidden_part, 0)
    units = jnp.broadcast_to(tile[2, pl.ds(8 + x * NY + y, 1), :], (8, BLK))
    mine = jnp.sum(jnp.where(lane == (z * NC + c) * 8 + sub, units, 0.0), axis=1, keepdims=True)
    by_grad.third_end(total, N)
    rows = total[N:, :] - mine * grad_mean[...]
    grad_weight[...] = late[...] + dots(rows, inv[:1024, :])


def body(hidden, weight, partners):
    count = hidden.shape[0] * lax.axis_size("group") * lax.axis_size("dp")
    vmem = pl.BlockSpec(memory_space=pltpu.VMEM)
    V, sem = pltpu.VMEM, pltpu.SemaphoreType.DMA
    return pl.pallas_call(
        functools.partial(kernel, count),
        out_shape=(
            jax.ShapeDtypeStruct((256, 1024), bf16),
            jax.ShapeDtypeStruct((8, 1024), f32),
            jax.ShapeDtypeStruct((256, 2048), bf16),
        ),
        in_specs=[pl.BlockSpec(memory_space=pl.ANY)] * 2 + [vmem],
        out_specs=(vmem,) * 3,
        scratch_shapes=[
            V((256, 2048), bf16), V((2048, 1024), bf16), sem((2,)),
            V((3, 24, 128), f32), V((2, 15, 24, 128), f32), sem((2, 30)),
            V((264, 1024), f32), V((576, 8, 128), f32), V((576, 8, 128), f32),
            V((288, 8, 128), f32), V((288, 8, 128), f32), V((2, 3, 36, 8, 128), f32), V((2, 36, 8, 128), f32),
            V((2, 3, T, 8, 128), f32), V((24, 8, 128), f32), V((7, 3, 8, 128), f32), V((24, 8, 128), f32),
            sem((2, 47)), sem((2, 47)),
            V((1920, 1024), f32), V((BLK, BLK), f32), V((768, 1024), bf16), V((264, 1024), f32),
            V((256, 1024), f32), V((1024, 1024), f32), V((264, 1024), f32), V((256, 1024), bf16),
            V((8, 1024), f32), V((8, 1024), f32), V((2048, 256), bf16), V((256, 1024), bf16), V((256, 1024), bf16),
            V((8, 2, 8, 1024), f32), V((4, 4, 8, 8, 1024), f32), V((4, 4, 8, 8, 1024), f32),
            V((4, 4, 8, 8, 512), f32), V((4, 4, 8, 8, 512), f32), V((2, 6, 2, 8, 8, 512), f32),
            V((2, 4, 8, 8, 512), f32), V((2, 3, 8, 8, 512), f32), V((8, 2, 8, 512), f32), V((7, 2, 8, 512), f32),
            sem((2, 26)), sem((2, 26)),
        ],
        compiler_params=pltpu.CompilerParams(collective_id=0, has_side_effects=True, vmem_limit_bytes=60 * MB),
        name="whitening_step",
    )(hidden, weight, partners)


def solution(mesh):
    return jax.shard_map(
        body,
        mesh=mesh,
        in_specs=(P(("group", "dp"), None), P(), P(("group", "dp"), None)),
        out_specs=(P(("group", "dp"), None), P(("group", "dp"), None), P(("group", "dp"), None)),
        check_vma=False,
    )
```

```python
import functools

import jax
import jax.numpy as jnp
from jax import lax
from jax.experimental import pallas as pl
from jax.experimental.pallas import tpu as pltpu
from jax.sharding import PartitionSpec as P

epsilon = 1e-06
highest = lax.Precision.HIGHEST
MESH = pl.DeviceIdType.MESH
NX, NY, NZ, NC = 4, 4, 8, 2
BLK = 128
MB = 1 << 20
f32, bf16 = jnp.float32, jnp.bfloat16


def place():
    dp = lax.axis_index("dp")
    x = lax.axis_index("group")
    return x, lax.div(dp, NZ * NC), lax.rem(lax.div(dp, NC), NZ), lax.rem(dp, NC)


def device(x, y, z, c):
    return (x, (y * NZ + z) * NC + c)


def remote(src, dst, sems, slot, peer):
    return pltpu.make_async_remote_copy(
        src_ref=src,
        dst_ref=dst,
        send_sem=sems.at[0, slot],
        recv_sem=sems.at[1, slot],
        device_id=peer,
        device_id_type=MESH,
    )


def start(copies):
    for copy in copies:
        copy.start()


def wait(copies):
    for copy in copies:
        copy.wait()


def send(src, dst, sems, slot, peer):
    copy = remote(src, dst, sems, slot, peer)
    copy.start()
    return copy


def nothing():
    pass


def dots(a, b, ca=1, cb=0):
    return lax.dot_general(a, b, (((ca,), (cb,)), ((), ())), precision=highest, preferred_element_type=f32)


def dot16(a, b, ca=1, cb=0):
    return lax.dot_general(a, b, (((ca,), (cb,)), ((), ())), preferred_element_type=f32)


def span(start, size):
    return pl.ds(pl.multiple_of(start, size), size)


def inverse_factor_block(pan):
    sub = lax.broadcasted_iota(jnp.int32, (8, BLK), 0)
    lane = lax.broadcasted_iota(jnp.int32, (8, BLK), 1)

    def over_sublanes(tile, k):
        return jnp.broadcast_to(tile[k : k + 1, :], (8, BLK))

    def over_lanes(tile, k):
        return jnp.broadcast_to(tile[:, k : k + 1], (8, BLK))

    pan = list(pan)
    for p in range(16):
        base = 8 * p
        inside = (lane >= base) & (lane < base + 8)
        own = pan[p]
        cols = [over_lanes(own, base + k) for k in range(8)]
        low = {(i, k): over_sublanes(cols[k], i) for k in range(8) for i in range(k, 8)}
        own = jnp.where(inside, jnp.where(lane - base == sub, 1.0, 0.0), own)
        rows = [over_sublanes(own, k) for k in range(8)]
        ahead = p + 1 < 16
        if ahead:
            left = [over_lanes(pan[p + 1], base + k) for k in range(8)]
            after = jnp.where(inside, 0.0, pan[p + 1])
        scale = []
        for k in range(8):
            rs = lax.rsqrt(low[k, k])
            scale.append(rs)
            rows[k] = rows[k] * rs
            for i in range(k + 1, 8):
                low[i, k] = low[i, k] * rs
            if ahead:
                left[k] = left[k] * rs
                after = after - left[k] * rows[k]
            for i in range(k + 1, 8):
                for m in range(k + 1, i + 1):
                    low[i, m] = low[i, m] - low[i, k] * low[m, k]
                rows[i] = rows[i] - low[i, k] * rows[k]
                if ahead:
                    left[i] = left[i] - left[k] * low[i, k]
        done = rows[0]
        for k in range(1, 8):
            done = jnp.where(sub == k, rows[k], done)
        pan[p] = done
        if ahead:
            pan[p + 1] = after
        if p + 2 < 16:
            back = [None] * 8
            for k in range(7, -1, -1):
                t = rows[k]
                for m in range(k + 1, 8):
                    t = t - low[m, k] * back[m]
                back[k] = t * scale[k]
            for q in range(p + 2, 16):
                t = jnp.where(inside, 0.0, pan[q])
                for k in range(8):
                    t = t - over_lanes(pan[q], base + k) * back[k]
                pan[q] = t
    return [jnp.where(lane <= sub + 8 * p, pan[p], 0.0) for p in range(16)]


def thirds(v):
    high = v.astype(bf16)
    rest = v - high.astype(f32)
    mid = rest.astype(bf16)
    return high, mid, (rest - mid.astype(f32)).astype(bf16)


def left_stack(v):
    h, m, l = thirds(v)
    return jnp.concatenate([h, h, m, h, l, m], axis=1)


def right_stack(v, axis):
    h, m, l = thirds(v)
    return jnp.concatenate([h, m, h, l, h, m], axis=axis)


def inverse_factor(scale, in_ref, out_ref, inv_ref, stack_ref, beside):
    for i in range(8):
        for j in range(i + 1):
            block = get_block(in_ref, i, j) * scale
            rows, cols = slice(i * BLK, (i + 1) * BLK), slice(j * BLK, (j + 1) * BLK)
            turned = block.T
            if i == j:
                r = lax.broadcasted_iota(jnp.int32, (BLK, BLK), 0)
                l = lax.broadcasted_iota(jnp.int32, (BLK, BLK), 1)
                out_ref[rows, cols] = jnp.where(r >= l, block, turned)
            else:
                out_ref[rows, cols] = block
                out_ref[cols, rows] = turned
    out_ref[1024:, :] = jnp.zeros((7 * BLK, 1024), f32)
    lane = lax.broadcasted_iota(jnp.int32, (BLK, 1024), 1)

    def factor(block):
        return inverse_factor_block([block[8 * p : 8 * p + 8, :] for p in range(16)])

    def keep(tiles):
        for p, tile in enumerate(tiles):
            inv_ref[8 * p : 8 * p + 8, :] = tile

    def scaled_row(i):
        own = span(i * BLK, BLK)
        inv = inv_ref[...]
        row = dot16(left_stack(inv), right_stack(out_ref[own, :], 0))
        inside = (lane >= i * BLK) & (lane < (i + 1) * BLK)
        row = jnp.where(inside, jnp.concatenate([inv] * 8, axis=1), row)
        out_ref[own, :] = jnp.where(lane < (i + 1) * BLK, row, 0.0)
        return row

    keep(factor(out_ref[0:BLK, 0:BLK]))

    def step(i, carry):
        for at, work in beside.items():
            pl.when(i == at)(work)
        own, nxt = span(i * BLK, BLK), span((i + 1) * BLK, BLK)
        below = pl.ds(pl.multiple_of((i + 1) * BLK, BLK), 7 * BLK)
        inv = inv_ref[...]
        left = dots(out_ref[nxt, own], inv, 1, 1)
        block = out_ref[nxt, nxt] - dots(left, left, 1, 1)
        tiles = factor(block)
        stack_ref[...] = right_stack(scaled_row(i), 0)
        left = dot16(left_stack(out_ref[below, own]), right_stack(inv, 1), 1, 1)
        out_ref[below, own] = jnp.zeros((7 * BLK, BLK), f32)
        left = left_stack(left)
        for part in range(4):
            cols = slice(part * 256, part * 256 + 256)
            out_ref[below, cols] = out_ref[below, cols] - dot16(left, stack_ref[:, cols])
        keep(tiles)
        return carry

    lax.fori_loop(0, 7, step, 0)
    scaled_row(7)


def get_block(ref, i, j):
    at = i * (i + 1) // 2 + j
    return ref[16 * at : 16 * at + 16].reshape(BLK, BLK)


def store_lower(out_ref, a, b):
    for half in range(4):
        strip = dots(a[:, half * 256 : half * 256 + 256], b[:, : half * 256 + 256], 0, 0)
        for i in (2 * half, 2 * half + 1):
            for j in range(i + 1):
                r = (i - 2 * half) * BLK
                at = i * (i + 1) // 2 + j
                out_ref[16 * at : 16 * at + 16] = strip[r : r + BLK, j * BLK : (j + 1) * BLK].reshape(16, 8, BLK)


def tile_sum(here, tile, got, sems):
    x, y, z, c = here
    copies = []
    for k in range(1, NZ * NC):
        own = lax.rem(z * NC + c + k, NZ * NC)
        peer = device(x, y, lax.div(own, NC), lax.rem(own, NC))
        copies.append(send(tile.at[0], got.at[0, k - 1], sems, k - 1, peer))
    wait(copies)
    total = tile[0]
    for k in range(15):
        total = total + got[0, k]
    tile[1] = total
    copies = []
    for k in range(1, NX * NY):
        own = lax.rem(x * NY + y + k, NX * NY)
        peer = device(lax.div(own, NY), lax.rem(own, NY), z, c)
        copies.append(send(tile.at[1], got.at[1, k - 1], sems, 14 + k, peer))
    wait(copies)
    for k in range(15):
        total = total + got[1, k]
    tile[2] = total


T = 9


def all_sum(here, in_ref, out_ref, acc, got_c, got_1, acc_1, got_2, acc_2, got_z, full_z, sems, during):
    x, y, z, c = here
    across = device(x, y, z, 1 - c)
    xs = [device(lax.rem(x + k, NX), y, z, c) for k in range(1, NX)]
    ys = [device(x, lax.rem(y + k, NY), z, c) for k in range(1, NY)]
    zs = [device(x, y, lax.rem(z + k, NZ), c) for k in range(1, NZ)]
    x_at = [lax.rem(x + k, NX) for k in range(1, NX)]
    y_at = [lax.rem(y + k, NY) for k in range(1, NY)]
    z_at = [lax.rem(z + k, NZ) for k in range(1, NZ)]
    copy = send(in_ref.at[pl.ds((1 - c) * 288, 288)], got_c, sems, 0, across)
    during.get("core", nothing)()
    copy.wait()
    acc[...] = in_ref[pl.ds(c * 288, 288)] + got_c[...]
    copies = []
    for k in range(3):
        copies.append(send(acc.at[pl.ds(x_at[k] * 36, 36)], got_1.at[0, k], sems, 1 + k, xs[k]))
        copies.append(send(acc.at[pl.ds(144 + y_at[k] * 36, 36)], got_1.at[1, k], sems, 4 + k, ys[k]))
    during.get("first", nothing)()
    wait(copies)
    acc_1[0] = acc[pl.ds(x * 36, 36)] + got_1[0, 0] + got_1[0, 1] + got_1[0, 2]
    acc_1[1] = acc[pl.ds(144 + y * 36, 36)] + got_1[1, 0] + got_1[1, 1] + got_1[1, 2]
    copies = []
    for k in range(3):
        copies.append(send(acc_1.at[0, pl.ds(y_at[k] * T, T)], got_2.at[0, k], sems, 7 + k, ys[k]))
        copies.append(send(acc_1.at[1, pl.ds(x_at[k] * T, T)], got_2.at[1, k], sems, 10 + k, xs[k]))
    during.get("second", nothing)()
    wait(copies)
    acc_2[0:T] = acc_1[0, pl.ds(y * T, T)] + got_2[0, 0] + got_2[0, 1] + got_2[0, 2]
    acc_2[T : 2 * T] = acc_1[1, pl.ds(x * T, T)] + got_2[1, 0] + got_2[1, 1] + got_2[1, 2]
    acc_2[2 * T : 24] = jnp.zeros((24 - 2 * T, 8, 128), f32)
    copies = [send(acc_2.at[pl.ds(3 * z_at[k], 3)], got_z.at[k], sems, 13 + k, zs[k]) for k in range(7)]
    during.get("third", nothing)()
    wait(copies)
    own = acc_2[pl.ds(3 * z, 3)]
    for k in range(7):
        own = own + got_z[k]
    mine = full_z.at[pl.ds(3 * z, 3)]
    mine[...] = own
    copies = [send(mine, mine, sems, 20 + k, zs[k]) for k in range(7)]
    during.get("third back", nothing)()
    wait(copies)
    base = c * 288
    first, second = out_ref.at[pl.ds(base + (x * 4 + y) * T, T)], out_ref.at[pl.ds(base + 144 + (y * 4 + x) * T, T)]
    first[...] = full_z[0:T]
    second[...] = full_z[T : 2 * T]
    copies = []
    for k in range(3):
        copies.append(send(first, first, sems, 27 + k, ys[k]))
        copies.append(send(second, second, sems, 30 + k, xs[k]))
    wait(copies)
    first, second = out_ref.at[pl.ds(base + x * 36, 36)], out_ref.at[pl.ds(base + 144 + y * 36, 36)]
    copies = []
    for k in range(3):
        copies.append(send(first, first, sems, 33 + k, xs[k]))
        copies.append(send(second, second, sems, 36 + k, ys[k]))
    over = [send(first, first, sems, 39, across), send(second, second, sems, 40, across)]
    during.get("first back", nothing)()
    for k in range(3):
        copies[2 * k].wait()
        chunk = out_ref.at[pl.ds(base + x_at[2 - k] * 36, 36)]
        over.append(send(chunk, chunk, sems, 41 + 2 * k, across))
        copies[2 * k + 1].wait()
        chunk = out_ref.at[pl.ds(base + 144 + y_at[2 - k] * 36, 36)]
        over.append(send(chunk, chunk, sems, 42 + 2 * k, across))
    during.get("core back", nothing)()
    wait(over)


class RowScatter:
    def __init__(self, here, hidden, high, low, strip, away, got_c, acc_a, acc_b, got_1, acc_1, got_2, acc_2, got_z, sems):
        self.here, self.hidden, self.high, self.low, self.strip, self.away = here, hidden, high, low, strip, away
        self.got_c, self.acc_a, self.acc_b, self.got_1, self.acc_1 = got_c, acc_a, acc_b, got_1, acc_1
        self.got_2, self.acc_2, self.got_z, self.sems = got_2, acc_2, got_z, sems

    def strips(self):
        c = self.here[3]

        def one(k, carry):
            i, j = lax.div(k, 4), lax.rem(k, 4)
            own = self.hidden[span(k * BLK, BLK), :]
            both = dot16(own, self.high[...]) + dot16(own, self.low[...])
            self.strip[...] = both.reshape(NZ, NC, 8, 1024)
            self.away[i, j] = self.strip[:, 1 - c]
            keep = self.strip[:, c]
            self.acc_a[i, j] = keep[:, :, :512]
            self.acc_b[j, i] = keep[:, :, 512:]
            return carry

        lax.fori_loop(0, 16, one, 0)

    def core(self):
        x, y, z, c = self.here
        return [remote(self.away, self.got_c, self.sems, 0, device(x, y, z, 1 - c))]

    def core_start(self):
        start(self.core())

    def core_end(self):
        wait(self.core())

        def add(k, carry):
            i, j = lax.div(k, 4), lax.rem(k, 4)
            self.acc_a[i, j] = self.acc_a[i, j] + self.got_c[i, j, :, :, :512]
            self.acc_b[j, i] = self.acc_b[j, i] + self.got_c[i, j, :, :, 512:]
            return carry

        lax.fori_loop(0, 16, add, 0)

    def ring(self, slots):
        x, y, z, c = self.here
        copies = []
        for axis, at, size, acc in ((0, x, NX, self.acc_a), (1, y, NY, self.acc_b)):
            up, far, down = lax.rem(at + 1, size), lax.rem(at + 2, size), lax.rem(at + 3, size)
            plus = device(up, y, z, c) if axis == 0 else device(x, up, z, c)
            minus = device(down, y, z, c) if axis == 0 else device(x, down, z, c)
            routes = (
                (acc.at[far, 0:2], plus),
                (acc.at[far, 2:4], minus),
                (acc.at[down, 0:2], minus),
                (acc.at[up, 2:4], plus),
                (acc.at[up, 0:2], plus),
                (acc.at[down, 2:4], minus),
            )
            for slot in slots:
                src, peer = routes[slot]
                copies.append(remote(src, self.got_1.at[axis, slot], self.sems, 1 + 6 * axis + slot, peer))
        return copies

    def far_start(self):
        start(self.ring((0, 1)))

    def near_start(self):
        start(self.ring((2, 3)))

    def pass_on(self):
        x, y, z, c = self.here
        wait(self.ring((0, 1)))
        for axis, at, size, acc in ((0, x, NX, self.acc_a), (1, y, NY, self.acc_b)):
            up, down = lax.rem(at + 1, size), lax.rem(at + 3, size)

            def add(j, carry):
                acc[up, j] = acc[up, j] + self.got_1[axis, 0, j]
                acc[down, 2 + j] = acc[down, 2 + j] + self.got_1[axis, 1, j]
                return carry

            lax.fori_loop(0, 2, add, 0)
        start(self.ring((4, 5)))

    def first_end(self):
        x, y, z, c = self.here
        wait(self.ring((2, 3)))
        wait(self.ring((4, 5)))
        for axis, at, acc in ((0, x, self.acc_a), (1, y, self.acc_b)):
            got = self.got_1

            def add(j, carry):
                self.acc_1[axis, j] = acc[at, j] + got[axis, 2, j] + got[axis, 4, j]
                self.acc_1[axis, 2 + j] = acc[at, 2 + j] + got[axis, 3, j] + got[axis, 5, j]
                return carry

            lax.fori_loop(0, 2, add, 0)

    def second(self):
        x, y, z, c = self.here
        copies = []
        for k in range(3):
            xk, yk = lax.rem(x + k + 1, NX), lax.rem(y + k + 1, NY)
            copies.append(remote(self.acc_1.at[0, yk], self.got_2.at[0, k], self.sems, 13 + k, device(x, yk, z, c)))
            copies.append(remote(self.acc_1.at[1, xk], self.got_2.at[1, k], self.sems, 16 + k, device(xk, y, z, c)))
        return copies

    def second_start(self):
        start(self.second())

    def second_end(self):
        x, y, z, c = self.here
        wait(self.second())
        got = self.got_2
        self.acc_2[:, 0] = self.acc_1[0, y] + got[0, 0] + got[0, 1] + got[0, 2]
        self.acc_2[:, 1] = self.acc_1[1, x] + got[1, 0] + got[1, 1] + got[1, 2]

    def third(self):
        x, y, z, c = self.here
        copies = []
        for k in range(7):
            zk = lax.rem(z + k + 1, NZ)
            copies.append(remote(self.acc_2.at[zk], self.got_z.at[k], self.sems, 19 + k, device(x, y, zk, c)))
        return copies

    def third_start(self):
        start(self.third())

    def third_end(self, out_ref, row):
        wait(self.third())
        own = self.acc_2[self.here[2]]
        for k in range(7):
            own = own + self.got_z[k]
        out_ref[row : row + 8, :512] = own[0]
        out_ref[row : row + 8, 512:] = own[1]


def split(rows, high, low):
    high[...] = rows.astype(bf16)
    low[...] = (rows - high[...].astype(f32)).astype(bf16)


def kernel(count, hidden_in, weight_in, partner, whitened, grad_weight, grad_hidden,
           hidden, weight, in_sems, tile, tile_got, tile_sems,
           cent, packed, summed, acc, got_c, got_1, acc_1, got_2, acc_2, got_z, full_z, sems_1, sems_2,
           inv, inv_block, inv_stack, white, grad, mirror, total, grad_z, grad_mean, late, hidden_t, high, low,
           strip, away, w_got_c, acc_a, acc_b, w_got_1, w_acc_1, w_got_2, w_acc_2, w_got_z, w_sems_1, w_sems_2):
    here = place()
    x, y, z, c = here
    N = 256
    loads = [
        pltpu.make_async_copy(hidden_in, hidden, in_sems.at[0]),
        pltpu.make_async_copy(weight_in, weight, in_sems.at[1]),
    ]
    start(loads)
    barrier = pltpu.get_barrier_semaphore()
    for k in range(1, NZ * NC):
        own = lax.rem(z * NC + c + k, NZ * NC)
        pl.semaphore_signal(barrier, inc=1, device_id=device(x, y, lax.div(own, NC), lax.rem(own, NC)), device_id_type=MESH)
    for k in range(1, NX * NY):
        own = lax.rem(x * NY + y + k, NX * NY)
        pl.semaphore_signal(barrier, inc=1, device_id=device(lax.div(own, NY), lax.rem(own, NY), z, c), device_id_type=MESH)
    loads[0].wait()
    hidden_t[...] = hidden[...].T
    loads[1].wait()
    for part in range(4):
        cols = slice(part * 256, part * 256 + 256)
        strip_e = dot16(hidden[...], weight[:, cols])
        cent[:N, cols] = strip_e
        sums = jnp.sum(strip_e, axis=0, keepdims=True)
        tile[0, 2 * part : 2 * part + 1, :] = sums[:, :BLK]
        tile[0, 2 * part + 1 : 2 * part + 2, :] = sums[:, BLK:]
    sums = dot16(jnp.ones((8, N), bf16), hidden[...])
    for i in range(16):
        tile[0, 8 + i : 9 + i, :] = sums[0:1, i * BLK : (i + 1) * BLK]
    pl.semaphore_wait(barrier, NZ * NC + NX * NY - 2)
    tile_sum(here, tile, tile_got, tile_sems)
    for i in range(8):
        cols = slice(i * BLK, (i + 1) * BLK)
        cent[:N, cols] = cent[:N, cols] - tile[2, i : i + 1, :] * (1.0 / count)
    store_lower(packed, cent[:N, :], cent[:N, :])
    split(cent[:N, :], high, low)
    reduce_buffers = (acc, got_c, got_1, acc_1, got_2, acc_2, got_z, full_z)
    row_buffers = (high, low, strip, away, w_got_c, acc_a, acc_b, w_got_1, w_acc_1, w_got_2, w_acc_2, w_got_z)
    by_cent = RowScatter(here, hidden_t, *row_buffers, w_sems_1)
    by_grad = RowScatter(here, hidden_t, *row_buffers, w_sems_2)

    def cent_strips():
        by_cent.strips()
        by_cent.core_start()

    all_sum(here, packed, summed, *reduce_buffers, sems_1, {"first": cent_strips, "core back": by_cent.core_end})
    by_cent.far_start()
    by_cent.near_start()

    def to_second():
        by_cent.first_end()
        by_cent.second_start()

    def to_third():
        by_cent.second_end()
        by_cent.third_start()

    inverse_factor(1.0 / (count - 1), summed, inv, inv_block, inv_stack, {2: by_cent.pass_on, 4: to_second, 6: to_third})
    by_cent.third_end(cent, N)
    for part in range(4):
        stop = part * 256 + 256
        white[:, stop - 256 : stop] = dots(cent[:, :stop], inv[stop - 256 : stop, :stop], 1, 1)
    wh = white[:N, :]
    whitened[...] = wh.astype(bf16)
    row_norm = jnp.sqrt(jnp.sum(wh * wh, axis=1, keepdims=True) + epsilon)
    unit = wh / row_norm
    pick = (lax.broadcasted_iota(jnp.int32, (N, N), 0) == partner[...]).astype(f32)
    pick = (pick + pick.T).astype(bf16)
    near = jnp.zeros_like(unit)
    rest = unit
    for _ in range(3):
        term = rest.astype(bf16)
        near = near + dot16(pick, term)
        rest = rest - term.astype(f32)
    grad_unit = 2.0 * (2.0 * unit - near)
    inner_prod = jnp.sum(wh * grad_unit, axis=1, keepdims=True)
    gr = grad_unit / row_norm - wh * (inner_prod / (row_norm * row_norm * row_norm))
    grad[...] = gr
    split(gr, high, low)
    store_lower(packed, grad[...], white[:N, :])
    sums = jnp.sum(gr, axis=0, keepdims=True)
    sub = lax.broadcasted_iota(jnp.int32, (8, BLK), 0)
    lane = lax.broadcasted_iota(jnp.int32, (8, BLK), 1)
    for i in range(8):
        at = 16 * (i * (i + 1) // 2 + i)
        own = jnp.broadcast_to(sums[:, i * BLK : (i + 1) * BLK], (8, BLK))
        swapped = pltpu.roll(own, 64, 1)
        packed[at] = jnp.where(
            (lane >= 64) & (sub == 0), swapped, jnp.where((lane >= 64) & (sub == 1), own, packed[at])
        )
    def to_second_grad():
        by_grad.first_end()
        by_grad.second_start()

    all_sum(
        here, packed, summed, *reduce_buffers, sems_2,
        {
            "core": by_grad.strips,
            "first": by_grad.core_start,
            "second": by_grad.core_end,
            "third": by_grad.far_start,
            "third back": by_grad.near_start,
            "first back": by_grad.pass_on,
            "core back": to_second_grad,
        },
    )
    lane1 = lax.broadcasted_iota(jnp.int32, (1, BLK), 1)
    r = lax.broadcasted_iota(jnp.int32, (BLK, BLK), 0)
    l = lax.broadcasted_iota(jnp.int32, (BLK, BLK), 1)
    scale = 1.0 / (count - 1)
    for i in range(8):
        for j in range(i + 1):
            block = get_block(summed, i, j)
            turned = block.T
            rows, cols = slice(i * BLK, (i + 1) * BLK), slice(j * BLK, (j + 1) * BLK)
            if i == j:
                mirror[rows, cols] = jnp.where(r >= l, block, turned) * scale
                sums = jnp.where(lane1 < 64, pltpu.roll(block[0:1, :], 64, 1), block[1:2, :]) * (1.0 / count)
                grad_mean[:, cols] = jnp.broadcast_to(sums, (8, BLK))
                total[:N, cols] = grad[:, cols] - sums
            else:
                mirror[rows, cols] = block * scale
                mirror[cols, rows] = turned * scale
    total[N:, :] = jnp.zeros((8, 1024), f32)
    for part in range(4):
        cols = slice(part * 256, part * 256 + 256)
        total[:, cols] = total[:, cols] - dots(white[...], mirror[:, cols])
    by_grad.second_end()
    by_grad.third_start()
    for part in range(4):
        start_at = part * 256
        cols = slice(start_at, start_at + 256)
        both = dots(total[:, start_at:], inv[start_at:1024, cols])
        grad_z[:, cols] = both[:N].astype(bf16)
        late[:, cols] = both[N:]

    def hidden_part(k, carry):
        own = span(k * 256, 256)
        grad_hidden[:, own] = dot16(grad_z[...], weight[own, :], 1, 1).astype(bf16)
        return carry

    lax.fori_loop(0, 8, hidden_part, 0)
    units = jnp.broadcast_to(tile[2, pl.ds(8 + x * NY + y, 1), :], (8, BLK))
    mine = jnp.sum(jnp.where(lane == (z * NC + c) * 8 + sub, units, 0.0), axis=1, keepdims=True)
    by_grad.third_end(total, N)
    rows = total[N:, :] - mine * grad_mean[...]
    grad_weight[...] = late[...] + dots(rows, inv[:1024, :])


def hand_over_kernel(whitened, grad_weight, grad_hidden, whitened_out, grad_weight_out, grad_hidden_out, sems):
    copies = [pltpu.make_async_copy(grad_weight, grad_weight_out, sems.at[0])]
    for k in range(2):
        rows = pl.ds(k * 128, 128)
        copies.append(pltpu.make_async_copy(whitened.at[rows], whitened_out.at[rows], sems.at[1 + k]))
    for k in range(4):
        rows = pl.ds(k * 64, 64)
        copies.append(pltpu.make_async_copy(grad_hidden.at[rows], grad_hidden_out.at[rows], sems.at[3 + k]))
    start(copies)
    wait(copies)


def hand_over(results):
    anywhere = pl.BlockSpec(memory_space=pl.ANY)
    return pl.pallas_call(
        hand_over_kernel,
        out_shape=tuple(jax.ShapeDtypeStruct(a.shape, a.dtype) for a in results),
        in_specs=[anywhere] * 3,
        out_specs=(anywhere,) * 3,
        scratch_shapes=[pltpu.SemaphoreType.DMA((7,))],
        name="hand_over",
    )(*results)


def body(hidden, weight, partners):
    count = hidden.shape[0] * lax.axis_size("group") * lax.axis_size("dp")
    vmem = pl.BlockSpec(memory_space=pltpu.VMEM)
    V, sem = pltpu.VMEM, pltpu.SemaphoreType.DMA
    results = pl.pallas_call(
        functools.partial(kernel, count),
        out_shape=(
            jax.ShapeDtypeStruct((256, 1024), bf16),
            jax.ShapeDtypeStruct((8, 1024), f32),
            jax.ShapeDtypeStruct((256, 2048), bf16),
        ),
        in_specs=[pl.BlockSpec(memory_space=pl.ANY)] * 2 + [vmem],
        out_specs=(vmem,) * 3,
        scratch_shapes=[
            V((256, 2048), bf16), V((2048, 1024), bf16), sem((2,)),
            V((3, 24, 128), f32), V((2, 15, 24, 128), f32), sem((2, 30)),
            V((264, 1024), f32), V((576, 8, 128), f32), V((576, 8, 128), f32),
            V((288, 8, 128), f32), V((288, 8, 128), f32), V((2, 3, 36, 8, 128), f32), V((2, 36, 8, 128), f32),
            V((2, 3, T, 8, 128), f32), V((24, 8, 128), f32), V((7, 3, 8, 128), f32), V((24, 8, 128), f32),
            sem((2, 47)), sem((2, 47)),
            V((1920, 1024), f32), V((BLK, BLK), f32), V((768, 1024), bf16), V((264, 1024), f32),
            V((256, 1024), f32), V((1024, 1024), f32), V((264, 1024), f32), V((256, 1024), bf16),
            V((8, 1024), f32), V((8, 1024), f32), V((2048, 256), bf16), V((256, 1024), bf16), V((256, 1024), bf16),
            V((8, 2, 8, 1024), f32), V((4, 4, 8, 8, 1024), f32), V((4, 4, 8, 8, 1024), f32),
            V((4, 4, 8, 8, 512), f32), V((4, 4, 8, 8, 512), f32), V((2, 6, 2, 8, 8, 512), f32),
            V((2, 4, 8, 8, 512), f32), V((2, 3, 8, 8, 512), f32), V((8, 2, 8, 512), f32), V((7, 2, 8, 512), f32),
            sem((2, 26)), sem((2, 26)),
        ],
        compiler_params=pltpu.CompilerParams(collective_id=0, has_side_effects=True, vmem_limit_bytes=60 * MB),
        name="whitening_step",
    )(hidden, weight, partners)
    return hand_over(results)


def solution(mesh):
    return jax.shard_map(
        body,
        mesh=mesh,
        in_specs=(P(("group", "dp"), None), P(), P(("group", "dp"), None)),
        out_specs=(P(("group", "dp"), None), P(("group", "dp"), None), P(("group", "dp"), None)),
        check_vma=False,
    )
```
